32 devices in a mesh: groups: 2 (over y), dp: 4 (over z), section: 2 (over x), mp: 2 (over core).
Axes of the slice: x: 2, y: 2, z: 4, core: 2. Of those that a mesh axis runs over, the one named last changes fastest.
Arguments:
- hidden_in: bfloat16 [2, 8, 128, 2560], P('section', ('groups', 'dp'), None, 'mp'), parts along dimension 1, may hold values from -6 to 6
- attn_out: bfloat16 [2, 8, 128, 2560], P('section', ('groups', 'dp'), None, 'mp'), parts along dimension 1, may hold values from -5 to 5
- queries: bfloat16 [2, 8, 128, 2560], P('section', ('groups', 'dp'), None, 'mp'), parts along dimension 1, may hold values from -72 to 72
- keys: bfloat16 [2, 8, 128, 512], P('section', ('groups', 'dp'), None, 'mp'), parts along dimension 1, may hold values from -5 to 5
- value_weight: bfloat16 [2, 2560, 512], P('section', 'mp'), may hold values from -0.125 to 0.125
- out_weight: bfloat16 [2, 2560, 2560], P('section', 'mp', 'dp'), may hold values from -0.125 to 0.125
- lengths: int32 [8], P(('groups', 'dp')), parts along dimension 0, may hold values from 32 to 128, as said below
Outputs:
- heat: float32 [2, 8, 128], P('section', ('groups', 'dp')), parts along dimension 1
- weight_relevance: float32 [4, 2560, 512], P(('groups', 'section'), ('mp', 'dp')), parts along dimension 0
The draws below stay inside these ranges and needn't reach their ends.
There are 2 independent parts, one for each index of `groups`. The reference program is written for one: setup_inputs(seed, part) draws one part's arguments, and reference() takes and returns one part's arrays. A program takes and returns all parts, laid end to end along the dimension named above; an argument that names none is the same for every part. Nothing has to cross between parts.
Inputs may be any that keep to these rules, and one draw needn't show every extreme that they name: `lengths`: the valid length of each reference sequence; positions at or past it are padding.
All inputs are finite; a program needn't handle non-finite values.
Results may differ from the reference program's by a relative error of at most 0.035.
Values may be sent and summed in bfloat16 or wider, within the bound.
A program may use at most 64 MiB of HBM per device.

```python
import math
import jax
import jax.numpy as jnp
from jax import lax

DW = 2560
HD = 128
QH = 20
KVH = 4
L = 128
SECTIONS = 2
SEQS = 4


def queries_keys(key):
    folded = jax.random.fold_in(key, 31)
    key_query, key_key = jax.random.split(folded, 2)
    group_size = QH // KVH
    keys_base = jnp.clip(jax.random.normal(key_key, (SECTIONS, SEQS, L, KVH, HD), jnp.float32), -4.0, 4.0)
    query_base = jnp.clip(jax.random.normal(key_query, (SECTIONS, SEQS, L, KVH, group_size, HD), jnp.float32), -4.0, 4.0)
    return (query_base.reshape(SECTIONS, SEQS, L, QH * HD), keys_base.reshape(SECTIONS, SEQS, L, KVH * HD))


def draw_queries(key, part):
    return queries_keys(key)[0].astype(jnp.bfloat16)


def draw_keys(key, part):
    return queries_keys(key)[1].astype(jnp.bfloat16)


def draw_lengths(key, part):
    key_length, key_spot = jax.random.split(jax.random.fold_in(key, 11))
    length_draw = jax.random.randint(key_length, (SEQS,), L // 4, L + 1)
    spot_order = jax.random.permutation(key_spot, SEQS)
    length_draw = jnp.where(spot_order == 0, L, length_draw)
    return jnp.where(spot_order == 1, L // 4, length_draw).astype(jnp.int32)


def level_of(key, shape, shards, least, high):
    gain = 1.0
    for axis_at, blocks in shards:
        heights = jax.random.uniform(jax.random.fold_in(jax.random.fold_in(key, 6), axis_at), (blocks,), jnp.float32, least / len(shards), high / len(shards))
        gain = gain * jnp.repeat(jnp.exp(heights), shape[axis_at] // blocks).reshape((-1,) + (1,) * (len(shape) - 1 - axis_at))
    return gain


def normal_values(rng, extent, spread, reach, pieces=(), kind=jnp.bfloat16):
    values = jax.random.normal(rng, extent, jnp.float32) * spread
    if len(pieces) > 0:
        values = level_of(rng, extent, pieces, -0.22, 0.18) * values
    return jnp.clip(values, min=-reach, max=reach).astype(kind)


def setup_inputs(seed: int = 0, part: int = 0) -> dict:
    splits = jax.random.split(jax.random.key(seed), 8)
    part_keys = jax.random.split(jax.random.fold_in(splits[7], part), 8)
    hidden_in = normal_values(part_keys[0], (SECTIONS, SEQS, L, DW), 1.0, 6.0, ((0, 2), (1, 4), (3, 2)))
    attn_out = normal_values(part_keys[1], (SECTIONS, SEQS, L, DW), 0.7, 5.0, ((0, 2), (1, 4), (3, 2)))
    queries = draw_queries(jax.random.fold_in(jax.random.fold_in(splits[7], part), 71), part)
    keys = draw_keys(jax.random.fold_in(jax.random.fold_in(splits[7], part), 71), part)
    value_weight = normal_values(splits[4], (SECTIONS, DW, KVH * HD), DW ** -0.5, 0.125, ((0, 2), (1, 2)))
    out_weight = normal_values(splits[5], (SECTIONS, QH * HD, DW), (QH * HD) ** -0.5, 0.125, ((0, 2), (1, 2), (2, 4)))
    lengths = draw_lengths(jax.random.fold_in(jax.random.fold_in(splits[7], part), 71), part)
    return dict(hidden_in=hidden_in, attn_out=attn_out, queries=queries, keys=keys, value_weight=value_weight, out_weight=out_weight, lengths=lengths)


EPS = 0.25

def stabilize(entries):
    return jnp.where(entries >= 0, entries + EPS, entries - EPS)

def section_rule(inputs, branch, query_rows, key_rows, length, incoming, value_rows, out_rows):
    group_size = QH // KVH
    seq_len = inputs.shape[0]
    inputs_f = inputs.astype(jnp.float32)
    branch_f = branch.astype(jnp.float32)
    totals = inputs_f + branch_f
    values_bf = lax.optimization_barrier(jnp.dot(inputs, value_rows, preferred_element_type=jnp.float32).astype(jnp.bfloat16))
    values_f = values_bf.astype(jnp.float32)
    query_heads = query_rows.astype(jnp.float32).reshape(seq_len, KVH, group_size, HD)
    key_heads = key_rows.astype(jnp.float32).reshape(seq_len, KVH, HD)
    scores = jnp.einsum('tgjd,sgd->gjts', query_heads, key_heads) / math.sqrt(HD)
    position = jnp.arange(seq_len, dtype=jnp.int32)
    allowed = (position[None, :] <= position[:, None]) & (position[None, :] < length)
    scores = jnp.where(allowed, scores, -1000000000.0)
    row_top = lax.optimization_barrier(jnp.max(scores, axis=-1, keepdims=True))
    weights = jnp.exp(scores - row_top)
    prob_rows = (weights / lax.optimization_barrier(jnp.sum(weights, axis=-1, keepdims=True))).astype(jnp.bfloat16)
    prob_f = prob_rows.astype(jnp.float32)
    mixed_heads = jnp.einsum('gjts,sgd->tgjd', prob_f, values_f.reshape(seq_len, KVH, HD)).reshape(seq_len, QH * HD)
    sens_total = incoming.astype(jnp.float32) / stabilize(totals)
    kept = inputs_f * sens_total
    sens_branch = (branch_f * sens_total / stabilize(branch_f)).astype(jnp.bfloat16)
    back_mixed = jnp.dot(sens_branch, out_rows.T, preferred_element_type=jnp.float32)
    sens_mixed = (mixed_heads * back_mixed / stabilize(mixed_heads)).astype(jnp.bfloat16)
    back_values = jnp.einsum('gjts,tgjd->sgd', prob_f, sens_mixed.astype(jnp.float32).reshape(seq_len, KVH, group_size, HD)).reshape(seq_len, KVH * HD)
    sens_values = (values_f * back_values / stabilize(values_f)).astype(jnp.bfloat16)
    back_inputs = jnp.dot(sens_values, value_rows.T, preferred_element_type=jnp.float32)
    outgoing = (kept + inputs_f * back_inputs).astype(jnp.bfloat16)
    return (outgoing, sens_values)

def reference(hidden_in, attn_out, queries, keys, value_weight, out_weight, lengths):
    vmapped = jax.vmap(section_rule, in_axes=(0, 0, 0, 0, 0, 0, None, None))
    position = jnp.arange(L, dtype=jnp.int32)
    valid_rows = (position[None, :] < lengths[:, None]).astype(jnp.float32)
    total_last = hidden_in[SECTIONS - 1].astype(jnp.float32) + attn_out[SECTIONS - 1].astype(jnp.float32)
    incoming = (total_last * valid_rows[:, :, None]).astype(jnp.bfloat16)
    heat_list = [None] * SECTIONS
    weight_list = [None] * SECTIONS
    for section_pos in range(SECTIONS - 1, -1, -1):
        outgoing, sens_values = vmapped(hidden_in[section_pos], attn_out[section_pos], queries[section_pos], keys[section_pos], lengths, incoming, value_weight[section_pos], out_weight[section_pos])
        heat_list[section_pos] = lax.optimization_barrier(jnp.sum(outgoing.astype(jnp.float32), axis=-1)) / DW
        summed = jnp.einsum('btc,btk->ck', hidden_in[section_pos].astype(jnp.float32), sens_values.astype(jnp.float32))
        weight_list[section_pos] = value_weight[section_pos].astype(jnp.float32) * summed
        incoming = outgoing
    return (jnp.stack(heat_list), jnp.stack(weight_list))
```

```python
import functools
import math

import jax
import jax.numpy as jnp
from jax import lax
from jax.experimental import pallas as pl
from jax.experimental.pallas import tpu as pltpu
from jax.sharding import PartitionSpec as P

DW = 2560
HD = 128
QH = 20
KVH = 4


EPS = 0.25


def from_behind(shard, axis, by):
    peers = lax.axis_size(axis)
    pairs = [(i, i + by) for i in range(peers) if 0 <= i + by < peers]
    return lax.ppermute(shard, axis, pairs)


def stabilize(entries):
    return jnp.where(entries >= 0, entries + EPS, entries - EPS)


def gated(active, compute, operand, out_shape, out_type):
    return lax.cond(active, compute, lambda unused: jnp.zeros(out_shape, out_type), operand)


def on_device(hidden_in, attn_out, queries, keys, value_weight, out_weight, lengths):
    inputs = hidden_in[0, 0]
    branch = attn_out[0, 0]
    query_rows = queries[0, 0]
    key_rows = keys[0, 0]
    value_rows = value_weight[0]
    seq_len = inputs.shape[0]
    half_width = inputs.shape[1]
    group_size = QH // KVH
    local_kv = key_rows.shape[1] // HD
    kv_width = value_rows.shape[1]
    sections = lax.axis_size("section")
    section_pos = lax.axis_index("section")
    core_pos = lax.axis_index("mp")
    out_cols = lax.all_gather(out_weight, "dp", axis=2, tiled=True)[0]
    inputs_f = inputs.astype(jnp.float32)
    branch_f = branch.astype(jnp.float32)
    totals = inputs_f + branch_f
    value_part = jnp.dot(inputs, value_rows, preferred_element_type=jnp.float32)
    value_all = lax.psum(value_part.astype(jnp.bfloat16), "mp").astype(jnp.float32)
    value_mine = lax.dynamic_slice_in_dim(value_all, core_pos * local_kv * HD, local_kv * HD, 1)
    values_bf = lax.optimization_barrier(value_mine.astype(jnp.bfloat16))
    values_f = values_bf.astype(jnp.float32)
    query_heads = query_rows.reshape(seq_len, local_kv, group_size, HD)
    key_heads = key_rows.reshape(seq_len, local_kv, HD)
    scores = jnp.einsum(
        "tgjd,sgd->gjts", query_heads, key_heads, preferred_element_type=jnp.float32
    ) / math.sqrt(HD)
    position = lax.iota(jnp.int32, seq_len)
    allowed = (position[None, :] <= position[:, None]) & (position[None, :] < lengths[0])
    scores = jnp.where(allowed, scores, -1000000000.0)
    row_top = jnp.max(scores, axis=-1, keepdims=True)
    weights = jnp.exp(scores - row_top)
    prob_rows = (weights / jnp.sum(weights, axis=-1, keepdims=True)).astype(jnp.bfloat16)
    mixed_heads = jnp.einsum(
        "gjts,sgd->tgjd",
        prob_rows,
        values_bf.reshape(seq_len, local_kv, HD),
        preferred_element_type=jnp.float32,
    ).reshape(seq_len, local_kv * group_size * HD)
    valid_rows = (position < lengths[0]).astype(jnp.float32)
    current = (totals * valid_rows[:, None]).astype(jnp.bfloat16)
    result = jnp.zeros((seq_len, half_width), jnp.bfloat16)
    sens_kept = jnp.zeros((seq_len, kv_width), jnp.bfloat16)
    for turn_index in range(sections):
        active = section_pos == sections - 1 - turn_index
        sens_total = current.astype(jnp.float32) / stabilize(totals)
        sens_branch = (branch_f * sens_total / stabilize(branch_f)).astype(jnp.bfloat16)
        sens_full = lax.all_gather(sens_branch, "mp", axis=1, tiled=True)

        def through_heads(operand):
            back_mixed = lax.dot_general(
                operand, out_cols, (((1,), (1,)), ((), ())), preferred_element_type=jnp.float32
            )
            sens_mixed = (mixed_heads * back_mixed / stabilize(mixed_heads)).astype(jnp.bfloat16)
            back_values = jnp.einsum(
                "gjts,tgjd->sgd",
                prob_rows,
                sens_mixed.reshape(seq_len, local_kv, group_size, HD),
                preferred_element_type=jnp.float32,
            ).reshape(seq_len, local_kv * HD)
            return (values_f * back_values / stabilize(values_f)).astype(jnp.bfloat16)

        sens_values = gated(
            active, through_heads, sens_full, (seq_len, local_kv * HD), jnp.bfloat16
        )
        sens_all = lax.all_gather(sens_values, "mp", axis=1, tiled=True)

        def through_values(operand):
            back_inputs = lax.dot_general(
                operand, value_rows, (((1,), (1,)), ((), ())), preferred_element_type=jnp.float32
            )
            return (inputs_f * sens_total + inputs_f * back_inputs).astype(jnp.bfloat16)

        outgoing = gated(active, through_values, sens_all, (seq_len, half_width), jnp.bfloat16)
        result = jnp.where(active, outgoing, result)
        sens_kept = jnp.where(active, sens_all, sens_kept)
        if turn_index + 1 < sections:
            arrived = from_behind(outgoing, "section", -1)
            current = jnp.where(section_pos == sections - 2 - turn_index, arrived, current)
    heat_part = jnp.sum(result.astype(jnp.float32), axis=1)
    heat_rows = lax.psum(heat_part, "mp") / DW
    block_rows = half_width // lax.axis_size("dp")
    row_start = lax.axis_index("dp") * block_rows
    value_block = lax.dynamic_slice_in_dim(value_rows, row_start, block_rows, 0).astype(jnp.float32)
    summed = lax.psum_scatter(
        lax.dot_general(
            inputs, sens_kept, (((0,), (0,)), ((), ())), preferred_element_type=jnp.float32
        ).astype(jnp.bfloat16),
        "dp",
        scatter_dimension=0,
        tiled=True,
    ).astype(jnp.float32)
    relevance_rows = value_block * summed
    return (heat_rows[None, None, :], relevance_rows[None])


CHUNKS = 4
RAW = 3
SEGMENTS = (((0, 128),), ((0, 64), (64, 32)), ((0, 64),), ((0, 32),))
TILE = 256
MESH_ID = pl.DeviceIdType.MESH
F32 = jnp.float32
BF16 = jnp.bfloat16
LAST_ORDER = (
    ("gather", 3), ("part", 0), ("part", 1), ("mix", 0), ("part", 2), ("head", 0), ("linear", 3),
    ("mix", 1), ("head", 1), ("mix", 2), ("head", 2), ("join", 3),
)
NEXT_ORDER = (
    ("gather", 0), ("gather", 1), ("take", 0), ("gather", 2), ("linear", 0), ("gather", 3),
    ("take", 1), ("join", 0), ("linear", 1), ("take", 2), ("join", 1), ("linear", 2), ("take", 3),
    ("join", 2), ("linear", 3), ("join", 3),
)


def tiles_of(heads, step):
    return sum(-(-heads // (HD // lanes)) for _, lanes in SEGMENTS[step])


def nt_dot(left, right):
    return lax.dot_general(left, right, (((1,), (1,)), ((), ())), preferred_element_type=F32)


def tn_dot(left, right):
    return lax.dot_general(left, right, (((0,), (0,)), ((), ())), preferred_element_type=F32)


def chain_kernel(
    peers, sections, len_ref, hid_in, att_in, que_in, key_in, vw_in, ow_in,
    heat_ref, rel_ref, hid_ref, att_ref, que_ref, key_ref, vw_ref, ow_ref, load_sem,
    through_ref, keep_ref, ratio_ref, inc_ref, out_ref, prob_ref, pack_ref, gval_ref, val_ref, bv_ref,
    vsend, vrecv, hidt_ref, hida_ref, sv_ref, heats, sm_ref, bvsend, bvbuf,
    asend, abuf, psend, pbuf,
    a_send, g_send, a_recv, p_send, p_recv, s_send, s_recv, f_send, f_recv,
    x_send, x_recv, h_send, h_recv, one_send, one_recv,
    k_send, k_recv, b_send, b_recv, w_send, w_recv,
):
    dp = lax.axis_index("dp")
    sec = lax.axis_index("section")
    core = lax.axis_index("mp")
    other = 1 - core
    seq_len, half = hid_ref.shape
    rows_n = seq_len // CHUNKS
    width = ow_ref.shape[1]
    blocks = peers // 2
    local_kv = key_ref.shape[1] // HD
    group = QH // KVH
    heads_n = local_kv * group
    kv_half = local_kv * HD
    block_rows = half // peers
    is_last = sec == sections - 1
    gets = core == dp // blocks
    hops = [(hop, lax.rem(dp + hop, peers)) for hop in range(1, peers)]

    loads = [
        pltpu.make_async_copy(source, target, load_sem.at[at])
        for at, (source, target) in enumerate((
            (hid_in, hid_ref), (att_in, att_ref), (vw_in, vw_ref),
            (que_in, que_ref), (key_in, key_ref), (ow_in, ow_ref),
        ))
    ]
    for load in loads:
        load.start()

    barrier = pltpu.get_barrier_semaphore()
    for hop, to in hops:
        for target in range(2):
            pl.semaphore_signal(
                barrier, inc=1, device_id={"dp": to, "mp": target}, device_id_type=MESH_ID
            )
    pl.semaphore_signal(barrier, inc=1, device_id={"mp": other}, device_id_type=MESH_ID)

    @pl.when(sec > 0)
    def _():
        pl.semaphore_signal(
            barrier, inc=1, device_id={"section": sec - 1}, device_id_type=MESH_ID
        )

    @pl.when(sec < sections - 1)
    def _():
        pl.semaphore_signal(
            barrier, inc=1, device_id={"section": sec + 1}, device_id_type=MESH_ID
        )

    def barrier_wait():
        greeted = 2 * (peers - 1) + 1
        if sections < 3:
            pl.semaphore_wait(barrier, greeted + sections - 1)
        else:
            inside = jnp.logical_and(sec > 0, sec < sections - 1)

            @pl.when(inside)
            def _():
                pl.semaphore_wait(barrier, greeted + 2)

            @pl.when(jnp.logical_not(inside))
            def _():
                pl.semaphore_wait(barrier, greeted + 1)

    def remote(source, target, send, recv, device):
        return pltpu.make_async_remote_copy(
            src_ref=source, dst_ref=target, send_sem=send, recv_sem=recv,
            device_id=device, device_id_type=MESH_ID,
        )

    def rows_of(step):
        return pl.ds((CHUNKS - 1 - step) * rows_n, rows_n)

    def branch_copy(step, block):
        return remote(
            asend.at[step, block], abuf.at[step, dp],
            a_send.at[step, block], a_recv.at[step, dp], {"dp": core * blocks + block},
        )

    def branch_forward(step, source):
        view = abuf.at[step, source]
        return remote(
            view, view, g_send.at[step, source], a_recv.at[step, source], {"mp": other}
        )

    rounds = peers.bit_length() - 1

    def slot_of(turn, target):
        return peers - (peers >> turn) + target // (2 << turn)

    def part_target(turn, at):
        bit = 1 << turn
        return lax.rem(dp, bit) + bit * (2 * at + 1 - lax.rem(dp // bit, 2))

    def part_copy(step, turn, at):
        bit = 1 << turn
        slot = peers - (peers >> turn) + at
        return remote(
            psend.at[step, part_target(turn, at)], pbuf.at[step, slot],
            p_send.at[step, slot], p_recv.at[step, slot],
            {"dp": dp + bit - 2 * bit * lax.rem(dp // bit, 2)},
        )

    def part_take(step, turn, target):
        slot = slot_of(turn, target)
        view = pbuf.at[step, slot]
        remote(
            view, view, p_send.at[step, slot], p_recv.at[step, slot], {"mp": other}
        ).wait_recv()
        return pbuf[step, slot].astype(F32)

    def mix_stage(step):
        for turn in range(1, rounds):
            for at in range(peers >> (turn + 1)):
                target = part_target(turn, at)
                running = psend[step, target].astype(F32)
                for before in range(turn):
                    running = running + part_take(step, before, target)
                psend[step, target] = running.astype(BF16)
                part_copy(step, turn, at).start()

    def value_rows(step, source):
        return gval_ref.at[source, pl.ds(0, (CHUNKS - step) * rows_n)]

    def prob_tiles(step, source):
        first = sum(tiles_of(heads_n, before) for before in range(step))
        return pack_ref.at[source, pl.ds(first, tiles_of(heads_n, step))]

    def gather_value(first, hop, to):
        view = value_rows(first, dp)
        return remote(
            view, view, k_send.at[CHUNKS, hop], k_recv.at[CHUNKS, dp], {"dp": to}
        )

    def gather_probs(step, hop, to):
        view = prob_tiles(step, dp)
        return remote(view, view, k_send.at[step, hop], k_recv.at[step, dp], {"dp": to})

    def sum_copy(step, hop, to):
        return remote(
            bvsend.at[step, hop], bvbuf.at[step, dp],
            b_send.at[step, hop], b_recv.at[step, dp], {"dp": to},
        )

    def sens_copy(step, owner):
        view = sv_ref.at[dp, owner, rows_of(step)]
        return remote(view, view, s_send.at[step], s_recv.at[step], {"mp": other})

    def final_copy(step, hop, to, side):
        view = sv_ref.at[dp, core, rows_of(step)]
        return remote(
            view, view, f_send.at[step, hop, side], f_recv.at[step, dp, core],
            {"dp": to, "mp": core if side == 0 else other},
        )

    def final_wait(step, source, owner):
        view = sv_ref.at[source, owner, rows_of(step)]
        remote(
            view, view, f_send.at[step, 0, 0], f_recv.at[step, source, owner], {"mp": other}
        ).wait_recv()

    def final_forward(source, owner):
        view = sv_ref.at[source, owner, pl.ds(rows_n, seq_len - rows_n)]
        return remote(view, view, w_send.at[source], w_recv.at[source], {"mp": other})

    def final_out(step):
        for hop, to in hops:
            for side in range(2 if step == CHUNKS - 1 else 1):
                final_copy(step, hop, to, side).start()

    def section_copy(step, target):
        return remote(
            out_ref.at[rows_of(step)], inc_ref.at[rows_of(step)],
            x_send.at[step], x_recv.at[step], {"section": target},
        )

    def hidden_copy(hop, to):
        return remote(
            hidt_ref.at[pl.ds(pl.multiple_of(to * block_rows, 16), block_rows)], hida_ref.at[dp],
            h_send.at[hop], h_recv.at[dp], {"dp": to},
        )

    def hidden_wait(hop, source):
        return remote(
            hidt_ref.at[pl.ds(0, block_rows)], hida_ref.at[source],
            h_send.at[hop], h_recv.at[source], {"mp": other},
        )

    def value_copy(slot):
        return remote(
            vsend.at[slot], vrecv, one_send.at[0], one_recv.at[0], {"mp": other}
        )

    def heat_copy(slot):
        return remote(
            heats.at[slot], heats.at[slot], one_send.at[1], one_recv.at[1], {"mp": other}
        )

    def branch_stage(step):
        rows = rows_of(step)
        sens = (inc_ref[rows, :].astype(F32) * through_ref[rows, :]).astype(BF16)
        for block in range(blocks):
            to = core * blocks + block
            piece = sens[:, block * width:(block + 1) * width]
            asend[step, block] = piece

            @pl.when(to == dp)
            def _():
                abuf[step, dp] = piece
                branch_forward(step, dp).start()

            @pl.when(to != dp)
            def _():
                branch_copy(step, block).start()

    def branch_wait(step):
        @pl.when(gets)
        def _():
            for hop, source in hops:
                branch_forward(step, source).wait_recv()
                branch_forward(step, source).start()

        @pl.when(jnp.logical_not(gets))
        def _():
            for source in range(peers):
                branch_forward(step, source).wait_recv()

        return abuf[step].reshape(peers * rows_n, width)

    def part_stage(step):
        stacked = branch_wait(step)

        def tile(at, unused):
            start = pl.multiple_of(at * TILE, TILE)
            part = nt_dot(stacked, ow_ref[pl.ds(start, TILE), :]).astype(BF16)
            psend[step, :, :, pl.ds(start, TILE)] = part.reshape(peers, rows_n, TILE)
            return unused

        lax.fori_loop(0, half // TILE, tile, 0, unroll=True)
        for at in range(peers // 2):
            part_copy(step, 0, at).start()

    def add_values(seq, rows, mixed):
        for kv in range(local_kv):
            heads = range(kv * group, (kv + 1) * group)
            left = jnp.concatenate([prob_ref[seq, h, rows, :] for h in heads], axis=0)
            right = jnp.concatenate([mixed[:, h * HD:(h + 1) * HD] for h in heads], axis=0)
            columns = pl.ds(kv * HD, HD)
            bv_ref[seq, :, columns] = bv_ref[seq, :, columns] + tn_dot(left, right)

    def head_stage(step):
        rows = rows_of(step)
        back = psend[step, dp].astype(F32)
        for turn in range(rounds):
            back = back + part_take(step, turn, dp)
        add_values(dp, rows, (ratio_ref[dp, rows, :] * back).astype(BF16))
        finish(step, bv_ref[dp, rows, :])

    def linear_stage(step):
        rows = rows_of(step)
        stacked = branch_wait(step)
        for at in range(half // TILE):
            columns = pl.ds(at * TILE, TILE)
            part = nt_dot(stacked, ow_ref[columns, :])
            ratio = ratio_ref[:, rows, columns].reshape(peers * rows_n, TILE)
            sm_ref[:, columns] = (ratio * part).astype(BF16)
        for seq in range(peers):
            add_values(seq, rows, sm_ref[seq * rows_n:(seq + 1) * rows_n, :])
        for hop, to in hops:
            bvsend[step, hop] = bv_ref[to, rows, :].astype(BF16)
            sum_copy(step, hop, to).start()

    def join_stage(step):
        total = bv_ref[dp, rows_of(step), :]
        for hop, source in hops:
            view = bvbuf.at[step, source]
            remote(
                view, view, b_send.at[step, hop], b_recv.at[step, source], {"mp": other}
            ).wait_recv()
            total = total + bvbuf[step, source].astype(F32)
        finish(step, total)

    def finish(step, back_values):
        rows = rows_of(step)
        sv_ref[dp, core, rows, :] = (val_ref[rows, :] * back_values).astype(BF16)
        sens_copy(step, core).start()

        @pl.when(jnp.logical_not(is_last))
        def _():
            final_out(step)

        sens_copy(step, other).wait_recv()
        sens = jnp.concatenate([sv_ref[dp, 0, rows, :], sv_ref[dp, 1, rows, :]], axis=1)
        sums = jnp.zeros((rows_n, HD), F32)
        for at in range(half // TILE):
            columns = pl.ds(at * TILE, TILE)
            back_in = nt_dot(sens, vw_ref[columns, :])
            out = (
                inc_ref[rows, columns].astype(F32) * keep_ref[rows, columns]
                + hid_ref[rows, columns].astype(F32) * back_in
            ).astype(BF16)
            out_ref[rows, columns] = out
            wide = out.astype(F32)
            for lane in range(TILE // HD):
                sums = sums + wide[:, lane * HD:(lane + 1) * HD]
        heats[core, rows, :] = sums

        @pl.when(sec > 0)
        def _():
            section_copy(step, sec - 1).start()

    lane_at = lax.broadcasted_iota(jnp.int32, (rows_n, HD), 1)

    def shifted(tile, start, count, to):
        inside = (lane_at >= start) & (lane_at < start + count)
        kept = jnp.where(inside, tile, 0.0)
        return kept if start == to else pltpu.roll(kept, (to - start) % HD, 1)

    def pack_stage(step):
        at = sum(tiles_of(heads_n, before) for before in range(step))
        for start, lanes in SEGMENTS[step]:
            per = HD // lanes
            for first in range(0, heads_n, per):
                tile = None
                for h in range(first, min(first + per, heads_n)):
                    piece = shifted(
                        prob_ref[dp, h, rows_of(step), :].astype(F32), start, lanes, (h - first) * lanes
                    )
                    tile = piece if tile is None else tile + piece
                pack_ref[dp, at] = tile.astype(BF16)
                at += 1
        for hop, to in hops:
            gather_probs(step, hop, to).start()

    def value_wait(first):
        for hop, source in hops:
            view = value_rows(first, source)
            remote(
                view, view, k_send.at[CHUNKS, hop], k_recv.at[CHUNKS, source], {"mp": other}
            ).wait_recv()

    def gather_stage(step):
        rows = rows_of(step)
        depth = (CHUNKS - step) * rows_n
        for hop, source in hops:
            view = prob_tiles(step, source)
            remote(
                view, view, k_send.at[step, hop], k_recv.at[step, source], {"mp": other}
            ).wait_recv()
            for h in range(heads_n):
                at = sum(tiles_of(heads_n, before) for before in range(step))
                whole = None
                for start, lanes in SEGMENTS[step]:
                    per = HD // lanes
                    piece = shifted(
                        pack_ref[source, at + h // per].astype(F32), h % per * lanes, lanes, start
                    )
                    whole = piece if whole is None else whole + piece
                    at += -(-heads_n // per)
                prob_ref[source, h, rows, :] = whole.astype(BF16)
            for kv in range(local_kv):
                heads = range(kv * group, (kv + 1) * group)
                left = jnp.concatenate(
                    [prob_ref[source, h, rows, pl.ds(0, depth)] for h in heads], axis=0
                )
                mixed = jnp.dot(
                    left, gval_ref[source, pl.ds(0, depth), pl.ds(kv * HD, HD)],
                    preferred_element_type=F32,
                )
                ratio = mixed / stabilize(mixed)
                for at, h in enumerate(heads):
                    ratio_ref[source, rows, h * HD:(h + 1) * HD] = (
                        ratio[at * rows_n:(at + 1) * rows_n, :]
                    )

    length = len_ref[0]
    loads[0].wait()
    loads[1].wait()
    for step in range(CHUNKS):
        rows = rows_of(step)
        hid = hid_ref[rows, :].astype(F32)
        att = att_ref[rows, :].astype(F32)
        totals = hid + att
        inverse = 1.0 / stabilize(totals)
        keep_ref[rows, :] = hid * inverse
        through_ref[rows, :] = att * inverse / stabilize(att)

        @pl.when(is_last)
        def _():
            token = (CHUNKS - 1 - step) * rows_n + lax.broadcasted_iota(
                jnp.int32, (rows_n, half), 0
            )
            inc_ref[rows, :] = jnp.where(token < length, totals, 0.0).astype(BF16)

    loads[2].wait()
    hid_all = hid_ref[...]
    for slot in range(2):
        part = jnp.dot(
            hid_all, vw_ref[:, slot * kv_half:(slot + 1) * kv_half], preferred_element_type=F32
        )
        vsend[slot] = part.astype(BF16)

        @pl.when(core == slot)
        def _():
            val_ref[...] = part

    for load in loads[3:]:
        load.wait()
    bv_ref[...] = jnp.zeros_like(bv_ref)
    barrier_wait()
    value_copy(other).start()

    @pl.when(is_last)
    def _():
        for step in range(CHUNKS - 1):
            branch_stage(step)

    query_at = lax.broadcasted_iota(jnp.int32, (seq_len, seq_len), 0)
    key_at = lax.broadcasted_iota(jnp.int32, (seq_len, seq_len), 1)
    allowed = (key_at <= query_at) & (key_at < length)
    for h in range(heads_n):
        kv = h // group
        scores = nt_dot(
            que_ref[:, h * HD:(h + 1) * HD], key_ref[:, kv * HD:(kv + 1) * HD]
        ) / math.sqrt(HD)
        scores = jnp.where(allowed, scores, -1000000000.0)
        weights = jnp.exp(scores - jnp.max(scores, axis=1, keepdims=True))
        prob_ref[dp, h] = (weights / jnp.sum(weights, axis=1, keepdims=True)).astype(BF16)

    value_copy(other).wait()
    values = (val_ref[...] + vrecv[...].astype(F32)).astype(BF16)
    gval_ref[dp] = values

    @pl.when(is_last)
    def _():
        for hop, to in hops:
            gather_value(RAW, hop, to).start()
        for step in range(RAW, CHUNKS):
            pack_stage(step)
        branch_stage(CHUNKS - 1)

    @pl.when(jnp.logical_not(is_last))
    def _():
        for hop, to in hops:
            gather_value(0, hop, to).start()
        for step in range(CHUNKS):
            pack_stage(step)

    wide_values = values.astype(F32)
    val_ref[...] = wide_values / stabilize(wide_values)
    for h in range(heads_n):
        kv = h // group
        mixed = jnp.dot(
            prob_ref[dp, h], values[:, kv * HD:(kv + 1) * HD], preferred_element_type=F32
        )
        ratio_ref[dp, :, h * HD:(h + 1) * HD] = mixed / stabilize(mixed)

    for at in range(half // HD):
        flipped = hid_ref[:, at * HD:(at + 1) * HD].astype(F32).T
        hidt_ref[pl.ds(at * HD, HD), :] = flipped.astype(BF16)
    hida_ref[dp] = hidt_ref[pl.ds(pl.multiple_of(dp * block_rows, 16), block_rows), :]

    def branch_next(step):
        section_copy(step, sec + 1).wait_recv()
        branch_stage(step)

    stages = {
        "gather": gather_stage, "part": part_stage, "mix": mix_stage, "head": head_stage,
        "take": branch_next, "linear": linear_stage, "join": join_stage,
    }

    @pl.when(is_last)
    def _():
        value_wait(RAW)
        for stage, step in LAST_ORDER:
            stages[stage](step)
        for hop, to in hops:
            hidden_copy(hop, to).start()
        for step in range(CHUNKS):
            final_out(step)

    @pl.when(jnp.logical_not(is_last))
    def _():
        for hop, to in hops:
            hidden_copy(hop, to).start()
        value_wait(0)
        for stage, step in NEXT_ORDER:
            stages[stage](step)

    heat_copy(core).start()
    for hop, source in hops:
        for step in range(CHUNKS - 1):
            final_wait(step, source, core)
        final_forward(source, core).start()
    for hop, source in hops:
        hidden_wait(hop, source).wait()
    block_at = pl.ds(pl.multiple_of(dp * block_rows, 16), block_rows)
    total = None
    for hop in range(peers):
        source = lax.rem(dp + hop, peers)
        if hop > 0:
            final_forward(source, other).wait_recv()
            for owner in range(2):
                final_wait(CHUNKS - 1, source, owner)
        sens = jnp.concatenate([sv_ref[source, 0], sv_ref[source, 1]], axis=1)
        term = jnp.dot(hida_ref[source], sens, preferred_element_type=F32)
        total = term if total is None else total + term
    rel_ref[...] = vw_ref[block_at, :].astype(F32) * total
    heat_copy(other).wait_recv()
    heat_copy(core).wait_send()
    heat_ref[...] = jnp.sum((heats[0] + heats[1]).T, axis=0, keepdims=True) / DW

    for step in range(CHUNKS):
        for block in range(blocks):
            @pl.when(core * blocks + block != dp)
            def _():
                branch_copy(step, block).wait_send()

        @pl.when(gets)
        def _():
            for source in range(peers):
                branch_forward(step, source).wait_send()

        sens_copy(step, core).wait_send()

        @pl.when(sec > 0)
        def _():
            section_copy(step, sec - 1).wait_send()

        for hop, to in hops:
            for side in range(2 if step == CHUNKS - 1 else 1):
                final_copy(step, hop, to, side).wait_send()

    for hop, source in hops:
        final_forward(source, core).wait_send()

    @pl.when(is_last)
    def _():
        for hop, to in hops:
            gather_value(RAW, hop, to).wait_send()
        for step in range(RAW):
            for turn in range(rounds):
                for at in range(peers >> (turn + 1)):
                    part_copy(step, turn, at).wait_send()
        for step in range(RAW, CHUNKS):
            for hop, to in hops:
                gather_probs(step, hop, to).wait_send()
                sum_copy(step, hop, to).wait_send()

    @pl.when(jnp.logical_not(is_last))
    def _():
        for hop, to in hops:
            gather_value(0, hop, to).wait_send()
        for step in range(CHUNKS):
            for hop, to in hops:
                gather_probs(step, hop, to).wait_send()
                sum_copy(step, hop, to).wait_send()


def on_device_chain(hidden_in, attn_out, queries, keys, value_weight, out_weight, lengths):
    peers = lax.axis_size("dp")
    sections = lax.axis_size("section")
    seq_len, half = hidden_in.shape[2:]
    kv_half = keys.shape[3]
    kv_width = value_weight.shape[2]
    width = out_weight.shape[2]
    heads = half // HD
    rows_n = seq_len // CHUNKS
    packed = sum(tiles_of(heads, step) for step in range(CHUNKS))
    vmem = pltpu.VMEM
    dma = pltpu.SemaphoreType.DMA
    whole = pl.BlockSpec(memory_space=pltpu.VMEM)
    heat, relevance = pl.pallas_call(
        functools.partial(chain_kernel, peers, sections),
        out_shape=(
            jax.ShapeDtypeStruct((1, seq_len), F32),
            jax.ShapeDtypeStruct((half // peers, kv_width), F32),
        ),
        in_specs=[pl.BlockSpec(memory_space=pltpu.SMEM)] + [pl.BlockSpec(memory_space=pl.ANY)] * 6,
        out_specs=(whole, whole),
        scratch_shapes=[
            vmem((seq_len, half), BF16),
            vmem((seq_len, half), BF16),
            vmem((seq_len, half), BF16),
            vmem((seq_len, kv_half), BF16),
            vmem((half, kv_width), BF16),
            vmem((half, width), BF16),
            dma((6,)),
            vmem((seq_len, half), F32),
            vmem((seq_len, half), F32),
            vmem((peers, seq_len, half), F32),
            vmem((seq_len, half), BF16),
            vmem((seq_len, half), BF16),
            vmem((peers, heads, seq_len, seq_len), BF16),
            vmem((peers, packed, rows_n, HD), BF16),
            vmem((peers, seq_len, kv_half), BF16),
            vmem((seq_len, kv_half), F32),
            vmem((peers, seq_len, kv_half), F32),
            vmem((2, seq_len, kv_half), BF16),
            vmem((seq_len, kv_half), BF16),
            vmem((half, seq_len), BF16),
            vmem((peers, half // peers, seq_len), BF16),
            vmem((peers, 2, seq_len, kv_half), BF16),
            vmem((2, seq_len, HD), F32),
            vmem((peers * rows_n, half), BF16),
            vmem((CHUNKS, peers, rows_n, kv_half), BF16),
            vmem((CHUNKS, peers, rows_n, kv_half), BF16),
            vmem((CHUNKS, peers // 2, rows_n, width), BF16),
            vmem((CHUNKS, peers, rows_n, width), BF16),
            vmem((RAW, peers, rows_n, half), BF16),
            vmem((RAW, peers - 1, rows_n, half), BF16),
            dma((CHUNKS, peers // 2)),
            dma((CHUNKS, peers)),
            dma((CHUNKS, peers)),
            dma((RAW, peers)),
            dma((RAW, peers)),
            dma((CHUNKS,)),
            dma((CHUNKS,)),
            dma((CHUNKS, peers, 2)),
            dma((CHUNKS, peers, 2)),
            dma((CHUNKS,)),
            dma((CHUNKS,)),
            dma((peers,)),
            dma((peers,)),
            dma((2,)),
            dma((2,)),
            dma((CHUNKS + 1, peers)),
            dma((CHUNKS + 1, peers)),
            dma((CHUNKS, peers)),
            dma((CHUNKS, peers)),
            dma((peers,)),
            dma((peers,)),
        ],
        compiler_params=pltpu.CompilerParams(
            collective_id=0, has_side_effects=True, vmem_limit_bytes=60 * 1024 * 1024
        ),
        name="relevance_chain",
    )(
        lengths, hidden_in[0, 0], attn_out[0, 0], queries[0, 0], keys[0, 0],
        value_weight[0], out_weight[0],
    )
    return heat[None], relevance[None]


def solution(mesh):
    placed = (
        P("section", ("groups", "dp"), None, "mp"),
        P("section", ("groups", "dp"), None, "mp"),
        P("section", ("groups", "dp"), None, "mp"),
        P("section", ("groups", "dp"), None, "mp"),
        P("section", "mp", None),
        P("section", "mp", "dp"),
        P(("groups", "dp")),
    )
    peers = mesh.shape["dp"]
    aligned = peers > 1 and peers & (peers - 1) == 0 and DW // peers % HD == 0
    return jax.shard_map(
        on_device_chain if aligned else on_device,
        mesh=mesh,
        in_specs=placed,
        out_specs=(
            P("section", ("groups", "dp"), None),
            P(("groups", "section"), ("mp", "dp"), None),
        ),
        check_vma=False,
    )
```

```python
import functools
import math

import jax
import jax.numpy as jnp
from jax import lax
from jax.experimental import pallas as pl
from jax.experimental.pallas import tpu as pltpu
from jax.sharding import PartitionSpec as P

DW = 2560
HD = 128
QH = 20
KVH = 4


EPS = 0.25


def from_behind(shard, axis, by):
    peers = lax.axis_size(axis)
    pairs = [(i, i + by) for i in range(peers) if 0 <= i + by < peers]
    return lax.ppermute(shard, axis, pairs)


def stabilize(entries):
    return jnp.where(entries >= 0, entries + EPS, entries - EPS)


def gated(active, compute, operand, out_shape, out_type):
    return lax.cond(active, compute, lambda unused: jnp.zeros(out_shape, out_type), operand)


def on_device(hidden_in, attn_out, queries, keys, value_weight, out_weight, lengths):
    inputs = hidden_in[0, 0]
    branch = attn_out[0, 0]
    query_rows = queries[0, 0]
    key_rows = keys[0, 0]
    value_rows = value_weight[0]
    seq_len = inputs.shape[0]
    half_width = inputs.shape[1]
    group_size = QH // KVH
    local_kv = key_rows.shape[1] // HD
    kv_width = value_rows.shape[1]
    sections = lax.axis_size("section")
    section_pos = lax.axis_index("section")
    core_pos = lax.axis_index("mp")
    out_cols = lax.all_gather(out_weight, "dp", axis=2, tiled=True)[0]
    inputs_f = inputs.astype(jnp.float32)
    branch_f = branch.astype(jnp.float32)
    totals = inputs_f + branch_f
    value_part = jnp.dot(inputs, value_rows, preferred_element_type=jnp.float32)
    value_all = lax.psum(value_part.astype(jnp.bfloat16), "mp").astype(jnp.float32)
    value_mine = lax.dynamic_slice_in_dim(value_all, core_pos * local_kv * HD, local_kv * HD, 1)
    values_bf = lax.optimization_barrier(value_mine.astype(jnp.bfloat16))
    values_f = values_bf.astype(jnp.float32)
    query_heads = query_rows.reshape(seq_len, local_kv, group_size, HD)
    key_heads = key_rows.reshape(seq_len, local_kv, HD)
    scores = jnp.einsum(
        "tgjd,sgd->gjts", query_heads, key_heads, preferred_element_type=jnp.float32
    ) / math.sqrt(HD)
    position = lax.iota(jnp.int32, seq_len)
    allowed = (position[None, :] <= position[:, None]) & (position[None, :] < lengths[0])
    scores = jnp.where(allowed, scores, -1000000000.0)
    row_top = jnp.max(scores, axis=-1, keepdims=True)
    weights = jnp.exp(scores - row_top)
    prob_rows = (weights / jnp.sum(weights, axis=-1, keepdims=True)).astype(jnp.bfloat16)
    mixed_heads = jnp.einsum(
        "gjts,sgd->tgjd",
        prob_rows,
        values_bf.reshape(seq_len, local_kv, HD),
        preferred_element_type=jnp.float32,
    ).reshape(seq_len, local_kv * group_size * HD)
    valid_rows = (position < lengths[0]).astype(jnp.float32)
    current = (totals * valid_rows[:, None]).astype(jnp.bfloat16)
    result = jnp.zeros((seq_len, half_width), jnp.bfloat16)
    sens_kept = jnp.zeros((seq_len, kv_width), jnp.bfloat16)
    for turn_index in range(sections):
        active = section_pos == sections - 1 - turn_index
        sens_total = current.astype(jnp.float32) / stabilize(totals)
        sens_branch = (branch_f * sens_total / stabilize(branch_f)).astype(jnp.bfloat16)
        sens_full = lax.all_gather(sens_branch, "mp", axis=1, tiled=True)

        def through_heads(operand):
            back_mixed = lax.dot_general(
                operand, out_cols, (((1,), (1,)), ((), ())), preferred_element_type=jnp.float32
            )
            sens_mixed = (mixed_heads * back_mixed / stabilize(mixed_heads)).astype(jnp.bfloat16)
            back_values = jnp.einsum(
                "gjts,tgjd->sgd",
                prob_rows,
                sens_mixed.reshape(seq_len, local_kv, group_size, HD),
                preferred_element_type=jnp.float32,
            ).reshape(seq_len, local_kv * HD)
            return (values_f * back_values / stabilize(values_f)).astype(jnp.bfloat16)

        sens_values = gated(
            active, through_heads, sens_full, (seq_len, local_kv * HD), jnp.bfloat16
        )
        sens_all = lax.all_gather(sens_values, "mp", axis=1, tiled=True)

        def through_values(operand):
            back_inputs = lax.dot_general(
                operand, value_rows, (((1,), (1,)), ((), ())), preferred_element_type=jnp.float32
            )
            return (inputs_f * sens_total + inputs_f * back_inputs).astype(jnp.bfloat16)

        outgoing = gated(active, through_values, sens_all, (seq_len, half_width), jnp.bfloat16)
        result = jnp.where(active, outgoing, result)
        sens_kept = jnp.where(active, sens_all, sens_kept)
        if turn_index + 1 < sections:
            arrived = from_behind(outgoing, "section", -1)
            current = jnp.where(section_pos == sections - 2 - turn_index, arrived, current)
    heat_part = jnp.sum(result.astype(jnp.float32), axis=1)
    heat_rows = lax.psum(heat_part, "mp") / DW
    block_rows = half_width // lax.axis_size("dp")
    row_start = lax.axis_index("dp") * block_rows
    value_block = lax.dynamic_slice_in_dim(value_rows, row_start, block_rows, 0).astype(jnp.float32)
    summed = lax.psum_scatter(
        lax.dot_general(
            inputs, sens_kept, (((0,), (0,)), ((), ())), preferred_element_type=jnp.float32
        ).astype(jnp.bfloat16),
        "dp",
        scatter_dimension=0,
        tiled=True,
    ).astype(jnp.float32)
    relevance_rows = value_block * summed
    return (heat_rows[None, None, :], relevance_rows[None])


CHUNKS = 4
RAW = 3
SEGMENTS = (((0, 128),), ((0, 64), (64, 32)), ((0, 64),), ((0, 32),))
TILE = 256
MESH_ID = pl.DeviceIdType.MESH
F32 = jnp.float32
BF16 = jnp.bfloat16
DIRECT = 2
LAST_ORDER = (
    ("part", 0), ("part", 1), ("branch", 3), ("mix", 0), ("part", 2), ("head", 0), ("mix", 1), ("values", 3),
    ("gather", 3), ("linear", 3), ("head", 1), ("mix", 2), ("head", 2), ("join", 3), ("hidden", 3),
)
NEXT_ORDER = (
    ("values", 0), ("gather", 0), ("gather", 1), ("gather", 2), ("gather", 3), ("hidden", 0),
    ("take", 0), ("linear", 0), ("take", 1), ("join", 0), ("linear", 1), ("join", 1),
    ("linear", 2), ("linear", 3), ("join", 2), ("join", 3),
)


def tiles_of(heads, step):
    return sum(-(-heads // (HD // lanes)) for _, lanes in SEGMENTS[step])


def nt_dot(left, right):
    return lax.dot_general(left, right, (((1,), (1,)), ((), ())), preferred_element_type=F32)


def tn_dot(left, right):
    return lax.dot_general(left, right, (((0,), (0,)), ((), ())), preferred_element_type=F32)


def chain_kernel(
    peers, sections, len_ref, hid_in, att_in, que_in, key_in, vw_in, ow_in,
    heat_ref, rel_ref, hid_ref, att_ref, que_ref, key_ref, vw_ref, ow_ref, load_sem,
    through_ref, keep_ref, ratio_ref, inc_ref, out_ref, prob_ref, pack_ref, gval_ref, val_ref, bv_ref,
    vsend, vrecv, hidt_ref, hida_ref, sv_ref, heats, sm_ref, bvsend, bvbuf,
    asend, abuf, psend, pbuf, below_ref, dsend,
    a_send, g_send, a_recv, p_send, p_recv, s_send, s_recv, f_send, f_recv,
    x_send, x_recv, h_send, h_recv, one_send, one_recv,
    k_send, k_recv, b_send, b_recv, w_send, w_recv, r_send, t_send, t_recv, d_send,
):
    dp = lax.axis_index("dp")
    sec = lax.axis_index("section")
    core = lax.axis_index("mp")
    other = 1 - core
    seq_len, half = hid_ref.shape
    rows_n = seq_len // CHUNKS
    width = ow_ref.shape[1]
    blocks = peers // 2
    local_kv = key_ref.shape[1] // HD
    group = QH // KVH
    heads_n = local_kv * group
    kv_half = local_kv * HD
    block_rows = half // peers
    is_last = sec == sections - 1
    gets = core == dp // blocks
    hops = [(hop, lax.rem(dp + hop, peers)) for hop in range(1, peers)]

    loads = [
        pltpu.make_async_copy(source, target, load_sem.at[at])
        for at, (source, target) in enumerate((
            (hid_in, hid_ref), (att_in, att_ref), (vw_in, vw_ref),
            (que_in, que_ref), (key_in, key_ref), (ow_in, ow_ref),
        ))
    ]
    for load in loads:
        load.start()

    barrier = pltpu.get_barrier_semaphore()
    for hop, to in hops:
        for target in range(2):
            pl.semaphore_signal(
                barrier, inc=1, device_id={"dp": to, "mp": target}, device_id_type=MESH_ID
            )
    pl.semaphore_signal(barrier, inc=1, device_id={"mp": other}, device_id_type=MESH_ID)

    @pl.when(sec > 0)
    def _():
        pl.semaphore_signal(
            barrier, inc=1, device_id={"section": sec - 1}, device_id_type=MESH_ID
        )

    @pl.when(sec < sections - 1)
    def _():
        for at in range(peers):
            pl.semaphore_signal(
                barrier, inc=1, device_id={"dp": at, "section": sec + 1}, device_id_type=MESH_ID
            )

    def barrier_wait():
        greeted = 2 * (peers - 1) + 1

        @pl.when(is_last)
        def _():
            pl.semaphore_wait(barrier, greeted + peers)

        @pl.when(jnp.logical_not(is_last))
        def _():
            pl.semaphore_wait(barrier, greeted + 1)

    def remote(source, target, send, recv, device):
        return pltpu.make_async_remote_copy(
            src_ref=source, dst_ref=target, send_sem=send, recv_sem=recv,
            device_id=device, device_id_type=MESH_ID,
        )

    def rows_of(step):
        return pl.ds((CHUNKS - 1 - step) * rows_n, rows_n)

    def branch_copy(step, block):
        return remote(
            asend.at[step, block], abuf.at[step, dp],
            a_send.at[step, block], a_recv.at[step, dp], {"dp": core * blocks + block},
        )

    def direct_copy(step, block):
        return remote(
            dsend.at[step - DIRECT, block], abuf.at[step, dp],
            d_send.at[step - DIRECT, block], a_recv.at[step, dp],
            {"dp": core * blocks + block, "section": sec - 1},
        )

    def through_copy(step, target):
        rows = rows_of(step)
        return remote(
            through_ref.at[rows], below_ref.at[rows],
            t_send.at[step], t_recv.at[step], {"section": target},
        )

    def branch_forward(step, source):
        view = abuf.at[step, source]
        return remote(
            view, view, g_send.at[step, source], a_recv.at[step, source], {"mp": other}
        )

    rounds = peers.bit_length() - 1

    def slot_of(turn, target):
        return peers - (peers >> turn) + target // (2 << turn)

    def part_target(turn, at):
        bit = 1 << turn
        return lax.rem(dp, bit) + bit * (2 * at + 1 - lax.rem(dp // bit, 2))

    def part_copy(step, turn, at):
        bit = 1 << turn
        slot = peers - (peers >> turn) + at
        return remote(
            psend.at[step, part_target(turn, at)], pbuf.at[step, slot],
            p_send.at[step, slot], p_recv.at[step, slot],
            {"dp": dp + bit - 2 * bit * lax.rem(dp // bit, 2)},
        )

    def part_take(step, turn, target):
        slot = slot_of(turn, target)
        view = pbuf.at[step, slot]
        remote(
            view, view, p_send.at[step, slot], p_recv.at[step, slot], {"mp": other}
        ).wait_recv()
        return pbuf[step, slot].astype(F32)

    def mix_stage(step):
        for turn in range(1, rounds):
            for at in range(peers >> (turn + 1)):
                target = part_target(turn, at)
                running = psend[step, target].astype(F32)
                for before in range(turn):
                    running = running + part_take(step, before, target)
                psend[step, target] = running.astype(BF16)
                part_copy(step, turn, at).start()

    def value_rows(step, source):
        return gval_ref.at[source, pl.ds(0, (CHUNKS - step) * rows_n)]

    def prob_tiles(step, source):
        first = sum(tiles_of(heads_n, before) for before in range(step))
        return pack_ref.at[source, pl.ds(first, tiles_of(heads_n, step))]

    def gather_value(first, hop, to):
        view = value_rows(first, dp)
        return remote(
            view, view, k_send.at[CHUNKS, hop], k_recv.at[CHUNKS, dp], {"dp": to}
        )

    def gather_probs(step, hop, to):
        view = prob_tiles(step, dp)
        return remote(view, view, k_send.at[step, hop], k_recv.at[step, dp], {"dp": to})

    def sum_copy(step, hop, to):
        return remote(
            bvsend.at[step, hop], bvbuf.at[step, dp],
            b_send.at[step, hop], b_recv.at[step, dp], {"dp": to},
        )

    def sens_copy(step, owner):
        view = sv_ref.at[dp, owner, rows_of(step)]
        return remote(view, view, s_send.at[step], s_recv.at[step], {"mp": other})

    def final_copy(step, hop, to, side):
        view = sv_ref.at[dp, core, rows_of(step)]
        return remote(
            view, view, f_send.at[step, hop, side], f_recv.at[step, dp, core],
            {"dp": to, "mp": core if side == 0 else other},
        )

    def final_wait(step, source, owner):
        view = sv_ref.at[source, owner, rows_of(step)]
        remote(
            view, view, f_send.at[step, 0, 0], f_recv.at[step, source, owner], {"mp": other}
        ).wait_recv()

    def final_forward(source, owner):
        view = sv_ref.at[source, owner, pl.ds(rows_n, seq_len - rows_n)]
        return remote(view, view, w_send.at[source], w_recv.at[source], {"mp": other})

    def final_out(step):
        for hop, to in hops:
            for side in range(2 if step == CHUNKS - 1 else 1):
                final_copy(step, hop, to, side).start()

    def section_copy(step, target):
        return remote(
            out_ref.at[rows_of(step)], inc_ref.at[rows_of(step)],
            x_send.at[step], x_recv.at[step], {"section": target},
        )

    def hidden_copy(hop, to):
        return remote(
            hidt_ref.at[pl.ds(pl.multiple_of(to * block_rows, 16), block_rows)], hida_ref.at[dp],
            h_send.at[hop], h_recv.at[dp], {"dp": to},
        )

    def hidden_wait(hop, source):
        return remote(
            hidt_ref.at[pl.ds(0, block_rows)], hida_ref.at[source],
            h_send.at[hop], h_recv.at[source], {"mp": other},
        )

    def value_copy(slot):
        return remote(
            vsend.at[slot], vrecv, one_send.at[0], one_recv.at[0], {"mp": other}
        )

    def heat_copy(slot):
        return remote(
            heats.at[slot], heats.at[slot], one_send.at[1], one_recv.at[1], {"mp": other}
        )

    def branch_stage(step):
        rows = rows_of(step)
        sens = (inc_ref[rows, :].astype(F32) * through_ref[rows, :]).astype(BF16)
        for block in range(blocks):
            to = core * blocks + block
            piece = sens[:, block * width:(block + 1) * width]
            asend[step, block] = piece

            @pl.when(to == dp)
            def _():
                abuf[step, dp] = piece
                branch_forward(step, dp).start()

            @pl.when(to != dp)
            def _():
                branch_copy(step, block).start()

    def branch_wait(step, direct):
        @pl.when(gets)
        def _():
            for hop in range(0 if direct else 1, peers):
                source = lax.rem(dp + hop, peers)
                branch_forward(step, source).wait_recv()
                branch_forward(step, source).start()

        @pl.when(jnp.logical_not(gets))
        def _():
            for source in range(peers):
                branch_forward(step, source).wait_recv()

        return abuf[step].reshape(peers * rows_n, width)

    def part_stage(step):
        stacked = branch_wait(step, False)

        def tile(at, unused):
            start = pl.multiple_of(at * TILE, TILE)
            part = nt_dot(stacked, ow_ref[pl.ds(start, TILE), :]).astype(BF16)
            psend[step, :, :, pl.ds(start, TILE)] = part.reshape(peers, rows_n, TILE)
            return unused

        lax.fori_loop(0, half // TILE, tile, 0, unroll=True)
        for at in range(peers // 2):
            part_copy(step, 0, at).start()

    def add_values(seq, rows, mixed):
        for kv in range(local_kv):
            heads = range(kv * group, (kv + 1) * group)
            left = jnp.concatenate([prob_ref[seq, h, rows, :] for h in heads], axis=0)
            right = jnp.concatenate([mixed[:, h * HD:(h + 1) * HD] for h in heads], axis=0)
            columns = pl.ds(kv * HD, HD)
            bv_ref[seq, :, columns] = bv_ref[seq, :, columns] + tn_dot(left, right)

    def head_stage(step):
        rows = rows_of(step)
        back = psend[step, dp].astype(F32)
        for turn in range(rounds):
            back = back + part_take(step, turn, dp)
        add_values(dp, rows, (ratio_ref[dp, rows, :] * back).astype(BF16))
        finish(step, bv_ref[dp, rows, :])

    def linear_stage(step, direct=False):
        rows = rows_of(step)
        stacked = branch_wait(step, direct)
        for at in range(half // TILE):
            columns = pl.ds(at * TILE, TILE)
            part = nt_dot(stacked, ow_ref[columns, :])
            ratio = ratio_ref[:, rows, columns].reshape(peers * rows_n, TILE)
            sm_ref[:, columns] = (ratio * part).astype(BF16)
        for seq in range(peers):
            add_values(seq, rows, sm_ref[seq * rows_n:(seq + 1) * rows_n, :])
        for hop, to in hops:
            bvsend[step, hop] = bv_ref[to, rows, :].astype(BF16)
            sum_copy(step, hop, to).start()

    def join_stage(step):
        total = bv_ref[dp, rows_of(step), :]
        for hop, source in hops:
            view = bvbuf.at[step, source]
            remote(
                view, view, b_send.at[step, hop], b_recv.at[step, source], {"mp": other}
            ).wait_recv()
            total = total + bvbuf[step, source].astype(F32)
        finish(step, total)

    def finish(step, back_values):
        rows = rows_of(step)
        sv_ref[dp, core, rows, :] = (val_ref[rows, :] * back_values).astype(BF16)
        sens_copy(step, core).start()

        @pl.when(jnp.logical_not(is_last))
        def _():
            final_out(step)

        sens_copy(step, other).wait_recv()
        sens = jnp.concatenate([sv_ref[dp, 0, rows, :], sv_ref[dp, 1, rows, :]], axis=1)
        sums = jnp.zeros((rows_n, HD), F32)
        for at in range(half // TILE):
            columns = pl.ds(at * TILE, TILE)
            back_in = nt_dot(sens, vw_ref[columns, :])
            out = (
                inc_ref[rows, columns].astype(F32) * keep_ref[rows, columns]
                + hid_ref[rows, columns].astype(F32) * back_in
            ).astype(BF16)
            out_ref[rows, columns] = out
            wide = out.astype(F32)
            for lane in range(TILE // HD):
                sums = sums + wide[:, lane * HD:(lane + 1) * HD]
        heats[core, rows, :] = sums

        @pl.when(sec > 0)
        def _():
            if step >= DIRECT:
                through_copy(step, sec - 1).wait_recv()
                below = (out_ref[rows, :].astype(F32) * below_ref[rows, :]).astype(BF16)
                for block in range(blocks):
                    dsend[step - DIRECT, block] = below[:, block * width:(block + 1) * width]
                    direct_copy(step, block).start()
            section_copy(step, sec - 1).start()

    lane_at = lax.broadcasted_iota(jnp.int32, (rows_n, HD), 1)

    def shifted(tile, start, count, to):
        inside = (lane_at >= start) & (lane_at < start + count)
        kept = jnp.where(inside, tile, 0.0)
        return kept if start == to else pltpu.roll(kept, (to - start) % HD, 1)

    def pack_stage(step, relay=False):
        at = sum(tiles_of(heads_n, before) for before in range(step))
        for start, lanes in SEGMENTS[step]:
            per = HD // lanes
            for first in range(0, heads_n, per):
                tile = None
                for h in range(first, min(first + per, heads_n)):
                    piece = shifted(
                        prob_ref[dp, h, rows_of(step), :].astype(F32), start, lanes, (h - first) * lanes
                    )
                    tile = piece if tile is None else tile + piece
                pack_ref[dp, at] = tile.astype(BF16)
                at += 1
        for hop, to in hops:
            if relay:
                @pl.when(jnp.logical_not(far(to)))
                def _():
                    gather_probs(step, hop, to).start()
            else:
                gather_probs(step, hop, to).start()

    def value_wait(first, relay=False):
        for hop, source in hops:
            view = value_rows(first, source)
            remote(
                view, view, k_send.at[CHUNKS, hop], k_recv.at[CHUNKS, source], {"mp": other}
            ).wait_recv()
            if relay:
                @pl.when(relays(source))
                def _():
                    relay_copy(CHUNKS, view, source).start()

    def relays(source):
        return jnp.logical_or(
            jnp.logical_and(source == 0, dp == peers - 2),
            jnp.logical_and(source == peers - 1, dp == 1),
        )

    def far(to):
        return jnp.logical_and(dp + to == peers - 1, jnp.logical_or(dp == 0, to == 0))

    def relay_copy(step, view, source):
        return remote(
            view, view, r_send.at[step], k_recv.at[step, source], {"dp": peers - 1 - source}
        )

    def gather_stage(step, relay=False):
        rows = rows_of(step)
        depth = (CHUNKS - step) * rows_n
        for hop, source in hops:
            view = prob_tiles(step, source)
            remote(
                view, view, k_send.at[step, hop], k_recv.at[step, source], {"mp": other}
            ).wait_recv()
            if relay:
                @pl.when(relays(source))
                def _():
                    relay_copy(step, view, source).start()
            for h in range(heads_n):
                at = sum(tiles_of(heads_n, before) for before in range(step))
                whole = None
                for start, lanes in SEGMENTS[step]:
                    per = HD // lanes
                    piece = shifted(
                        pack_ref[source, at + h // per].astype(F32), h % per * lanes, lanes, start
                    )
                    whole = piece if whole is None else whole + piece
                    at += -(-heads_n // per)
                prob_ref[source, h, rows, :] = whole.astype(BF16)
            for kv in range(local_kv):
                heads = range(kv * group, (kv + 1) * group)
                left = jnp.concatenate(
                    [prob_ref[source, h, rows, pl.ds(0, depth)] for h in heads], axis=0
                )
                mixed = jnp.dot(
                    left, gval_ref[source, pl.ds(0, depth), pl.ds(kv * HD, HD)],
                    preferred_element_type=F32,
                )
                ratio = mixed / stabilize(mixed)
                for at, h in enumerate(heads):
                    ratio_ref[source, rows, h * HD:(h + 1) * HD] = (
                        ratio[at * rows_n:(at + 1) * rows_n, :]
                    )

    length = len_ref[0]
    loads[0].wait()
    loads[1].wait()
    for step in range(CHUNKS):
        rows = rows_of(step)
        hid = hid_ref[rows, :].astype(F32)
        att = att_ref[rows, :].astype(F32)
        totals = hid + att
        inverse = 1.0 / stabilize(totals)
        keep_ref[rows, :] = hid * inverse
        through_ref[rows, :] = att * inverse / stabilize(att)

        @pl.when(is_last)
        def _():
            token = (CHUNKS - 1 - step) * rows_n + lax.broadcasted_iota(
                jnp.int32, (rows_n, half), 0
            )
            inc_ref[rows, :] = jnp.where(token < length, totals, 0.0).astype(BF16)

    loads[2].wait()
    hid_all = hid_ref[...]
    for slot in range(2):
        part = jnp.dot(
            hid_all, vw_ref[:, slot * kv_half:(slot + 1) * kv_half], preferred_element_type=F32
        )
        vsend[slot] = part.astype(BF16)

        @pl.when(core == slot)
        def _():
            val_ref[...] = part

    for load in loads[3:]:
        load.wait()
    bv_ref[...] = jnp.zeros_like(bv_ref)
    barrier_wait()
    value_copy(other).start()

    @pl.when(is_last)
    def _():
        branch_stage(0)

    @pl.when(jnp.logical_not(is_last))
    def _():
        for step in range(DIRECT, CHUNKS):
            through_copy(step, sec + 1).start()

    query_at = lax.broadcasted_iota(jnp.int32, (seq_len, seq_len), 0)
    key_at = lax.broadcasted_iota(jnp.int32, (seq_len, seq_len), 1)
    allowed = (key_at <= query_at) & (key_at < length)
    for h in range(heads_n):
        kv = h // group
        scores = nt_dot(
            que_ref[:, h * HD:(h + 1) * HD], key_ref[:, kv * HD:(kv + 1) * HD]
        ) / math.sqrt(HD)
        scores = jnp.where(allowed, scores, -1000000000.0)
        weights = jnp.exp(scores - jnp.max(scores, axis=1, keepdims=True))
        prob_ref[dp, h] = (weights / jnp.sum(weights, axis=1, keepdims=True)).astype(BF16)

    @pl.when(is_last)
    def _():
        branch_stage(1)

    value_copy(other).wait()
    values = (val_ref[...] + vrecv[...].astype(F32)).astype(BF16)
    gval_ref[dp] = values

    @pl.when(is_last)
    def _():
        for hop, to in hops:
            gather_value(RAW, hop, to).start()
        for step in range(RAW, CHUNKS):
            pack_stage(step)
        branch_stage(2)

    @pl.when(jnp.logical_not(is_last))
    def _():
        for hop, to in hops:
            @pl.when(jnp.logical_not(far(to)))
            def _():
                gather_value(0, hop, to).start()
        for step in range(CHUNKS):
            pack_stage(step, True)

    wide_values = values.astype(F32)
    val_ref[...] = wide_values / stabilize(wide_values)
    for h in range(heads_n):
        kv = h // group
        mixed = jnp.dot(
            prob_ref[dp, h], values[:, kv * HD:(kv + 1) * HD], preferred_element_type=F32
        )
        ratio_ref[dp, :, h * HD:(h + 1) * HD] = mixed / stabilize(mixed)

    for at in range(half // HD):
        flipped = hid_ref[:, at * HD:(at + 1) * HD].astype(F32).T
        hidt_ref[pl.ds(at * HD, HD), :] = flipped.astype(BF16)
    hida_ref[dp] = hidt_ref[pl.ds(pl.multiple_of(dp * block_rows, 16), block_rows), :]

    def branch_next(step):
        section_copy(step, sec + 1).wait_recv()
        branch_stage(step)

    def hidden_stage(step):
        if step == CHUNKS - 1:
            for at in range(DIRECT, CHUNKS):
                for block in range(blocks):
                    direct_copy(at, block).wait_send()
        for hop, to in hops:
            hidden_copy(hop, to).start()

    def join_next(step):
        if step >= DIRECT:
            section_copy(step, sec + 1).wait_recv()
        join_stage(step)

    stages = {
        "values": value_wait, "hidden": hidden_stage, "branch": branch_stage,
        "gather": gather_stage, "part": part_stage, "mix": mix_stage, "head": head_stage,
        "take": branch_next, "linear": linear_stage, "join": join_stage,
    }

    @pl.when(is_last)
    def _():
        for stage, step in LAST_ORDER:
            stages[stage](step)
        for step in range(CHUNKS):
            final_out(step)

    @pl.when(jnp.logical_not(is_last))
    def _():
        stages["values"] = functools.partial(value_wait, relay=True)
        stages["gather"] = functools.partial(gather_stage, relay=True)
        stages["join"] = join_next
        for stage, step in NEXT_ORDER:
            if stage == "linear":
                stages[stage] = functools.partial(linear_stage, direct=step >= DIRECT)
            stages[stage](step)

    heat_copy(core).start()
    for hop, source in hops:
        for step in range(CHUNKS - 1):
            final_wait(step, source, core)
        final_forward(source, core).start()
    for hop, source in hops:
        hidden_wait(hop, source).wait()
    for step in range(CHUNKS):
        for block in range(blocks):
            mine = core * blocks + block != dp

            @pl.when(mine if step < DIRECT else jnp.logical_and(mine, is_last))
            def _():
                branch_copy(step, block).wait_send()

        @pl.when(gets)
        def _():
            for source in range(peers):
                branch_forward(step, source).wait_send()

        sens_copy(step, core).wait_send()

        @pl.when(sec > 0)
        def _():
            section_copy(step, sec - 1).wait_send()

    def sent(first, hop, to):
        gather_value(first, hop, to).wait_send()
        for step in range(first, CHUNKS):
            gather_probs(step, hop, to).wait_send()

    @pl.when(is_last)
    def _():
        for hop, to in hops:
            sent(RAW, hop, to)
            for step in range(RAW, CHUNKS):
                sum_copy(step, hop, to).wait_send()
        for step in range(RAW):
            for turn in range(rounds):
                for at in range(peers >> (turn + 1)):
                    part_copy(step, turn, at).wait_send()

    @pl.when(jnp.logical_not(is_last))
    def _():
        for step in range(DIRECT, CHUNKS):
            through_copy(step, sec + 1).wait_send()
        for hop, to in hops:
            @pl.when(jnp.logical_not(far(to)))
            def _():
                sent(0, hop, to)

            @pl.when(relays(to))
            def _():
                relay_copy(CHUNKS, value_rows(0, to), to).wait_send()
                for step in range(CHUNKS):
                    relay_copy(step, prob_tiles(step, to), to).wait_send()
            for step in range(CHUNKS):
                sum_copy(step, hop, to).wait_send()

    block_at = pl.ds(pl.multiple_of(dp * block_rows, 16), block_rows)
    total = None
    for hop in range(peers):
        source = lax.rem(dp + hop, peers)
        if hop > 0:
            final_forward(source, other).wait_recv()
            for owner in range(2):
                final_wait(CHUNKS - 1, source, owner)
        sens = jnp.concatenate([sv_ref[source, 0], sv_ref[source, 1]], axis=1)
        term = jnp.dot(hida_ref[source], sens, preferred_element_type=F32)
        total = term if total is None else total + term
    rel_ref[...] = vw_ref[block_at, :].astype(F32) * total
    heat_copy(other).wait_recv()
    heat_copy(core).wait_send()
    heat_ref[...] = jnp.sum((heats[0] + heats[1]).T, axis=0, keepdims=True) / DW

    for hop, to in hops:
        for step in range(CHUNKS):
            for side in range(2 if step == CHUNKS - 1 else 1):
                final_copy(step, hop, to, side).wait_send()
    for hop, source in hops:
        final_forward(source, core).wait_send()


def on_device_chain(hidden_in, attn_out, queries, keys, value_weight, out_weight, lengths):
    peers = lax.axis_size("dp")
    sections = lax.axis_size("section")
    seq_len, half = hidden_in.shape[2:]
    kv_half = keys.shape[3]
    kv_width = value_weight.shape[2]
    width = out_weight.shape[2]
    heads = half // HD
    rows_n = seq_len // CHUNKS
    packed = sum(tiles_of(heads, step) for step in range(CHUNKS))
    vmem = pltpu.VMEM
    dma = pltpu.SemaphoreType.DMA
    whole = pl.BlockSpec(memory_space=pltpu.VMEM)
    heat, relevance = pl.pallas_call(
        functools.partial(chain_kernel, peers, sections),
        out_shape=(
            jax.ShapeDtypeStruct((1, seq_len), F32),
            jax.ShapeDtypeStruct((half // peers, kv_width), F32),
        ),
        in_specs=[pl.BlockSpec(memory_space=pltpu.SMEM)] + [pl.BlockSpec(memory_space=pl.ANY)] * 6,
        out_specs=(whole, whole),
        scratch_shapes=[
            vmem((seq_len, half), BF16),
            vmem((seq_len, half), BF16),
            vmem((seq_len, half), BF16),
            vmem((seq_len, kv_half), BF16),
            vmem((half, kv_width), BF16),
            vmem((half, width), BF16),
            dma((6,)),
            vmem((seq_len, half), F32),
            vmem((seq_len, half), F32),
            vmem((peers, seq_len, half), F32),
            vmem((seq_len, half), BF16),
            vmem((seq_len, half), BF16),
            vmem((peers, heads, seq_len, seq_len), BF16),
            vmem((peers, packed, rows_n, HD), BF16),
            vmem((peers, seq_len, kv_half), BF16),
            vmem((seq_len, kv_half), F32),
            vmem((peers, seq_len, kv_half), F32),
            vmem((2, seq_len, kv_half), BF16),
            vmem((seq_len, kv_half), BF16),
            vmem((half, seq_len), BF16),
            vmem((peers, half // peers, seq_len), BF16),
            vmem((peers, 2, seq_len, kv_half), BF16),
            vmem((2, seq_len, HD), F32),
            vmem((peers * rows_n, half), BF16),
            vmem((CHUNKS, peers, rows_n, kv_half), BF16),
            vmem((CHUNKS, peers, rows_n, kv_half), BF16),
            vmem((CHUNKS, peers // 2, rows_n, width), BF16),
            vmem((CHUNKS, peers, rows_n, width), BF16),
            vmem((RAW, peers, rows_n, half), BF16),
            vmem((RAW, peers - 1, rows_n, half), BF16),
            vmem((seq_len, half), F32),
            vmem((CHUNKS - DIRECT, peers // 2, rows_n, width), BF16),
            dma((CHUNKS, peers // 2)),
            dma((CHUNKS, peers)),
            dma((CHUNKS, peers)),
            dma((RAW, peers)),
            dma((RAW, peers)),
            dma((CHUNKS,)),
            dma((CHUNKS,)),
            dma((CHUNKS, peers, 2)),
            dma((CHUNKS, peers, 2)),
            dma((CHUNKS,)),
            dma((CHUNKS,)),
            dma((peers,)),
            dma((peers,)),
            dma((2,)),
            dma((2,)),
            dma((CHUNKS + 1, peers)),
            dma((CHUNKS + 1, peers)),
            dma((CHUNKS, peers)),
            dma((CHUNKS, peers)),
            dma((peers,)),
            dma((peers,)),
            dma((CHUNKS + 1,)),
            dma((CHUNKS,)),
            dma((CHUNKS,)),
            dma((CHUNKS - DIRECT, peers // 2)),
        ],
        compiler_params=pltpu.CompilerParams(
            collective_id=0, has_side_effects=True, vmem_limit_bytes=60 * 1024 * 1024
        ),
        name="relevance_chain",
    )(
        lengths, hidden_in[0, 0], attn_out[0, 0], queries[0, 0], keys[0, 0],
        value_weight[0], out_weight[0],
    )
    return heat[None], relevance[None]


def solution(mesh):
    placed = (
        P("section", ("groups", "dp"), None, "mp"),
        P("section", ("groups", "dp"), None, "mp"),
        P("section", ("groups", "dp"), None, "mp"),
        P("section", ("groups", "dp"), None, "mp"),
        P("section", "mp", None),
        P("section", "mp", "dp"),
        P(("groups", "dp")),
    )
    peers = mesh.shape["dp"]
    aligned = peers == 4 and mesh.shape["section"] == 2
    return jax.shard_map(
        on_device_chain if aligned else on_device,
        mesh=mesh,
        in_specs=placed,
        out_specs=(
            P("section", ("groups", "dp"), None),
            P(("groups", "section"), ("mp", "dp"), None),
        ),
        check_vma=False,
    )
```

```python
import functools
import math

import jax
import jax.numpy as jnp
from jax import lax
from jax.experimental import pallas as pl
from jax.experimental.pallas import tpu as pltpu
from jax.sharding import PartitionSpec as P

DW = 2560
HD = 128
QH = 20
KVH = 4


EPS = 0.25


def from_behind(shard, axis, by):
    peers = lax.axis_size(axis)
    pairs = [(i, i + by) for i in range(peers) if 0 <= i + by < peers]
    return lax.ppermute(shard, axis, pairs)


def stabilize(entries):
    return jnp.where(entries >= 0, entries + EPS, entries - EPS)


def gated(active, compute, operand, out_shape, out_type):
    return lax.cond(active, compute, lambda unused: jnp.zeros(out_shape, out_type), operand)


def on_device(hidden_in, attn_out, queries, keys, value_weight, out_weight, lengths):
    inputs = hidden_in[0, 0]
    branch = attn_out[0, 0]
    query_rows = queries[0, 0]
    key_rows = keys[0, 0]
    value_rows = value_weight[0]
    seq_len = inputs.shape[0]
    half_width = inputs.shape[1]
    group_size = QH // KVH
    local_kv = key_rows.shape[1] // HD
    kv_width = value_rows.shape[1]
    sections = lax.axis_size("section")
    section_pos = lax.axis_index("section")
    core_pos = lax.axis_index("mp")
    out_cols = lax.all_gather(out_weight, "dp", axis=2, tiled=True)[0]
    inputs_f = inputs.astype(jnp.float32)
    branch_f = branch.astype(jnp.float32)
    totals = inputs_f + branch_f
    value_part = jnp.dot(inputs, value_rows, preferred_element_type=jnp.float32)
    value_all = lax.psum(value_part.astype(jnp.bfloat16), "mp").astype(jnp.float32)
    value_mine = lax.dynamic_slice_in_dim(value_all, core_pos * local_kv * HD, local_kv * HD, 1)
    values_bf = lax.optimization_barrier(value_mine.astype(jnp.bfloat16))
    values_f = values_bf.astype(jnp.float32)
    query_heads = query_rows.reshape(seq_len, local_kv, group_size, HD)
    key_heads = key_rows.reshape(seq_len, local_kv, HD)
    scores = jnp.einsum(
        "tgjd,sgd->gjts", query_heads, key_heads, preferred_element_type=jnp.float32
    ) / math.sqrt(HD)
    position = lax.iota(jnp.int32, seq_len)
    allowed = (position[None, :] <= position[:, None]) & (position[None, :] < lengths[0])
    scores = jnp.where(allowed, scores, -1000000000.0)
    row_top = jnp.max(scores, axis=-1, keepdims=True)
    weights = jnp.exp(scores - row_top)
    prob_rows = (weights / jnp.sum(weights, axis=-1, keepdims=True)).astype(jnp.bfloat16)
    mixed_heads = jnp.einsum(
        "gjts,sgd->tgjd",
        prob_rows,
        values_bf.reshape(seq_len, local_kv, HD),
        preferred_element_type=jnp.float32,
    ).reshape(seq_len, local_kv * group_size * HD)
    valid_rows = (position < lengths[0]).astype(jnp.float32)
    current = (totals * valid_rows[:, None]).astype(jnp.bfloat16)
    result = jnp.zeros((seq_len, half_width), jnp.bfloat16)
    sens_kept = jnp.zeros((seq_len, kv_width), jnp.bfloat16)
    for turn_index in range(sections):
        active = section_pos == sections - 1 - turn_index
        sens_total = current.astype(jnp.float32) / stabilize(totals)
        sens_branch = (branch_f * sens_total / stabilize(branch_f)).astype(jnp.bfloat16)
        sens_full = lax.all_gather(sens_branch, "mp", axis=1, tiled=True)

        def through_heads(operand):
            back_mixed = lax.dot_general(
                operand, out_cols, (((1,), (1,)), ((), ())), preferred_element_type=jnp.float32
            )
            sens_mixed = (mixed_heads * back_mixed / stabilize(mixed_heads)).astype(jnp.bfloat16)
            back_values = jnp.einsum(
                "gjts,tgjd->sgd",
                prob_rows,
                sens_mixed.reshape(seq_len, local_kv, group_size, HD),
                preferred_element_type=jnp.float32,
            ).reshape(seq_len, local_kv * HD)
            return (values_f * back_values / stabilize(values_f)).astype(jnp.bfloat16)

        sens_values = gated(
            active, through_heads, sens_full, (seq_len, local_kv * HD), jnp.bfloat16
        )
        sens_all = lax.all_gather(sens_values, "mp", axis=1, tiled=True)

        def through_values(operand):
            back_inputs = lax.dot_general(
                operand, value_rows, (((1,), (1,)), ((), ())), preferred_element_type=jnp.float32
            )
            return (inputs_f * sens_total + inputs_f * back_inputs).astype(jnp.bfloat16)

        outgoing = gated(active, through_values, sens_all, (seq_len, half_width), jnp.bfloat16)
        result = jnp.where(active, outgoing, result)
        sens_kept = jnp.where(active, sens_all, sens_kept)
        if turn_index + 1 < sections:
            arrived = from_behind(outgoing, "section", -1)
            current = jnp.where(section_pos == sections - 2 - turn_index, arrived, current)
    heat_part = jnp.sum(result.astype(jnp.float32), axis=1)
    heat_rows = lax.psum(heat_part, "mp") / DW
    block_rows = half_width // lax.axis_size("dp")
    row_start = lax.axis_index("dp") * block_rows
    value_block = lax.dynamic_slice_in_dim(value_rows, row_start, block_rows, 0).astype(jnp.float32)
    summed = lax.psum_scatter(
        lax.dot_general(
            inputs, sens_kept, (((0,), (0,)), ((), ())), preferred_element_type=jnp.float32
        ).astype(jnp.bfloat16),
        "dp",
        scatter_dimension=0,
        tiled=True,
    ).astype(jnp.float32)
    relevance_rows = value_block * summed
    return (heat_rows[None, None, :], relevance_rows[None])


CHUNKS = 4
RAW = 2
SEGMENTS = (((0, 128),), ((0, 64), (64, 32)), ((0, 64),), ((0, 32),))
TILE = 256
MESH_ID = pl.DeviceIdType.MESH
F32 = jnp.float32
BF16 = jnp.bfloat16
DIRECT = 1
LAST_ORDER = (
    ("branch", 1), ("give", 2), ("give", 3), ("branch", 2), ("part", 0), ("branch", 3),
    ("mix", 0), ("part", 1), ("head", 0), ("mix", 1), ("values", 2), ("gather", 2),
    ("gather", 3), ("linear", 2), ("linear", 3), ("head", 1), ("join", 2), ("join", 3),
    ("hidden", 3),
)
NEXT_ORDER = (
    ("relay", 0), ("relay", 1), ("relay", 2), ("relay", 3), ("values", 0), ("gather", 0),
    ("hidden", 0), ("gather", 1), ("take", 0), ("gather", 2), ("gather", 3), ("linear", 0),
    ("join", 0), ("linear", 1), ("linear", 2), ("linear", 3), ("join", 1), ("join", 2),
    ("join", 3),
)


def tiles_of(heads, step):
    return sum(-(-heads // (HD // lanes)) for _, lanes in SEGMENTS[step])


def nt_dot(left, right):
    return lax.dot_general(left, right, (((1,), (1,)), ((), ())), preferred_element_type=F32)


def tn_dot(left, right):
    return lax.dot_general(left, right, (((0,), (0,)), ((), ())), preferred_element_type=F32)


def chain_kernel(
    peers, sections, len_ref, hid_in, att_in, que_in, key_in, vw_in, ow_in,
    heat_ref, rel_ref, hid_ref, att_ref, que_ref, key_ref, vw_ref, ow_ref, load_sem,
    through_ref, keep_ref, ratio_ref, inc_ref, out_ref, prob_ref, pack_ref, gval_ref, val_ref, bv_ref,
    vsend, vrecv, hidt_ref, hida_ref, sv_ref, heats, sm_ref, bvsend, bvbuf,
    asend, abuf, psend, pbuf, below_ref, dsend,
    a_send, g_send, a_recv, p_send, p_recv, s_send, s_recv, f_send, f_recv,
    x_send, x_recv, h_send, h_recv, one_send, one_recv,
    k_send, k_recv, b_send, b_recv, w_send, w_recv, r_send, t_send, t_recv, d_send,
):
    dp = lax.axis_index("dp")
    sec = lax.axis_index("section")
    core = lax.axis_index("mp")
    other = 1 - core
    seq_len, half = hid_ref.shape
    rows_n = seq_len // CHUNKS
    width = ow_ref.shape[1]
    blocks = peers // 2
    local_kv = key_ref.shape[1] // HD
    group = QH // KVH
    heads_n = local_kv * group
    kv_half = local_kv * HD
    block_rows = half // peers
    is_last = sec == sections - 1
    gets = core == dp // blocks
    hops = [(hop, lax.rem(dp + hop, peers)) for hop in range(1, peers)]

    loads = [
        pltpu.make_async_copy(source, target, load_sem.at[at])
        for at, (source, target) in enumerate((
            (hid_in, hid_ref), (att_in, att_ref), (vw_in, vw_ref),
            (que_in, que_ref), (key_in, key_ref), (ow_in, ow_ref),
        ))
    ]
    for load in loads:
        load.start()

    barrier = pltpu.get_barrier_semaphore()
    for hop, to in hops:
        for target in range(2):
            pl.semaphore_signal(
                barrier, inc=1, device_id={"dp": to, "mp": target}, device_id_type=MESH_ID
            )
    pl.semaphore_signal(barrier, inc=1, device_id={"mp": other}, device_id_type=MESH_ID)

    @pl.when(sec > 0)
    def _():
        pl.semaphore_signal(
            barrier, inc=1, device_id={"section": sec - 1}, device_id_type=MESH_ID
        )

    @pl.when(sec < sections - 1)
    def _():
        for at in range(peers):
            pl.semaphore_signal(
                barrier, inc=1, device_id={"dp": at, "section": sec + 1}, device_id_type=MESH_ID
            )

    def barrier_wait():
        greeted = 2 * (peers - 1) + 1

        @pl.when(is_last)
        def _():
            pl.semaphore_wait(barrier, greeted + peers)

        @pl.when(jnp.logical_not(is_last))
        def _():
            pl.semaphore_wait(barrier, greeted + 1)

    def remote(source, target, send, recv, device):
        return pltpu.make_async_remote_copy(
            src_ref=source, dst_ref=target, send_sem=send, recv_sem=recv,
            device_id=device, device_id_type=MESH_ID,
        )

    def rows_of(step):
        return pl.ds((CHUNKS - 1 - step) * rows_n, rows_n)

    def branch_copy(step, block):
        return remote(
            asend.at[step, block], abuf.at[step, dp],
            a_send.at[step, block], a_recv.at[step, dp], {"dp": core * blocks + block},
        )

    def direct_copy(step, block):
        return remote(
            dsend.at[step - DIRECT, block], abuf.at[step, dp],
            d_send.at[step - DIRECT, block], a_recv.at[step, dp],
            {"dp": core * blocks + block, "section": sec - 1},
        )

    def through_copy(step, target):
        rows = rows_of(step)
        return remote(
            through_ref.at[rows], below_ref.at[rows],
            t_send.at[step], t_recv.at[step], {"section": target},
        )

    def branch_forward(step, source):
        view = abuf.at[step, source]
        return remote(
            view, view, g_send.at[step, source], a_recv.at[step, source], {"mp": other}
        )

    rounds = peers.bit_length() - 1

    def slot_of(turn, target):
        return peers - (peers >> turn) + target // (2 << turn)

    def part_target(turn, at):
        bit = 1 << turn
        return lax.rem(dp, bit) + bit * (2 * at + 1 - lax.rem(dp // bit, 2))

    def part_copy(step, turn, at):
        bit = 1 << turn
        slot = peers - (peers >> turn) + at
        return remote(
            psend.at[step, part_target(turn, at)], pbuf.at[step, slot],
            p_send.at[step, slot], p_recv.at[step, slot],
            {"dp": dp + bit - 2 * bit * lax.rem(dp // bit, 2)},
        )

    def part_take(step, turn, target):
        slot = slot_of(turn, target)
        view = pbuf.at[step, slot]
        remote(
            view, view, p_send.at[step, slot], p_recv.at[step, slot], {"mp": other}
        ).wait_recv()
        return pbuf[step, slot].astype(F32)

    def mix_stage(step):
        for turn in range(1, rounds):
            for at in range(peers >> (turn + 1)):
                target = part_target(turn, at)
                running = psend[step, target].astype(F32)
                for before in range(turn):
                    running = running + part_take(step, before, target)
                psend[step, target] = running.astype(BF16)
                part_copy(step, turn, at).start()

    def value_rows(step, source):
        return gval_ref.at[source, pl.ds(0, (CHUNKS - step) * rows_n)]

    def prob_tiles(step, source):
        first = sum(tiles_of(heads_n, before) for before in range(step))
        return pack_ref.at[source, pl.ds(first, tiles_of(heads_n, step))]

    def gather_value(first, hop, to):
        view = value_rows(first, dp)
        return remote(
            view, view, k_send.at[CHUNKS, hop], k_recv.at[CHUNKS, dp], {"dp": to}
        )

    def gather_probs(step, hop, to):
        view = prob_tiles(step, dp)
        return remote(view, view, k_send.at[step, hop], k_recv.at[step, dp], {"dp": to})

    def sum_copy(step, hop, to):
        return remote(
            bvsend.at[step, hop], bvbuf.at[step, dp],
            b_send.at[step, hop], b_recv.at[step, dp], {"dp": to},
        )

    def sens_copy(step, owner):
        view = sv_ref.at[dp, owner, rows_of(step)]
        return remote(view, view, s_send.at[step], s_recv.at[step], {"mp": other})

    def final_copy(step, hop, to, side):
        view = sv_ref.at[dp, core, rows_of(step)]
        return remote(
            view, view, f_send.at[step, hop, side], f_recv.at[step, dp, core],
            {"dp": to, "mp": core if side == 0 else other},
        )

    def final_wait(step, source, owner):
        view = sv_ref.at[source, owner, rows_of(step)]
        remote(
            view, view, f_send.at[step, 0, 0], f_recv.at[step, source, owner], {"mp": other}
        ).wait_recv()

    def final_forward(source, owner):
        view = sv_ref.at[source, owner, pl.ds(rows_n, seq_len - rows_n)]
        return remote(view, view, w_send.at[source], w_recv.at[source], {"mp": other})

    def final_out(step):
        for hop, to in hops:
            for side in range(2 if step == CHUNKS - 1 else 1):
                final_copy(step, hop, to, side).start()

    def section_copy(step, target):
        return remote(
            out_ref.at[rows_of(step)], inc_ref.at[rows_of(step)],
            x_send.at[step], x_recv.at[step], {"section": target},
        )

    def hidden_copy(hop, to):
        return remote(
            hidt_ref.at[pl.ds(pl.multiple_of(to * block_rows, 16), block_rows)], hida_ref.at[dp],
            h_send.at[hop], h_recv.at[dp], {"dp": to},
        )

    def hidden_wait(hop, source):
        return remote(
            hidt_ref.at[pl.ds(0, block_rows)], hida_ref.at[source],
            h_send.at[hop], h_recv.at[source], {"mp": other},
        )

    def value_copy(slot):
        return remote(
            vsend.at[slot], vrecv, one_send.at[0], one_recv.at[0], {"mp": other}
        )

    def heat_copy(slot):
        return remote(
            heats.at[slot], heats.at[slot], one_send.at[1], one_recv.at[1], {"mp": other}
        )

    def branch_stage(step):
        rows = rows_of(step)
        sens = (inc_ref[rows, :].astype(F32) * through_ref[rows, :]).astype(BF16)
        for block in range(blocks):
            to = core * blocks + block
            piece = sens[:, block * width:(block + 1) * width]
            asend[step, block] = piece

            @pl.when(to == dp)
            def _():
                abuf[step, dp] = piece
                branch_forward(step, dp).start()

            @pl.when(to != dp)
            def _():
                branch_copy(step, block).start()

    def branch_wait(step, direct):
        @pl.when(gets)
        def _():
            for hop in range(0 if direct else 1, peers):
                source = lax.rem(dp + hop, peers)
                branch_forward(step, source).wait_recv()
                branch_forward(step, source).start()

        @pl.when(jnp.logical_not(gets))
        def _():
            for source in range(peers):
                branch_forward(step, source).wait_recv()

        return abuf[step].reshape(peers * rows_n, width)

    def part_stage(step):
        stacked = branch_wait(step, False)

        def tile(at, unused):
            start = pl.multiple_of(at * TILE, TILE)
            part = nt_dot(stacked, ow_ref[pl.ds(start, TILE), :]).astype(BF16)
            psend[step, :, :, pl.ds(start, TILE)] = part.reshape(peers, rows_n, TILE)
            return unused

        lax.fori_loop(0, half // TILE, tile, 0, unroll=True)
        for at in range(peers // 2):
            part_copy(step, 0, at).start()

    def add_values(seq, rows, mixed):
        for kv in range(local_kv):
            heads = range(kv * group, (kv + 1) * group)
            left = jnp.concatenate([prob_ref[seq, h, rows, :] for h in heads], axis=0)
            right = jnp.concatenate([mixed[:, h * HD:(h + 1) * HD] for h in heads], axis=0)
            columns = pl.ds(kv * HD, HD)
            bv_ref[seq, :, columns] = bv_ref[seq, :, columns] + tn_dot(left, right)

    def head_stage(step):
        rows = rows_of(step)
        back = psend[step, dp].astype(F32)
        for turn in range(rounds):
            back = back + part_take(step, turn, dp)
        add_values(dp, rows, (ratio_ref[dp, rows, :] * back).astype(BF16))
        finish(step, bv_ref[dp, rows, :])

    def linear_stage(step, direct=False):
        rows = rows_of(step)
        stacked = branch_wait(step, direct)
        for at in range(half // TILE):
            columns = pl.ds(at * TILE, TILE)
            part = nt_dot(stacked, ow_ref[columns, :])
            ratio = ratio_ref[:, rows, columns].reshape(peers * rows_n, TILE)
            sm_ref[:, columns] = (ratio * part).astype(BF16)
        for seq in range(peers):
            add_values(seq, rows, sm_ref[seq * rows_n:(seq + 1) * rows_n, :])
        for hop, to in hops:
            bvsend[step, hop] = bv_ref[to, rows, :].astype(BF16)
            sum_copy(step, hop, to).start()

    def join_stage(step):
        total = bv_ref[dp, rows_of(step), :]
        for hop, source in hops:
            view = bvbuf.at[step, source]
            remote(
                view, view, b_send.at[step, hop], b_recv.at[step, source], {"mp": other}
            ).wait_recv()
            total = total + bvbuf[step, source].astype(F32)
        finish(step, total)

    def finish(step, back_values):
        rows = rows_of(step)
        sv_ref[dp, core, rows, :] = (val_ref[rows, :] * back_values).astype(BF16)
        sens_copy(step, core).start()

        @pl.when(jnp.logical_not(is_last))
        def _():
            final_out(step)

        sens_copy(step, other).wait_recv()
        sens = jnp.concatenate([sv_ref[dp, 0, rows, :], sv_ref[dp, 1, rows, :]], axis=1)
        sums = jnp.zeros((rows_n, HD), F32)
        for at in range(half // TILE):
            columns = pl.ds(at * TILE, TILE)
            back_in = nt_dot(sens, vw_ref[columns, :])
            out = (
                inc_ref[rows, columns].astype(F32) * keep_ref[rows, columns]
                + hid_ref[rows, columns].astype(F32) * back_in
            ).astype(BF16)
            out_ref[rows, columns] = out
            wide = out.astype(F32)
            for lane in range(TILE // HD):
                sums = sums + wide[:, lane * HD:(lane + 1) * HD]
        heats[core, rows, :] = sums

        @pl.when(sec > 0)
        def _():
            if step >= DIRECT:
                through_copy(step, sec - 1).wait_recv()
                below = (out_ref[rows, :].astype(F32) * below_ref[rows, :]).astype(BF16)
                for block in range(blocks):
                    dsend[step - DIRECT, block] = below[:, block * width:(block + 1) * width]
                    direct_copy(step, block).start()
            section_copy(step, sec - 1).start()

    lane_at = lax.broadcasted_iota(jnp.int32, (rows_n, HD), 1)

    def shifted(tile, start, count, to):
        inside = (lane_at >= start) & (lane_at < start + count)
        kept = jnp.where(inside, tile, 0.0)
        return kept if start == to else pltpu.roll(kept, (to - start) % HD, 1)

    def pack_stage(step):
        at = sum(tiles_of(heads_n, before) for before in range(step))
        for start, lanes in SEGMENTS[step]:
            per = HD // lanes
            for first in range(0, heads_n, per):
                tile = None
                for h in range(first, min(first + per, heads_n)):
                    piece = shifted(
                        prob_ref[dp, h, rows_of(step), :].astype(F32), start, lanes, (h - first) * lanes
                    )
                    tile = piece if tile is None else tile + piece
                pack_ref[dp, at] = tile.astype(BF16)
                at += 1

    def value_wait(first, relay=False):
        for hop, source in hops:
            gather_wait(CHUNKS, value_rows(first, source), hop, source, relay)

    def relays(source):
        return jnp.logical_or(
            jnp.logical_and(source == 0, dp == peers - 2),
            jnp.logical_and(source == peers - 1, dp == 1),
        )

    def far(to):
        return jnp.logical_and(dp + to == peers - 1, jnp.logical_or(dp == 0, to == 0))

    def relay_copy(step, view, source):
        return remote(
            view, view, r_send.at[step], k_recv.at[step, source], {"dp": peers - 1 - source}
        )

    def gather_wait(step, view, hop, source, relay):
        copy = remote(
            view, view, k_send.at[step, hop], k_recv.at[step, source], {"mp": other}
        )
        if relay:
            @pl.when(jnp.logical_not(relays(source)))
            def _():
                copy.wait_recv()
        else:
            copy.wait_recv()

    def relay_stage(step):
        for end, through in ((0, peers - 2), (peers - 1, 1)):
            @pl.when(dp == through)
            def _():
                views = [(step, prob_tiles(step, end))]
                if step == 0:
                    views.insert(0, (CHUNKS, value_rows(0, end)))
                for at, view in views:
                    copy = relay_copy(at, view, end)
                    copy.wait_recv()
                    copy.start()

    def gather_stage(step, relay=False):
        rows = rows_of(step)
        depth = (CHUNKS - step) * rows_n
        for hop, source in hops:
            gather_wait(step, prob_tiles(step, source), hop, source, relay)
            for h in range(heads_n):
                at = sum(tiles_of(heads_n, before) for before in range(step))
                whole = None
                for start, lanes in SEGMENTS[step]:
                    per = HD // lanes
                    piece = shifted(
                        pack_ref[source, at + h // per].astype(F32), h % per * lanes, lanes, start
                    )
                    whole = piece if whole is None else whole + piece
                    at += -(-heads_n // per)
                prob_ref[source, h, rows, :] = whole.astype(BF16)
            for kv in range(local_kv):
                heads = range(kv * group, (kv + 1) * group)
                left = jnp.concatenate(
                    [prob_ref[source, h, rows, pl.ds(0, depth)] for h in heads], axis=0
                )
                mixed = jnp.dot(
                    left, gval_ref[source, pl.ds(0, depth), pl.ds(kv * HD, HD)],
                    preferred_element_type=F32,
                )
                ratio = mixed / stabilize(mixed)
                for at, h in enumerate(heads):
                    ratio_ref[source, rows, h * HD:(h + 1) * HD] = (
                        ratio[at * rows_n:(at + 1) * rows_n, :]
                    )

    length = len_ref[0]
    loads[0].wait()
    loads[1].wait()
    for step in range(CHUNKS):
        rows = rows_of(step)
        hid = hid_ref[rows, :].astype(F32)
        att = att_ref[rows, :].astype(F32)
        totals = hid + att
        inverse = 1.0 / stabilize(totals)
        keep_ref[rows, :] = hid * inverse
        through_ref[rows, :] = att * inverse / stabilize(att)

        @pl.when(is_last)
        def _():
            token = (CHUNKS - 1 - step) * rows_n + lax.broadcasted_iota(
                jnp.int32, (rows_n, half), 0
            )
            inc_ref[rows, :] = jnp.where(token < length, totals, 0.0).astype(BF16)

    loads[2].wait()
    hid_all = hid_ref[...]
    for slot in range(2):
        part = jnp.dot(
            hid_all, vw_ref[:, slot * kv_half:(slot + 1) * kv_half], preferred_element_type=F32
        )
        vsend[slot] = part.astype(BF16)

        @pl.when(core == slot)
        def _():
            val_ref[...] = part

    for load in loads[3:]:
        load.wait()
    bv_ref[...] = jnp.zeros_like(bv_ref)
    barrier_wait()
    value_copy(other).start()

    @pl.when(is_last)
    def _():
        branch_stage(0)

    @pl.when(jnp.logical_not(is_last))
    def _():
        for step in range(DIRECT, CHUNKS):
            through_copy(step, sec + 1).start()

    query_at = lax.broadcasted_iota(jnp.int32, (seq_len, seq_len), 0)
    key_at = lax.broadcasted_iota(jnp.int32, (seq_len, seq_len), 1)
    allowed = (key_at <= query_at) & (key_at < length)
    for h in range(heads_n):
        kv = h // group
        scores = nt_dot(
            que_ref[:, h * HD:(h + 1) * HD], key_ref[:, kv * HD:(kv + 1) * HD]
        ) / math.sqrt(HD)
        scores = jnp.where(allowed, scores, -1000000000.0)
        weights = jnp.exp(scores - jnp.max(scores, axis=1, keepdims=True))
        prob_ref[dp, h] = (weights / jnp.sum(weights, axis=1, keepdims=True)).astype(BF16)

    value_copy(other).wait()
    values = (val_ref[...] + vrecv[...].astype(F32)).astype(BF16)
    gval_ref[dp] = values

    @pl.when(is_last)
    def _():
        for step in range(RAW, CHUNKS):
            pack_stage(step)

    @pl.when(jnp.logical_not(is_last))
    def _():
        for step in range(CHUNKS):
            pack_stage(step)
        for hop, to in (hops[1], hops[0], hops[2]):
            @pl.when(jnp.logical_not(far(to)))
            def _():
                gather_value(0, hop, to).start()
                for step in range(CHUNKS):
                    gather_probs(step, hop, to).start()

    wide_values = values.astype(F32)
    val_ref[...] = wide_values / stabilize(wide_values)
    for h in range(heads_n):
        kv = h // group
        mixed = jnp.dot(
            prob_ref[dp, h], values[:, kv * HD:(kv + 1) * HD], preferred_element_type=F32
        )
        ratio_ref[dp, :, h * HD:(h + 1) * HD] = mixed / stabilize(mixed)

    for at in range(half // HD):
        flipped = hid_ref[:, at * HD:(at + 1) * HD].astype(F32).T
        hidt_ref[pl.ds(at * HD, HD), :] = flipped.astype(BF16)
    hida_ref[dp] = hidt_ref[pl.ds(pl.multiple_of(dp * block_rows, 16), block_rows), :]

    def branch_next(step):
        section_copy(step, sec + 1).wait_recv()
        branch_stage(step)

    def hidden_stage(step):
        if step == CHUNKS - 1:
            for at in range(DIRECT, CHUNKS):
                for block in range(blocks):
                    direct_copy(at, block).wait_send()
        for hop, to in hops:
            hidden_copy(hop, to).start()

    def join_next(step):
        if step >= DIRECT:
            section_copy(step, sec + 1).wait_recv()
        join_stage(step)

    def give_stage(step):
        for hop, to in hops:
            if step == RAW:
                gather_value(RAW, hop, to).start()
            gather_probs(step, hop, to).start()

    stages = {
        "give": give_stage,
        "values": value_wait, "hidden": hidden_stage, "branch": branch_stage, "relay": relay_stage,
        "gather": gather_stage, "part": part_stage, "mix": mix_stage, "head": head_stage,
        "take": branch_next, "linear": linear_stage, "join": join_stage,
    }

    @pl.when(is_last)
    def _():
        for stage, step in LAST_ORDER:
            stages[stage](step)
        for step in range(CHUNKS):
            final_out(step)

    @pl.when(jnp.logical_not(is_last))
    def _():
        stages["values"] = functools.partial(value_wait, relay=True)
        stages["gather"] = functools.partial(gather_stage, relay=True)
        stages["join"] = join_next
        for stage, step in NEXT_ORDER:
            if stage == "linear":
                stages[stage] = functools.partial(linear_stage, direct=step >= DIRECT)
            stages[stage](step)

    heat_copy(core).start()
    for hop, source in hops:
        for step in range(CHUNKS - 1):
            final_wait(step, source, core)
        final_forward(source, core).start()
    for hop, source in hops:
        hidden_wait(hop, source).wait()
    for step in range(CHUNKS):
        for block in range(blocks):
            mine = core * blocks + block != dp

            @pl.when(mine if step < DIRECT else jnp.logical_and(mine, is_last))
            def _():
                branch_copy(step, block).wait_send()

        @pl.when(gets)
        def _():
            for source in range(peers):
                branch_forward(step, source).wait_send()

        sens_copy(step, core).wait_send()

        @pl.when(sec > 0)
        def _():
            section_copy(step, sec - 1).wait_send()

    def sent(first, hop, to):
        gather_value(first, hop, to).wait_send()
        for step in range(first, CHUNKS):
            gather_probs(step, hop, to).wait_send()

    @pl.when(is_last)
    def _():
        for hop, to in hops:
            sent(RAW, hop, to)
            for step in range(RAW, CHUNKS):
                sum_copy(step, hop, to).wait_send()
        for step in range(RAW):
            for turn in range(rounds):
                for at in range(peers >> (turn + 1)):
                    part_copy(step, turn, at).wait_send()

    @pl.when(jnp.logical_not(is_last))
    def _():
        for step in range(DIRECT, CHUNKS):
            through_copy(step, sec + 1).wait_send()
        for hop, to in hops:
            @pl.when(jnp.logical_not(far(to)))
            def _():
                sent(0, hop, to)

            @pl.when(relays(to))
            def _():
                relay_copy(CHUNKS, value_rows(0, to), to).wait_send()
                for step in range(CHUNKS):
                    relay_copy(step, prob_tiles(step, to), to).wait_send()
            for step in range(CHUNKS):
                sum_copy(step, hop, to).wait_send()

    block_at = pl.ds(pl.multiple_of(dp * block_rows, 16), block_rows)
    total = None
    for hop in range(peers):
        source = lax.rem(dp + hop, peers)
        if hop > 0:
            final_forward(source, other).wait_recv()
            for owner in range(2):
                final_wait(CHUNKS - 1, source, owner)
        sens = jnp.concatenate([sv_ref[source, 0], sv_ref[source, 1]], axis=1)
        term = jnp.dot(hida_ref[source], sens, preferred_element_type=F32)
        total = term if total is None else total + term
    rel_ref[...] = vw_ref[block_at, :].astype(F32) * total
    heat_copy(other).wait_recv()
    heat_copy(core).wait_send()
    heat_ref[...] = jnp.sum((heats[0] + heats[1]).T, axis=0, keepdims=True) / DW

    for hop, to in hops:
        for step in range(CHUNKS):
            for side in range(2 if step == CHUNKS - 1 else 1):
                final_copy(step, hop, to, side).wait_send()
    for hop, source in hops:
        final_forward(source, core).wait_send()


def on_device_chain(hidden_in, attn_out, queries, keys, value_weight, out_weight, lengths):
    peers = lax.axis_size("dp")
    sections = lax.axis_size("section")
    seq_len, half = hidden_in.shape[2:]
    kv_half = keys.shape[3]
    kv_width = value_weight.shape[2]
    width = out_weight.shape[2]
    heads = half // HD
    rows_n = seq_len // CHUNKS
    packed = sum(tiles_of(heads, step) for step in range(CHUNKS))
    vmem = pltpu.VMEM
    dma = pltpu.SemaphoreType.DMA
    whole = pl.BlockSpec(memory_space=pltpu.VMEM)
    heat, relevance = pl.pallas_call(
        functools.partial(chain_kernel, peers, sections),
        out_shape=(
            jax.ShapeDtypeStruct((1, seq_len), F32),
            jax.ShapeDtypeStruct((half // peers, kv_width), F32),
        ),
        in_specs=[pl.BlockSpec(memory_space=pltpu.SMEM)] + [pl.BlockSpec(memory_space=pl.ANY)] * 6,
        out_specs=(whole, whole),
        scratch_shapes=[
            vmem((seq_len, half), BF16),
            vmem((seq_len, half), BF16),
            vmem((seq_len, half), BF16),
            vmem((seq_len, kv_half), BF16),
            vmem((half, kv_width), BF16),
            vmem((half, width), BF16),
            dma((6,)),
            vmem((seq_len, half), F32),
            vmem((seq_len, half), F32),
            vmem((peers, seq_len, half), F32),
            vmem((seq_len, half), BF16),
            vmem((seq_len, half), BF16),
            vmem((peers, heads, seq_len, seq_len), BF16),
            vmem((peers, packed, rows_n, HD), BF16),
            vmem((peers, seq_len, kv_half), BF16),
            vmem((seq_len, kv_half), F32),
            vmem((peers, seq_len, kv_half), F32),
            vmem((2, seq_len, kv_half), BF16),
            vmem((seq_len, kv_half), BF16),
            vmem((half, seq_len), BF16),
            vmem((peers, half // peers, seq_len), BF16),
            vmem((peers, 2, seq_len, kv_half), BF16),
            vmem((2, seq_len, HD), F32),
            vmem((peers * rows_n, half), BF16),
            vmem((CHUNKS, peers, rows_n, kv_half), BF16),
            vmem((CHUNKS, peers, rows_n, kv_half), BF16),
            vmem((CHUNKS, peers // 2, rows_n, width), BF16),
            vmem((CHUNKS, peers, rows_n, width), BF16),
            vmem((RAW, peers, rows_n, half), BF16),
            vmem((RAW, peers - 1, rows_n, half), BF16),
            vmem((seq_len, half), F32),
            vmem((CHUNKS - DIRECT, peers // 2, rows_n, width), BF16),
            dma((CHUNKS, peers // 2)),
            dma((CHUNKS, peers)),
            dma((CHUNKS, peers)),
            dma((RAW, peers)),
            dma((RAW, peers)),
            dma((CHUNKS,)),
            dma((CHUNKS,)),
            dma((CHUNKS, peers, 2)),
            dma((CHUNKS, peers, 2)),
            dma((CHUNKS,)),
            dma((CHUNKS,)),
            dma((peers,)),
            dma((peers,)),
            dma((2,)),
            dma((2,)),
            dma((CHUNKS + 1, peers)),
            dma((CHUNKS + 1, peers)),
            dma((CHUNKS, peers)),
            dma((CHUNKS, peers)),
            dma((peers,)),
            dma((peers,)),
            dma((CHUNKS + 1,)),
            dma((CHUNKS,)),
            dma((CHUNKS,)),
            dma((CHUNKS - DIRECT, peers // 2)),
        ],
        compiler_params=pltpu.CompilerParams(
            collective_id=0, has_side_effects=True, vmem_limit_bytes=60 * 1024 * 1024
        ),
        name="relevance_chain",
    )(
        lengths, hidden_in[0, 0], attn_out[0, 0], queries[0, 0], keys[0, 0],
        value_weight[0], out_weight[0],
    )
    return heat[None], relevance[None]


def solution(mesh):
    placed = (
        P("section", ("groups", "dp"), None, "mp"),
        P("section", ("groups", "dp"), None, "mp"),
        P("section", ("groups", "dp"), None, "mp"),
        P("section", ("groups", "dp"), None, "mp"),
        P("section", "mp", None),
        P("section", "mp", "dp"),
        P(("groups", "dp")),
    )
    peers = mesh.shape["dp"]
    aligned = peers == 4 and mesh.shape["section"] == 2
    return jax.shard_map(
        on_device_chain if aligned else on_device,
        mesh=mesh,
        in_specs=placed,
        out_specs=(
            P("section", ("groups", "dp"), None),
            P(("groups", "section"), ("mp", "dp"), None),
        ),
        check_vma=False,
    )
```

```python
import functools
import math

import jax
import jax.numpy as jnp
from jax import lax
from jax.experimental import pallas as pl
from jax.experimental.pallas import tpu as pltpu
from jax.sharding import PartitionSpec as P

DW = 2560
HD = 128
QH = 20
KVH = 4


EPS = 0.25


def from_behind(shard, axis, by):
    peers = lax.axis_size(axis)
    pairs = [(i, i + by) for i in range(peers) if 0 <= i + by < peers]
    return lax.ppermute(shard, axis, pairs)


def stabilize(entries):
    return jnp.where(entries >= 0, entries + EPS, entries - EPS)


def gated(active, compute, operand, out_shape, out_type):
    return lax.cond(active, compute, lambda unused: jnp.zeros(out_shape, out_type), operand)


def on_device(hidden_in, attn_out, queries, keys, value_weight, out_weight, lengths):
    inputs = hidden_in[0, 0]
    branch = attn_out[0, 0]
    query_rows = queries[0, 0]
    key_rows = keys[0, 0]
    value_rows = value_weight[0]
    seq_len = inputs.shape[0]
    half_width = inputs.shape[1]
    group_size = QH // KVH
    local_kv = key_rows.shape[1] // HD
    kv_width = value_rows.shape[1]
    sections = lax.axis_size("section")
    section_pos = lax.axis_index("section")
    core_pos = lax.axis_index("mp")
    out_cols = lax.all_gather(out_weight, "dp", axis=2, tiled=True)[0]
    inputs_f = inputs.astype(jnp.float32)
    branch_f = branch.astype(jnp.float32)
    totals = inputs_f + branch_f
    value_part = jnp.dot(inputs, value_rows, preferred_element_type=jnp.float32)
    value_all = lax.psum(value_part.astype(jnp.bfloat16), "mp").astype(jnp.float32)
    value_mine = lax.dynamic_slice_in_dim(value_all, core_pos * local_kv * HD, local_kv * HD, 1)
    values_bf = lax.optimization_barrier(value_mine.astype(jnp.bfloat16))
    values_f = values_bf.astype(jnp.float32)
    query_heads = query_rows.reshape(seq_len, local_kv, group_size, HD)
    key_heads = key_rows.reshape(seq_len, local_kv, HD)
    scores = jnp.einsum(
        "tgjd,sgd->gjts", query_heads, key_heads, preferred_element_type=jnp.float32
    ) / math.sqrt(HD)
    position = lax.iota(jnp.int32, seq_len)
    allowed = (position[None, :] <= position[:, None]) & (position[None, :] < lengths[0])
    scores = jnp.where(allowed, scores, -1000000000.0)
    row_top = jnp.max(scores, axis=-1, keepdims=True)
    weights = jnp.exp(scores - row_top)
    prob_rows = (weights / jnp.sum(weights, axis=-1, keepdims=True)).astype(jnp.bfloat16)
    mixed_heads = jnp.einsum(
        "gjts,sgd->tgjd",
        prob_rows,
        values_bf.reshape(seq_len, local_kv, HD),
        preferred_element_type=jnp.float32,
    ).reshape(seq_len, local_kv * group_size * HD)
    valid_rows = (position < lengths[0]).astype(jnp.float32)
    current = (totals * valid_rows[:, None]).astype(jnp.bfloat16)
    result = jnp.zeros((seq_len, half_width), jnp.bfloat16)
    sens_kept = jnp.zeros((seq_len, kv_width), jnp.bfloat16)
    for turn_index in range(sections):
        active = section_pos == sections - 1 - turn_index
        sens_total = current.astype(jnp.float32) / stabilize(totals)
        sens_branch = (branch_f * sens_total / stabilize(branch_f)).astype(jnp.bfloat16)
        sens_full = lax.all_gather(sens_branch, "mp", axis=1, tiled=True)

        def through_heads(operand):
            back_mixed = lax.dot_general(
                operand, out_cols, (((1,), (1,)), ((), ())), preferred_element_type=jnp.float32
            )
            sens_mixed = (mixed_heads * back_mixed / stabilize(mixed_heads)).astype(jnp.bfloat16)
            back_values = jnp.einsum(
                "gjts,tgjd->sgd",
                prob_rows,
                sens_mixed.reshape(seq_len, local_kv, group_size, HD),
                preferred_element_type=jnp.float32,
            ).reshape(seq_len, local_kv * HD)
            return (values_f * back_values / stabilize(values_f)).astype(jnp.bfloat16)

        sens_values = gated(
            active, through_heads, sens_full, (seq_len, local_kv * HD), jnp.bfloat16
        )
        sens_all = lax.all_gather(sens_values, "mp", axis=1, tiled=True)

        def through_values(operand):
            back_inputs = lax.dot_general(
                operand, value_rows, (((1,), (1,)), ((), ())), preferred_element_type=jnp.float32
            )
            return (inputs_f * sens_total + inputs_f * back_inputs).astype(jnp.bfloat16)

        outgoing = gated(active, through_values, sens_all, (seq_len, half_width), jnp.bfloat16)
        result = jnp.where(active, outgoing, result)
        sens_kept = jnp.where(active, sens_all, sens_kept)
        if turn_index + 1 < sections:
            arrived = from_behind(outgoing, "section", -1)
            current = jnp.where(section_pos == sections - 2 - turn_index, arrived, current)
    heat_part = jnp.sum(result.astype(jnp.float32), axis=1)
    heat_rows = lax.psum(heat_part, "mp") / DW
    block_rows = half_width // lax.axis_size("dp")
    row_start = lax.axis_index("dp") * block_rows
    value_block = lax.dynamic_slice_in_dim(value_rows, row_start, block_rows, 0).astype(jnp.float32)
    summed = lax.psum_scatter(
        lax.dot_general(
            inputs, sens_kept, (((0,), (0,)), ((), ())), preferred_element_type=jnp.float32
        ).astype(jnp.bfloat16),
        "dp",
        scatter_dimension=0,
        tiled=True,
    ).astype(jnp.float32)
    relevance_rows = value_block * summed
    return (heat_rows[None, None, :], relevance_rows[None])


CHUNKS = 4
RAW = 2
SEGMENTS = (((0, 128),), ((0, 64), (64, 32)), ((0, 64),), ((0, 32),))
TILE = 256
MESH_ID = pl.DeviceIdType.MESH
F32 = jnp.float32
BF16 = jnp.bfloat16
DIRECT = 1
LAST_ORDER = (
    ("branch", 1), ("give", 2), ("give", 3), ("branch", 2), ("part", 0), ("branch", 3),
    ("mix", 0), ("part", 1), ("head", 0), ("mix", 1), ("values", 2), ("gather", 2),
    ("gather", 3), ("linear", 2), ("linear", 3), ("head", 1), ("join", 2), ("join", 3),
    ("hidden", 3),
)
NEXT_ORDER = (
    ("relay", 0), ("relay", 1), ("relay", 2), ("relay", 3), ("values", 0), ("gather", 0),
    ("hidden", 0), ("gather", 1), ("take", 0), ("gather", 2), ("gather", 3), ("linear", 0),
    ("join", 0), ("linear", 1), ("linear", 2), ("linear", 3), ("join", 1), ("join", 2),
    ("join", 3),
)


def tiles_of(heads, step):
    return sum(-(-heads // (HD // lanes)) for _, lanes in SEGMENTS[step])


def nt_dot(left, right):
    return lax.dot_general(left, right, (((1,), (1,)), ((), ())), preferred_element_type=F32)


def tn_dot(left, right):
    return lax.dot_general(left, right, (((0,), (0,)), ((), ())), preferred_element_type=F32)


def chain_kernel(
    peers, sections, len_ref, hid_in, att_in, que_in, key_in, vw_in, ow_in,
    heat_ref, rel_ref, hid_ref, att_ref, que_ref, key_ref, vw_ref, ow_ref, load_sem,
    through_ref, keep_ref, ratio_ref, inc_ref, out_ref, prob_ref, pack_ref, gval_ref, val_ref, bv_ref,
    vsend, vrecv, hidt_ref, hida_ref, sv_ref, heats, sm_ref, bvsend, bvbuf,
    asend, abuf, psend, pbuf, below_ref, dsend,
    a_send, g_send, a_recv, p_send, p_recv, s_send, s_recv, f_send, f_recv,
    x_send, x_recv, h_send, h_recv, one_send, one_recv,
    k_send, k_recv, b_send, b_recv, w_send, w_recv, r_send, t_send, t_recv, d_send,
):
    dp = lax.axis_index("dp")
    sec = lax.axis_index("section")
    core = lax.axis_index("mp")
    other = 1 - core
    seq_len, half = hid_ref.shape
    rows_n = seq_len // CHUNKS
    width = ow_ref.shape[1]
    blocks = peers // 2
    local_kv = key_ref.shape[1] // HD
    group = QH // KVH
    heads_n = local_kv * group
    kv_half = local_kv * HD
    block_rows = half // peers
    is_last = sec == sections - 1
    gets = core == dp // blocks
    hops = [(hop, lax.rem(dp + hop, peers)) for hop in range(1, peers)]

    loads = [
        pltpu.make_async_copy(source, target, load_sem.at[at])
        for at, (source, target) in enumerate((
            (hid_in, hid_ref), (att_in, att_ref), (vw_in, vw_ref),
            (que_in, que_ref), (key_in, key_ref), (ow_in, ow_ref),
        ))
    ]
    for load in loads:
        load.start()

    barrier = pltpu.get_barrier_semaphore()
    for hop, to in hops:
        for target in range(2):
            pl.semaphore_signal(
                barrier, inc=1, device_id={"dp": to, "mp": target}, device_id_type=MESH_ID
            )
    pl.semaphore_signal(barrier, inc=1, device_id={"mp": other}, device_id_type=MESH_ID)

    @pl.when(sec > 0)
    def _():
        pl.semaphore_signal(
            barrier, inc=1, device_id={"section": sec - 1}, device_id_type=MESH_ID
        )

    @pl.when(sec < sections - 1)
    def _():
        for at in range(peers):
            pl.semaphore_signal(
                barrier, inc=1, device_id={"dp": at, "section": sec + 1}, device_id_type=MESH_ID
            )

    def barrier_wait():
        greeted = 2 * (peers - 1) + 1

        @pl.when(is_last)
        def _():
            pl.semaphore_wait(barrier, greeted + peers)

        @pl.when(jnp.logical_not(is_last))
        def _():
            pl.semaphore_wait(barrier, greeted + 1)

    def remote(source, target, send, recv, device):
        return pltpu.make_async_remote_copy(
            src_ref=source, dst_ref=target, send_sem=send, recv_sem=recv,
            device_id=device, device_id_type=MESH_ID,
        )

    def rows_of(step):
        return pl.ds((CHUNKS - 1 - step) * rows_n, rows_n)

    def branch_copy(step, block):
        return remote(
            asend.at[step, block], abuf.at[step, dp],
            a_send.at[step, block], a_recv.at[step, dp], {"dp": core * blocks + block},
        )

    def direct_copy(step, block):
        return remote(
            dsend.at[step - DIRECT, block], abuf.at[step, dp],
            d_send.at[step - DIRECT, block], a_recv.at[step, dp],
            {"dp": core * blocks + block, "section": sec - 1},
        )

    def through_copy(step, target):
        rows = rows_of(step)
        return remote(
            through_ref.at[rows], below_ref.at[rows],
            t_send.at[step], t_recv.at[step], {"section": target},
        )

    def branch_forward(step, source):
        view = abuf.at[step, source]
        return remote(
            view, view, g_send.at[step, source], a_recv.at[step, source], {"mp": other}
        )

    rounds = peers.bit_length() - 1

    def slot_of(turn, target):
        return peers - (peers >> turn) + target // (2 << turn)

    def part_target(turn, at):
        bit = 1 << turn
        return lax.rem(dp, bit) + bit * (2 * at + 1 - lax.rem(dp // bit, 2))

    def part_copy(step, turn, at):
        bit = 1 << turn
        slot = peers - (peers >> turn) + at
        return remote(
            psend.at[step, part_target(turn, at)], pbuf.at[step, slot],
            p_send.at[step, slot], p_recv.at[step, slot],
            {"dp": dp + bit - 2 * bit * lax.rem(dp // bit, 2)},
        )

    def part_take(step, turn, target):
        slot = slot_of(turn, target)
        view = pbuf.at[step, slot]
        remote(
            view, view, p_send.at[step, slot], p_recv.at[step, slot], {"mp": other}
        ).wait_recv()
        return pbuf[step, slot].astype(F32)

    def mix_stage(step):
        for turn in range(1, rounds):
            for at in range(peers >> (turn + 1)):
                target = part_target(turn, at)
                running = psend[step, target].astype(F32)
                for before in range(turn):
                    running = running + part_take(step, before, target)
                psend[step, target] = running.astype(BF16)
                part_copy(step, turn, at).start()

    def value_rows(step, source):
        return gval_ref.at[source, pl.ds(0, (CHUNKS - step) * rows_n)]

    def prob_tiles(step, source):
        first = sum(tiles_of(heads_n, before) for before in range(step))
        return pack_ref.at[source, pl.ds(first, tiles_of(heads_n, step))]

    def gather_value(first, hop, to):
        view = value_rows(first, dp)
        return remote(
            view, view, k_send.at[CHUNKS, hop], k_recv.at[CHUNKS, dp], {"dp": to}
        )

    def gather_probs(step, hop, to):
        view = prob_tiles(step, dp)
        return remote(view, view, k_send.at[step, hop], k_recv.at[step, dp], {"dp": to})

    def sum_copy(step, hop, to):
        return remote(
            bvsend.at[step, hop], bvbuf.at[step, dp],
            b_send.at[step, hop], b_recv.at[step, dp], {"dp": to},
        )

    def sens_copy(step, owner):
        view = sv_ref.at[dp, owner, rows_of(step)]
        return remote(view, view, s_send.at[step], s_recv.at[step], {"mp": other})

    def final_copy(step, hop, to, side):
        view = sv_ref.at[dp, core, rows_of(step)]
        return remote(
            view, view, f_send.at[step, hop, side], f_recv.at[step, dp, core],
            {"dp": to, "mp": core if side == 0 else other},
        )

    def final_wait(step, source, owner):
        view = sv_ref.at[source, owner, rows_of(step)]
        remote(
            view, view, f_send.at[step, 0, 0], f_recv.at[step, source, owner], {"mp": other}
        ).wait_recv()

    def final_forward(source, owner):
        view = sv_ref.at[source, owner, pl.ds(rows_n, seq_len - rows_n)]
        return remote(view, view, w_send.at[source], w_recv.at[source], {"mp": other})

    def final_out(step):
        for hop, to in hops:
            for side in range(2 if step == CHUNKS - 1 else 1):
                final_copy(step, hop, to, side).start()

    def section_copy(step, target):
        return remote(
            out_ref.at[rows_of(step)], inc_ref.at[rows_of(step)],
            x_send.at[step], x_recv.at[step], {"section": target},
        )

    def hidden_copy(hop, to):
        return remote(
            hidt_ref.at[pl.ds(pl.multiple_of(to * block_rows, 16), block_rows)], hida_ref.at[dp],
            h_send.at[hop], h_recv.at[dp], {"dp": to},
        )

    def hidden_wait(hop, source):
        return remote(
            hidt_ref.at[pl.ds(0, block_rows)], hida_ref.at[source],
            h_send.at[hop], h_recv.at[source], {"mp": other},
        )

    def value_copy(slot):
        return remote(
            vsend.at[slot], vrecv, one_send.at[0], one_recv.at[0], {"mp": other}
        )

    def heat_copy(slot):
        return remote(
            heats.at[slot], heats.at[slot], one_send.at[1], one_recv.at[1], {"mp": other}
        )

    def branch_stage(step):
        rows = rows_of(step)
        sens = (inc_ref[rows, :].astype(F32) * through_ref[rows, :]).astype(BF16)
        for block in range(blocks):
            to = core * blocks + block
            piece = sens[:, block * width:(block + 1) * width]
            asend[step, block] = piece

            @pl.when(to == dp)
            def _():
                abuf[step, dp] = piece
                branch_forward(step, dp).start()

            @pl.when(to != dp)
            def _():
                branch_copy(step, block).start()

    def branch_wait(step, direct):
        @pl.when(gets)
        def _():
            for hop in range(0 if direct else 1, peers):
                source = lax.rem(dp + hop, peers)
                branch_forward(step, source).wait_recv()
                branch_forward(step, source).start()

        @pl.when(jnp.logical_not(gets))
        def _():
            for source in range(peers):
                branch_forward(step, source).wait_recv()

        return abuf[step].reshape(peers * rows_n, width)

    def part_stage(step):
        stacked = branch_wait(step, False)

        def tile(at, unused):
            start = pl.multiple_of(at * TILE, TILE)
            part = nt_dot(stacked, ow_ref[pl.ds(start, TILE), :]).astype(BF16)
            psend[step, :, :, pl.ds(start, TILE)] = part.reshape(peers, rows_n, TILE)
            return unused

        lax.fori_loop(0, half // TILE, tile, 0, unroll=True)
        for at in range(peers // 2):
            part_copy(step, 0, at).start()

    def add_values(seq, rows, mixed):
        for kv in range(local_kv):
            heads = range(kv * group, (kv + 1) * group)
            left = jnp.concatenate([prob_ref[seq, h, rows, :] for h in heads], axis=0)
            right = jnp.concatenate([mixed[:, h * HD:(h + 1) * HD] for h in heads], axis=0)
            columns = pl.ds(kv * HD, HD)
            bv_ref[seq, :, columns] = bv_ref[seq, :, columns] + tn_dot(left, right)

    def head_stage(step):
        rows = rows_of(step)
        back = psend[step, dp].astype(F32)
        for turn in range(rounds):
            back = back + part_take(step, turn, dp)
        add_values(dp, rows, (ratio_ref[dp, rows, :] * back).astype(BF16))
        finish(step, bv_ref[dp, rows, :])

    def linear_stage(step, direct=False):
        rows = rows_of(step)
        stacked = branch_wait(step, direct)
        for at in range(half // TILE):
            columns = pl.ds(at * TILE, TILE)
            part = nt_dot(stacked, ow_ref[columns, :])
            ratio = ratio_ref[:, rows, columns].reshape(peers * rows_n, TILE)
            sm_ref[:, columns] = (ratio * part).astype(BF16)
        for seq in range(peers):
            add_values(seq, rows, sm_ref[seq * rows_n:(seq + 1) * rows_n, :])
        for hop, to in hops:
            bvsend[step, hop] = bv_ref[to, rows, :].astype(BF16)
            sum_copy(step, hop, to).start()

    def join_stage(step):
        total = bv_ref[dp, rows_of(step), :]
        for hop, source in hops:
            view = bvbuf.at[step, source]
            remote(
                view, view, b_send.at[step, hop], b_recv.at[step, source], {"mp": other}
            ).wait_recv()
            total = total + bvbuf[step, source].astype(F32)
        finish(step, total)

    def finish(step, back_values):
        rows = rows_of(step)
        sv_ref[dp, core, rows, :] = (val_ref[rows, :] * back_values).astype(BF16)
        sens_copy(step, core).start()

        @pl.when(jnp.logical_not(is_last))
        def _():
            final_out(step)

        sens_copy(step, other).wait_recv()
        sens = jnp.concatenate([sv_ref[dp, 0, rows, :], sv_ref[dp, 1, rows, :]], axis=1)
        sums = jnp.zeros((rows_n, HD), F32)
        for at in range(half // TILE):
            columns = pl.ds(at * TILE, TILE)
            back_in = nt_dot(sens, vw_ref[columns, :])
            out = (
                inc_ref[rows, columns].astype(F32) * keep_ref[rows, columns]
                + hid_ref[rows, columns].astype(F32) * back_in
            ).astype(BF16)
            out_ref[rows, columns] = out
            wide = out.astype(F32)
            for lane in range(TILE // HD):
                sums = sums + wide[:, lane * HD:(lane + 1) * HD]
        heats[core, rows, :] = sums

        @pl.when(sec > 0)
        def _():
            if step >= DIRECT:
                through_copy(step, sec - 1).wait_recv()
                below = (out_ref[rows, :].astype(F32) * below_ref[rows, :]).astype(BF16)
                for block in range(blocks):
                    dsend[step - DIRECT, block] = below[:, block * width:(block + 1) * width]
                    direct_copy(step, block).start()
            section_copy(step, sec - 1).start()

    lane_at = lax.broadcasted_iota(jnp.int32, (rows_n, HD), 1)

    def shifted(tile, start, count, to):
        inside = (lane_at >= start) & (lane_at < start + count)
        kept = jnp.where(inside, tile, 0.0)
        return kept if start == to else pltpu.roll(kept, (to - start) % HD, 1)

    def pack_stage(step):
        at = sum(tiles_of(heads_n, before) for before in range(step))
        for start, lanes in SEGMENTS[step]:
            per = HD // lanes
            for first in range(0, heads_n, per):
                tile = None
                for h in range(first, min(first + per, heads_n)):
                    piece = shifted(
                        prob_ref[dp, h, rows_of(step), :].astype(F32), start, lanes, (h - first) * lanes
                    )
                    tile = piece if tile is None else tile + piece
                pack_ref[dp, at] = tile.astype(BF16)
                at += 1

    def value_wait(first, relay=False):
        for hop, source in hops:
            gather_wait(CHUNKS, value_rows(first, source), hop, source, relay)

    def relays(source):
        return jnp.logical_or(
            jnp.logical_and(source == 0, dp == peers - 2),
            jnp.logical_and(source == peers - 1, dp == 1),
        )

    def far(to):
        return jnp.logical_and(dp + to == peers - 1, jnp.logical_or(dp == 0, to == 0))

    def relay_copy(step, view, source):
        return remote(
            view, view, r_send.at[step], k_recv.at[step, source], {"dp": peers - 1 - source}
        )

    def gather_wait(step, view, hop, source, relay):
        copy = remote(
            view, view, k_send.at[step, hop], k_recv.at[step, source], {"mp": other}
        )
        if relay:
            @pl.when(jnp.logical_not(relays(source)))
            def _():
                copy.wait_recv()
        else:
            copy.wait_recv()

    def relay_stage(step):
        for end, through in ((0, peers - 2), (peers - 1, 1)):
            @pl.when(dp == through)
            def _():
                views = [(step, prob_tiles(step, end))]
                if step == 0:
                    views.insert(0, (CHUNKS, value_rows(0, end)))
                for at, view in views:
                    copy = relay_copy(at, view, end)
                    copy.wait_recv()
                    copy.start()

    def gather_stage(step, relay=False):
        rows = rows_of(step)
        depth = (CHUNKS - step) * rows_n
        for hop, source in hops:
            gather_wait(step, prob_tiles(step, source), hop, source, relay)
            for h in range(heads_n):
                at = sum(tiles_of(heads_n, before) for before in range(step))
                whole = None
                for start, lanes in SEGMENTS[step]:
                    per = HD // lanes
                    piece = shifted(
                        pack_ref[source, at + h // per].astype(F32), h % per * lanes, lanes, start
                    )
                    whole = piece if whole is None else whole + piece
                    at += -(-heads_n // per)
                prob_ref[source, h, rows, :] = whole.astype(BF16)
            for kv in range(local_kv):
                heads = range(kv * group, (kv + 1) * group)
                left = jnp.concatenate(
                    [prob_ref[source, h, rows, pl.ds(0, depth)] for h in heads], axis=0
                )
                mixed = jnp.dot(
                    left, gval_ref[source, pl.ds(0, depth), pl.ds(kv * HD, HD)],
                    preferred_element_type=F32,
                )
                ratio = mixed / stabilize(mixed)
                for at, h in enumerate(heads):
                    ratio_ref[source, rows, h * HD:(h + 1) * HD] = (
                        ratio[at * rows_n:(at + 1) * rows_n, :]
                    )

    length = len_ref[0]
    loads[0].wait()
    loads[1].wait()
    for step in range(CHUNKS):
        rows = rows_of(step)
        hid = hid_ref[rows, :].astype(F32)
        att = att_ref[rows, :].astype(F32)
        totals = hid + att
        inverse = 1.0 / stabilize(totals)
        keep_ref[rows, :] = hid * inverse
        through_ref[rows, :] = att * inverse / stabilize(att)

        @pl.when(is_last)
        def _():
            token = (CHUNKS - 1 - step) * rows_n + lax.broadcasted_iota(
                jnp.int32, (rows_n, half), 0
            )
            inc_ref[rows, :] = jnp.where(token < length, totals, 0.0).astype(BF16)

    loads[2].wait()
    hid_all = hid_ref[...]
    for slot in range(2):
        part = jnp.dot(
            hid_all, vw_ref[:, slot * kv_half:(slot + 1) * kv_half], preferred_element_type=F32
        )
        vsend[slot] = part.astype(BF16)

        @pl.when(core == slot)
        def _():
            val_ref[...] = part

    for load in loads[3:]:
        load.wait()
    bv_ref[...] = jnp.zeros_like(bv_ref)
    barrier_wait()
    value_copy(other).start()

    @pl.when(is_last)
    def _():
        branch_stage(0)

    @pl.when(jnp.logical_not(is_last))
    def _():
        for step in range(DIRECT, CHUNKS):
            through_copy(step, sec + 1).start()

    query_at = lax.broadcasted_iota(jnp.int32, (seq_len, seq_len), 0)
    key_at = lax.broadcasted_iota(jnp.int32, (seq_len, seq_len), 1)
    allowed = (key_at <= query_at) & (key_at < length)
    for h in range(heads_n):
        kv = h // group
        scores = nt_dot(
            que_ref[:, h * HD:(h + 1) * HD], key_ref[:, kv * HD:(kv + 1) * HD]
        ) / math.sqrt(HD)
        scores = jnp.where(allowed, scores, -1000000000.0)
        weights = jnp.exp(scores - jnp.max(scores, axis=1, keepdims=True))
        prob_ref[dp, h] = (weights / jnp.sum(weights, axis=1, keepdims=True)).astype(BF16)

    value_copy(other).wait()
    values = (val_ref[...] + vrecv[...].astype(F32)).astype(BF16)
    gval_ref[dp] = values

    @pl.when(is_last)
    def _():
        for step in range(RAW, CHUNKS):
            pack_stage(step)

    @pl.when(jnp.logical_not(is_last))
    def _():
        for step in range(CHUNKS):
            pack_stage(step)
        for hop, to in (hops[1], hops[0], hops[2]):
            @pl.when(jnp.logical_not(far(to)))
            def _():
                gather_value(0, hop, to).start()
                for step in range(CHUNKS):
                    gather_probs(step, hop, to).start()

    wide_values = values.astype(F32)
    val_ref[...] = wide_values / stabilize(wide_values)
    for h in range(heads_n):
        kv = h // group
        mixed = jnp.dot(
            prob_ref[dp, h], values[:, kv * HD:(kv + 1) * HD], preferred_element_type=F32
        )
        ratio_ref[dp, :, h * HD:(h + 1) * HD] = mixed / stabilize(mixed)

    for at in range(half // HD):
        flipped = hid_ref[:, at * HD:(at + 1) * HD].astype(F32).T
        hidt_ref[pl.ds(at * HD, HD), :] = flipped.astype(BF16)
    hida_ref[dp] = hidt_ref[pl.ds(pl.multiple_of(dp * block_rows, 16), block_rows), :]

    def branch_next(step):
        section_copy(step, sec + 1).wait_recv()
        branch_stage(step)

    def hidden_stage(step):
        if step == CHUNKS - 1:
            for at in range(DIRECT, CHUNKS):
                for block in range(blocks):
                    direct_copy(at, block).wait_send()
        for hop, to in hops:
            hidden_copy(hop, to).start()

    def join_next(step):
        if step >= DIRECT:
            section_copy(step, sec + 1).wait_recv()
        join_stage(step)

    def give_stage(step):
        for hop, to in hops:
            if step == RAW:
                gather_value(RAW, hop, to).start()
            gather_probs(step, hop, to).start()

    stages = {
        "give": give_stage,
        "values": value_wait, "hidden": hidden_stage, "branch": branch_stage, "relay": relay_stage,
        "gather": gather_stage, "part": part_stage, "mix": mix_stage, "head": head_stage,
        "take": branch_next, "linear": linear_stage, "join": join_stage,
    }

    @pl.when(is_last)
    def _():
        for stage, step in LAST_ORDER:
            stages[stage](step)
        for step in range(CHUNKS):
            final_out(step)

    @pl.when(jnp.logical_not(is_last))
    def _():
        stages["values"] = functools.partial(value_wait, relay=True)
        stages["gather"] = functools.partial(gather_stage, relay=True)
        stages["join"] = join_next
        for stage, step in NEXT_ORDER:
            if stage == "linear":
                stages[stage] = functools.partial(linear_stage, direct=step >= DIRECT)
            stages[stage](step)

    heat_copy(core).start()
    for hop, source in hops:
        for step in range(CHUNKS - 1):
            final_wait(step, source, core)
        final_forward(source, core).start()
    for hop, source in hops:
        hidden_wait(hop, source).wait()
    for step in range(CHUNKS):
        for block in range(blocks):
            mine = core * blocks + block != dp

            @pl.when(mine if step < DIRECT else jnp.logical_and(mine, is_last))
            def _():
                branch_copy(step, block).wait_send()

        @pl.when(gets)
        def _():
            for source in range(peers):
                branch_forward(step, source).wait_send()

        sens_copy(step, core).wait_send()

        @pl.when(sec > 0)
        def _():
            section_copy(step, sec - 1).wait_send()

    def sent(first, hop, to):
        gather_value(first, hop, to).wait_send()
        for step in range(first, CHUNKS):
            gather_probs(step, hop, to).wait_send()

    @pl.when(is_last)
    def _():
        for hop, to in hops:
            sent(RAW, hop, to)
            for step in range(RAW, CHUNKS):
                sum_copy(step, hop, to).wait_send()
        for step in range(RAW):
            for turn in range(rounds):
                for at in range(peers >> (turn + 1)):
                    part_copy(step, turn, at).wait_send()

    @pl.when(jnp.logical_not(is_last))
    def _():
        for step in range(DIRECT, CHUNKS):
            through_copy(step, sec + 1).wait_send()
        for hop, to in hops:
            @pl.when(jnp.logical_not(far(to)))
            def _():
                sent(0, hop, to)

            @pl.when(relays(to))
            def _():
                relay_copy(CHUNKS, value_rows(0, to), to).wait_send()
                for step in range(CHUNKS):
                    relay_copy(step, prob_tiles(step, to), to).wait_send()
            for step in range(CHUNKS):
                sum_copy(step, hop, to).wait_send()

    block_at = pl.ds(pl.multiple_of(dp * block_rows, 16), block_rows)
    total = None
    for hop in range(peers):
        source = lax.rem(dp + hop, peers)
        if hop > 0:
            final_forward(source, other).wait_recv()
            for owner in range(2):
                final_wait(CHUNKS - 1, source, owner)
        sens = jnp.concatenate([sv_ref[source, 0], sv_ref[source, 1]], axis=1)
        term = jnp.dot(hida_ref[source], sens, preferred_element_type=F32)
        total = term if total is None else total + term
    rel_ref[...] = vw_ref[block_at, :].astype(F32) * total
    heat_copy(other).wait_recv()
    heat_copy(core).wait_send()
    heat_ref[...] = jnp.sum((heats[0] + heats[1]).T, axis=0, keepdims=True) / DW

    for hop, to in hops:
        for step in range(CHUNKS):
            for side in range(2 if step == CHUNKS - 1 else 1):
                final_copy(step, hop, to, side).wait_send()
    for hop, source in hops:
        final_forward(source, core).wait_send()


def on_device_chain(hidden_in, attn_out, queries, keys, value_weight, out_weight, lengths):
    peers = lax.axis_size("dp")
    sections = lax.axis_size("section")
    seq_len, half = hidden_in.shape[2:]
    kv_half = keys.shape[3]
    kv_width = value_weight.shape[2]
    width = out_weight.shape[2]
    heads = half // HD
    rows_n = seq_len // CHUNKS
    packed = sum(tiles_of(heads, step) for step in range(CHUNKS))
    vmem = pltpu.VMEM
    dma = pltpu.SemaphoreType.DMA
    whole = pl.BlockSpec(memory_space=pltpu.VMEM)
    heat, relevance = pl.pallas_call(
        functools.partial(chain_kernel, peers, sections),
        out_shape=(
            jax.ShapeDtypeStruct((1, seq_len), F32),
            jax.ShapeDtypeStruct((half // peers, kv_width), F32),
        ),
        in_specs=[pl.BlockSpec(memory_space=pltpu.SMEM)] + [pl.BlockSpec(memory_space=pl.ANY)] * 6,
        out_specs=(whole, whole),
        scratch_shapes=[
            vmem((seq_len, half), BF16),
            vmem((seq_len, half), BF16),
            vmem((seq_len, half), BF16),
            vmem((seq_len, kv_half), BF16),
            vmem((half, kv_width), BF16),
            vmem((half, width), BF16),
            dma((6,)),
            vmem((seq_len, half), F32),
            vmem((seq_len, half), F32),
            vmem((peers, seq_len, half), F32),
            vmem((seq_len, half), BF16),
            vmem((seq_len, half), BF16),
            vmem((peers, heads, seq_len, seq_len), BF16),
            vmem((peers, packed, rows_n, HD), BF16),
            vmem((peers, seq_len, kv_half), BF16),
            vmem((seq_len, kv_half), F32),
            vmem((peers, seq_len, kv_half), F32),
            vmem((2, seq_len, kv_half), BF16),
            vmem((seq_len, kv_half), BF16),
            vmem((half, seq_len), BF16),
            vmem((peers, half // peers, seq_len), BF16),
            vmem((peers, 2, seq_len, kv_half), BF16),
            vmem((2, seq_len, HD), F32),
            vmem((peers * rows_n, half), BF16),
            vmem((CHUNKS, peers, rows_n, kv_half), BF16),
            vmem((CHUNKS, peers, rows_n, kv_half), BF16),
            vmem((CHUNKS, peers // 2, rows_n, width), BF16),
            vmem((CHUNKS, peers, rows_n, width), BF16),
            vmem((RAW, peers, rows_n, half), BF16),
            vmem((RAW, peers - 1, rows_n, half), BF16),
            vmem((seq_len, half), F32),
            vmem((CHUNKS - DIRECT, peers // 2, rows_n, width), BF16),
            dma((CHUNKS, peers // 2)),
            dma((CHUNKS, peers)),
            dma((CHUNKS, peers)),
            dma((RAW, peers)),
            dma((RAW, peers)),
            dma((CHUNKS,)),
            dma((CHUNKS,)),
            dma((CHUNKS, peers, 2)),
            dma((CHUNKS, peers, 2)),
            dma((CHUNKS,)),
            dma((CHUNKS,)),
            dma((peers,)),
            dma((peers,)),
            dma((2,)),
            dma((2,)),
            dma((CHUNKS + 1, peers)),
            dma((CHUNKS + 1, peers)),
            dma((CHUNKS, peers)),
            dma((CHUNKS, peers)),
            dma((peers,)),
            dma((peers,)),
            dma((CHUNKS + 1,)),
            dma((CHUNKS,)),
            dma((CHUNKS,)),
            dma((CHUNKS - DIRECT, peers // 2)),
        ],
        compiler_params=pltpu.CompilerParams(
            collective_id=0, has_side_effects=True, vmem_limit_bytes=40 * 1024 * 1024
        ),
        name="relevance_chain",
    )(
        lengths,
        *(
            pltpu.with_memory_space_constraint(operand, pltpu.MemorySpace.HBM)
            for operand in (
                hidden_in[0, 0], attn_out[0, 0], queries[0, 0], keys[0, 0], value_weight[0], out_weight[0],
            )
        ),
    )
    return heat[None], relevance[None]


def solution(mesh):
    placed = (
        P("section", ("groups", "dp"), None, "mp"),
        P("section", ("groups", "dp"), None, "mp"),
        P("section", ("groups", "dp"), None, "mp"),
        P("section", ("groups", "dp"), None, "mp"),
        P("section", "mp", None),
        P("section", "mp", "dp"),
        P(("groups", "dp")),
    )
    peers = mesh.shape["dp"]
    aligned = peers == 4 and mesh.shape["section"] == 2
    return jax.shard_map(
        on_device_chain if aligned else on_device,
        mesh=mesh,
        in_specs=placed,
        out_specs=(
            P("section", ("groups", "dp"), None),
            P(("groups", "section"), ("mp", "dp"), None),
        ),
        check_vma=False,
    )
```

```python
import functools
import math

import jax
import jax.numpy as jnp
from jax import lax
from jax.experimental import pallas as pl
from jax.experimental.pallas import tpu as pltpu
from jax.sharding import PartitionSpec as P

DW = 2560
HD = 128
QH = 20
KVH = 4


EPS = 0.25


def from_behind(shard, axis, by):
    peers = lax.axis_size(axis)
    pairs = [(i, i + by) for i in range(peers) if 0 <= i + by < peers]
    return lax.ppermute(shard, axis, pairs)


def stabilize(entries):
    return jnp.where(entries >= 0, entries + EPS, entries - EPS)


def gated(active, compute, operand, out_shape, out_type):
    return lax.cond(active, compute, lambda unused: jnp.zeros(out_shape, out_type), operand)


def on_device(hidden_in, attn_out, queries, keys, value_weight, out_weight, lengths):
    inputs = hidden_in[0, 0]
    branch = attn_out[0, 0]
    query_rows = queries[0, 0]
    key_rows = keys[0, 0]
    value_rows = value_weight[0]
    seq_len = inputs.shape[0]
    half_width = inputs.shape[1]
    group_size = QH // KVH
    local_kv = key_rows.shape[1] // HD
    kv_width = value_rows.shape[1]
    sections = lax.axis_size("section")
    section_pos = lax.axis_index("section")
    core_pos = lax.axis_index("mp")
    out_cols = lax.all_gather(out_weight, "dp", axis=2, tiled=True)[0]
    inputs_f = inputs.astype(jnp.float32)
    branch_f = branch.astype(jnp.float32)
    totals = inputs_f + branch_f
    value_part = jnp.dot(inputs, value_rows, preferred_element_type=jnp.float32)
    value_all = lax.psum(value_part.astype(jnp.bfloat16), "mp").astype(jnp.float32)
    value_mine = lax.dynamic_slice_in_dim(value_all, core_pos * local_kv * HD, local_kv * HD, 1)
    values_bf = lax.optimization_barrier(value_mine.astype(jnp.bfloat16))
    values_f = values_bf.astype(jnp.float32)
    query_heads = query_rows.reshape(seq_len, local_kv, group_size, HD)
    key_heads = key_rows.reshape(seq_len, local_kv, HD)
    scores = jnp.einsum(
        "tgjd,sgd->gjts", query_heads, key_heads, preferred_element_type=jnp.float32
    ) / math.sqrt(HD)
    position = lax.iota(jnp.int32, seq_len)
    allowed = (position[None, :] <= position[:, None]) & (position[None, :] < lengths[0])
    scores = jnp.where(allowed, scores, -1000000000.0)
    row_top = jnp.max(scores, axis=-1, keepdims=True)
    weights = jnp.exp(scores - row_top)
    prob_rows = (weights / jnp.sum(weights, axis=-1, keepdims=True)).astype(jnp.bfloat16)
    mixed_heads = jnp.einsum(
        "gjts,sgd->tgjd",
        prob_rows,
        values_bf.reshape(seq_len, local_kv, HD),
        preferred_element_type=jnp.float32,
    ).reshape(seq_len, local_kv * group_size * HD)
    valid_rows = (position < lengths[0]).astype(jnp.float32)
    current = (totals * valid_rows[:, None]).astype(jnp.bfloat16)
    result = jnp.zeros((seq_len, half_width), jnp.bfloat16)
    sens_kept = jnp.zeros((seq_len, kv_width), jnp.bfloat16)
    for turn_index in range(sections):
        active = section_pos == sections - 1 - turn_index
        sens_total = current.astype(jnp.float32) / stabilize(totals)
        sens_branch = (branch_f * sens_total / stabilize(branch_f)).astype(jnp.bfloat16)
        sens_full = lax.all_gather(sens_branch, "mp", axis=1, tiled=True)

        def through_heads(operand):
            back_mixed = lax.dot_general(
                operand, out_cols, (((1,), (1,)), ((), ())), preferred_element_type=jnp.float32
            )
            sens_mixed = (mixed_heads * back_mixed / stabilize(mixed_heads)).astype(jnp.bfloat16)
            back_values = jnp.einsum(
                "gjts,tgjd->sgd",
                prob_rows,
                sens_mixed.reshape(seq_len, local_kv, group_size, HD),
                preferred_element_type=jnp.float32,
            ).reshape(seq_len, local_kv * HD)
            return (values_f * back_values / stabilize(values_f)).astype(jnp.bfloat16)

        sens_values = gated(
            active, through_heads, sens_full, (seq_len, local_kv * HD), jnp.bfloat16
        )
        sens_all = lax.all_gather(sens_values, "mp", axis=1, tiled=True)

        def through_values(operand):
            back_inputs = lax.dot_general(
                operand, value_rows, (((1,), (1,)), ((), ())), preferred_element_type=jnp.float32
            )
            return (inputs_f * sens_total + inputs_f * back_inputs).astype(jnp.bfloat16)

        outgoing = gated(active, through_values, sens_all, (seq_len, half_width), jnp.bfloat16)
        result = jnp.where(active, outgoing, result)
        sens_kept = jnp.where(active, sens_all, sens_kept)
        if turn_index + 1 < sections:
            arrived = from_behind(outgoing, "section", -1)
            current = jnp.where(section_pos == sections - 2 - turn_index, arrived, current)
    heat_part = jnp.sum(result.astype(jnp.float32), axis=1)
    heat_rows = lax.psum(heat_part, "mp") / DW
    block_rows = half_width // lax.axis_size("dp")
    row_start = lax.axis_index("dp") * block_rows
    value_block = lax.dynamic_slice_in_dim(value_rows, row_start, block_rows, 0).astype(jnp.float32)
    summed = lax.psum_scatter(
        lax.dot_general(
            inputs, sens_kept, (((0,), (0,)), ((), ())), preferred_element_type=jnp.float32
        ).astype(jnp.bfloat16),
        "dp",
        scatter_dimension=0,
        tiled=True,
    ).astype(jnp.float32)
    relevance_rows = value_block * summed
    return (heat_rows[None, None, :], relevance_rows[None])


CHUNKS = 4
RAW = 2
SEGMENTS = (((0, 128),), ((0, 64), (64, 32)), ((0, 64),), ((0, 32),))
TILE = 256
MESH_ID = pl.DeviceIdType.MESH
F32 = jnp.float32
BF16 = jnp.bfloat16
DIRECT = 1
LAST_ORDER = (
    ("branch", 1), ("give", 2), ("give", 3), ("branch", 2), ("part", 0), ("branch", 3),
    ("mix", 0), ("part", 1), ("head", 0), ("emit", 0), ("mix", 1), ("values", 2), ("gather", 2),
    ("gather", 3), ("linear", 2), ("linear", 3), ("head", 1), ("emit", 1), ("join", 2),
    ("join", 3), ("emit", 2), ("emit", 3), ("hidden", 3),
)
NEXT_ORDER = (
    ("relay", 0), ("relay", 1), ("relay", 2), ("relay", 3), ("values", 0), ("gather", 0),
    ("hidden", 0), ("gather", 1), ("take", 0), ("gather", 2), ("gather", 3), ("linear", 0),
    ("join", 0), ("emit", 0), ("linear", 1), ("linear", 2), ("linear", 3), ("join", 1),
    ("join", 2), ("join", 3), ("emit", 1), ("emit", 2), ("emit", 3),
)


def tiles_of(heads, step):
    return sum(-(-heads // (HD // lanes)) for _, lanes in SEGMENTS[step])


def nt_dot(left, right):
    return lax.dot_general(left, right, (((1,), (1,)), ((), ())), preferred_element_type=F32)


def tn_dot(left, right):
    return lax.dot_general(left, right, (((0,), (0,)), ((), ())), preferred_element_type=F32)


def chain_kernel(
    peers, sections, len_ref, hid_in, att_in, que_in, key_in, vw_in, ow_in,
    heat_out, rel_out, hid_ref, att_ref, que_ref, key_ref, vw_ref, ow_ref, load_sem,
    through_ref, keep_ref, ratio_ref, inc_ref, out_ref, prob_ref, pack_ref, gval_ref, val_ref, bv_ref,
    vsend, vrecv, hidt_ref, hida_ref, sv_ref, heats, sm_ref, bvsend, bvbuf,
    asend, abuf, psend, pbuf, below_ref, dsend,
    done, a_recv, p_recv, s_recv, f_recv, x_recv, one_recv, k_recv, b_recv,
    heat_ref, rel_ref, out_sem,
):
    dp = lax.axis_index("dp")
    sec = lax.axis_index("section")
    core = lax.axis_index("mp")
    other = 1 - core
    seq_len, half = hid_ref.shape
    rows_n = seq_len // CHUNKS
    width = ow_ref.shape[1]
    blocks = peers // 2
    local_kv = key_ref.shape[1] // HD
    group = QH // KVH
    heads_n = local_kv * group
    kv_half = local_kv * HD
    block_rows = half // peers
    is_last = sec == sections - 1
    gets = core == dp // blocks
    hops = [(hop, lax.rem(dp + hop, peers)) for hop in range(1, peers)]

    loads = [
        pltpu.make_async_copy(source, target, load_sem.at[at])
        for at, (source, target) in enumerate((
            (hid_in, hid_ref), (att_in, att_ref), (vw_in, vw_ref),
            (que_in, que_ref), (key_in, key_ref), (ow_in, ow_ref),
        ))
    ]
    for load in loads:
        load.start()

    barrier = pltpu.get_barrier_semaphore()
    for hop, to in hops:
        for target in range(2):
            pl.semaphore_signal(
                barrier, inc=1, device_id={"dp": to, "mp": target}, device_id_type=MESH_ID
            )
    pl.semaphore_signal(barrier, inc=1, device_id={"mp": other}, device_id_type=MESH_ID)

    @pl.when(sec > 0)
    def _():
        pl.semaphore_signal(
            barrier, inc=1, device_id={"section": sec - 1}, device_id_type=MESH_ID
        )

    @pl.when(sec < sections - 1)
    def _():
        for at in range(peers):
            pl.semaphore_signal(
                barrier, inc=1, device_id={"dp": at, "section": sec + 1}, device_id_type=MESH_ID
            )

    def barrier_wait():
        greeted = 2 * (peers - 1) + 1

        @pl.when(is_last)
        def _():
            pl.semaphore_wait(barrier, greeted + peers)

        @pl.when(jnp.logical_not(is_last))
        def _():
            pl.semaphore_wait(barrier, greeted + 1)

    def remote(source, target, send, recv, device):
        return pltpu.make_async_remote_copy(
            src_ref=source, dst_ref=target, send_sem=send, recv_sem=recv,
            device_id=device, device_id_type=MESH_ID,
        )

    def rows_of(step):
        return pl.ds((CHUNKS - 1 - step) * rows_n, rows_n)

    def branch_copy(step, block):
        return remote(
            asend.at[step, block], abuf.at[step, dp],
            done.at[0], a_recv.at[step, dp], {"dp": core * blocks + block},
        )

    def direct_copy(step, block):
        return remote(
            dsend.at[step - DIRECT, block], abuf.at[step, dp],
            done.at[1], a_recv.at[step, dp],
            {"dp": core * blocks + block, "section": sec - 1},
        )

    def through_copy(step, target):
        rows = rows_of(step)
        return remote(
            through_ref.at[rows], below_ref.at[rows],
            done.at[0], one_recv.at[3], {"section": target},
        )

    def branch_forward(step, source):
        view = abuf.at[step, source]
        return remote(
            view, view, done.at[0], a_recv.at[step, source], {"mp": other}
        )

    rounds = peers.bit_length() - 1

    def slot_of(turn, target):
        return peers - (peers >> turn) + target // (2 << turn)

    def part_target(turn, at):
        bit = 1 << turn
        return lax.rem(dp, bit) + bit * (2 * at + 1 - lax.rem(dp // bit, 2))

    def part_copy(step, turn, at):
        bit = 1 << turn
        slot = peers - (peers >> turn) + at
        return remote(
            psend.at[step, part_target(turn, at)], pbuf.at[step, slot],
            done.at[0], p_recv.at[step, slot],
            {"dp": dp + bit - 2 * bit * lax.rem(dp // bit, 2)},
        )

    def part_take(step, turn, target):
        slot = slot_of(turn, target)
        view = pbuf.at[step, slot]
        remote(
            view, view, done.at[0], p_recv.at[step, slot], {"mp": other}
        ).wait_recv()
        return pbuf[step, slot].astype(F32)

    def mix_stage(step):
        for turn in range(1, rounds):
            for at in range(peers >> (turn + 1)):
                target = part_target(turn, at)
                running = psend[step, target].astype(F32)
                for before in range(turn):
                    running = running + part_take(step, before, target)
                psend[step, target] = running.astype(BF16)
                part_copy(step, turn, at).start()

    def value_rows(step, source):
        return gval_ref.at[source, pl.ds(0, (CHUNKS - step) * rows_n)]

    def prob_tiles(step, source):
        first = sum(tiles_of(heads_n, before) for before in range(step))
        return pack_ref.at[source, pl.ds(first, tiles_of(heads_n, step))]

    def relays(source, through):
        return jnp.logical_or(
            jnp.logical_and(source == 0, through == peers - 2),
            jnp.logical_and(source == peers - 1, through == 1),
        )

    def lane(relay, source, to):
        return relays(source, to).astype(jnp.int32) if relay else 0

    def gather_value(first, to, relay=False):
        view = value_rows(first, dp)
        return remote(
            view, view, done.at[0], k_recv.at[CHUNKS, lane(relay, dp, to)], {"dp": to}
        )

    def gather_probs(step, to, relay=False):
        view = prob_tiles(step, dp)
        return remote(
            view, view, done.at[0], k_recv.at[step, lane(relay, dp, to)], {"dp": to}
        )

    def sum_copy(step, hop, to):
        return remote(
            bvsend.at[step, hop], bvbuf.at[step, dp],
            done.at[0], b_recv.at[step], {"dp": to},
        )

    def sens_copy(step, owner):
        view = sv_ref.at[dp, owner, rows_of(step)]
        return remote(view, view, done.at[0], s_recv.at[step], {"mp": other})

    def final_copy(step, hop, to, side):
        view = sv_ref.at[dp, core, rows_of(step)]
        return remote(
            view, view, done.at[0], f_recv.at[step // (CHUNKS - 1)],
            {"dp": to, "mp": core if side == 0 else other},
        )

    def final_wait():
        view = sv_ref.at[pl.ds(0, peers - 1), 0, pl.ds(rows_n, seq_len - rows_n)]
        remote(view, view, done.at[0], f_recv.at[0], {"mp": other}).wait_recv()

    def final_wait_last():
        view = sv_ref.at[pl.ds(0, peers - 1), :, rows_of(CHUNKS - 1)]
        remote(view, view, done.at[0], f_recv.at[1], {"mp": other}).wait_recv()

    def forward_wait():
        view = sv_ref.at[pl.ds(0, peers - 1), 0, pl.ds(rows_n, seq_len - rows_n)]
        remote(view, view, done.at[0], f_recv.at[2], {"mp": other}).wait_recv()

    def final_forward(source, owner):
        view = sv_ref.at[source, owner, pl.ds(rows_n, seq_len - rows_n)]
        return remote(view, view, done.at[0], f_recv.at[2], {"mp": other})

    def final_out(step):
        for hop, to in hops:
            for side in range(2 if step == CHUNKS - 1 else 1):
                final_copy(step, hop, to, side).start()

    def section_copy(step, target):
        return remote(
            out_ref.at[rows_of(step)], inc_ref.at[rows_of(step)],
            done.at[0], x_recv.at[step], {"section": target},
        )

    def hidden_copy(hop, to):
        return remote(
            hidt_ref.at[pl.ds(pl.multiple_of(to * block_rows, 16), block_rows)], hida_ref.at[dp],
            done.at[0], one_recv.at[2], {"dp": to},
        )

    def hidden_wait():
        view = hida_ref.at[pl.ds(0, peers - 1)]
        remote(view, view, done.at[0], one_recv.at[2], {"mp": other}).wait_recv()

    def value_copy(slot):
        return remote(
            vsend.at[slot], vrecv, done.at[0], one_recv.at[0], {"mp": other}
        )

    def heat_copy(slot):
        return remote(
            heats.at[slot], heats.at[slot], done.at[0], one_recv.at[1], {"mp": other}
        )

    def branch_stage(step):
        rows = rows_of(step)
        sens = (inc_ref[rows, :].astype(F32) * through_ref[rows, :]).astype(BF16)
        for block in range(blocks):
            to = core * blocks + block
            piece = sens[:, block * width:(block + 1) * width]
            asend[step, block] = piece

            @pl.when(to == dp)
            def _():
                abuf[step, dp] = piece
                branch_forward(step, dp).start()

            @pl.when(to != dp)
            def _():
                branch_copy(step, block).start()

    def branch_wait(step, direct):
        @pl.when(gets)
        def _():
            for hop in range(0 if direct else 1, peers):
                source = lax.rem(dp + hop, peers)
                branch_forward(step, source).wait_recv()
                branch_forward(step, source).start()

        @pl.when(jnp.logical_not(gets))
        def _():
            for source in range(peers):
                branch_forward(step, source).wait_recv()

        return abuf[step].reshape(peers * rows_n, width)

    def part_stage(step):
        stacked = branch_wait(step, False)

        def tile(at, unused):
            start = pl.multiple_of(at * TILE, TILE)
            part = nt_dot(stacked, ow_ref[pl.ds(start, TILE), :]).astype(BF16)
            psend[step, :, :, pl.ds(start, TILE)] = part.reshape(peers, rows_n, TILE)
            return unused

        lax.fori_loop(0, half // TILE, tile, 0, unroll=True)
        for at in range(peers // 2):
            part_copy(step, 0, at).start()

    def add_values(seq, rows, mixed):
        for kv in range(local_kv):
            heads = range(kv * group, (kv + 1) * group)
            left = jnp.concatenate([prob_ref[seq, h, rows, :] for h in heads], axis=0)
            right = jnp.concatenate([mixed[:, h * HD:(h + 1) * HD] for h in heads], axis=0)
            columns = pl.ds(kv * HD, HD)
            bv_ref[seq, :, columns] = bv_ref[seq, :, columns] + tn_dot(left, right)

    def head_stage(step):
        rows = rows_of(step)
        back = psend[step, dp].astype(F32)
        for turn in range(rounds):
            back = back + part_take(step, turn, dp)
        add_values(dp, rows, (ratio_ref[dp, rows, :] * back).astype(BF16))
        settle(step, bv_ref[dp, rows, :])

    def linear_stage(step, direct=False):
        rows = rows_of(step)
        stacked = branch_wait(step, direct)
        for at in range(half // TILE):
            columns = pl.ds(at * TILE, TILE)
            part = nt_dot(stacked, ow_ref[columns, :])
            ratio = ratio_ref[:, rows, columns].reshape(peers * rows_n, TILE)
            sm_ref[:, columns] = (ratio * part).astype(BF16)
        for seq in range(peers):
            add_values(seq, rows, sm_ref[seq * rows_n:(seq + 1) * rows_n, :])
        for hop, to in hops:
            bvsend[step, hop] = bv_ref[to, rows, :].astype(BF16)
            sum_copy(step, hop, to).start()

    def join_stage(step):
        total = bv_ref[dp, rows_of(step), :]
        view = bvbuf.at[step, pl.ds(0, peers - 1)]
        remote(view, view, done.at[0], b_recv.at[step], {"mp": other}).wait_recv()
        for hop, source in hops:
            total = total + bvbuf[step, source].astype(F32)
        settle(step, total)

    def settle(step, back_values):
        rows = rows_of(step)
        sv_ref[dp, core, rows, :] = (val_ref[rows, :] * back_values).astype(BF16)
        sens_copy(step, core).start()

        @pl.when(jnp.logical_not(is_last))
        def _():
            final_out(step)

    def emit_stage(step):
        rows = rows_of(step)
        sens_copy(step, other).wait_recv()
        sens = jnp.concatenate([sv_ref[dp, 0, rows, :], sv_ref[dp, 1, rows, :]], axis=1)
        sums = jnp.zeros((rows_n, HD), F32)
        for at in range(half // TILE):
            columns = pl.ds(at * TILE, TILE)
            back_in = nt_dot(sens, vw_ref[columns, :])
            out = (
                inc_ref[rows, columns].astype(F32) * keep_ref[rows, columns]
                + hid_ref[rows, columns].astype(F32) * back_in
            ).astype(BF16)
            out_ref[rows, columns] = out
            wide = out.astype(F32)
            for lane in range(TILE // HD):
                sums = sums + wide[:, lane * HD:(lane + 1) * HD]
        heats[core, rows, :] = sums

        @pl.when(sec > 0)
        def _():
            if step >= DIRECT:
                if step == DIRECT:
                    view = below_ref.at[pl.ds(0, (CHUNKS - DIRECT) * rows_n)]
                    remote(view, view, done.at[0], one_recv.at[3], {"mp": other}).wait_recv()
                below = (out_ref[rows, :].astype(F32) * below_ref[rows, :]).astype(BF16)
                for block in range(blocks):
                    dsend[step - DIRECT, block] = below[:, block * width:(block + 1) * width]
                    direct_copy(step, block).start()
            else:
                section_copy(step, sec - 1).start()

    lane_at = lax.broadcasted_iota(jnp.int32, (rows_n, HD), 1)

    def shifted(tile, start, count, to):
        inside = (lane_at >= start) & (lane_at < start + count)
        kept = jnp.where(inside, tile, 0.0)
        return kept if start == to else pltpu.roll(kept, (to - start) % HD, 1)

    def pack_stage(step):
        at = sum(tiles_of(heads_n, before) for before in range(step))
        for start, lanes in SEGMENTS[step]:
            per = HD // lanes
            for first in range(0, heads_n, per):
                tile = None
                for h in range(first, min(first + per, heads_n)):
                    piece = shifted(
                        prob_ref[dp, h, rows_of(step), :].astype(F32), start, lanes, (h - first) * lanes
                    )
                    tile = piece if tile is None else tile + piece
                pack_ref[dp, at] = tile.astype(BF16)
                at += 1

    def value_wait(first, relay=False):
        gather_wait(
            CHUNKS, lambda count: gval_ref.at[pl.ds(0, count), pl.ds(0, (CHUNKS - first) * rows_n)], relay
        )

    def far(to):
        return jnp.logical_and(dp + to == peers - 1, jnp.logical_or(dp == 0, to == 0))

    def relay_copy(step, view, source):
        return remote(
            view, view, done.at[0], k_recv.at[step, 0], {"dp": peers - 1 - source}
        )

    def gather_wait(step, views, relay):
        def wait(view):
            remote(view, view, done.at[0], k_recv.at[step, 0], {"mp": other}).wait_recv()

        if relay:
            inner = jnp.logical_and(dp > 0, dp < peers - 1)

            @pl.when(inner)
            def _():
                wait(views(peers - 2))

            @pl.when(jnp.logical_not(inner))
            def _():
                wait(views(peers - 1))
        else:
            wait(views(peers - 1))

    def relay_stage(step):
        for end, through in ((0, peers - 2), (peers - 1, 1)):
            @pl.when(dp == through)
            def _():
                views = [(step, prob_tiles(step, end))]
                if step == 0:
                    views.insert(0, (CHUNKS, value_rows(0, end)))
                for at, view in views:
                    remote(view, view, done.at[0], k_recv.at[at, 1], {"mp": other}).wait_recv()
                    relay_copy(at, view, end).start()

    def gather_stage(step, relay=False):
        rows = rows_of(step)
        depth = (CHUNKS - step) * rows_n
        first_tile = sum(tiles_of(heads_n, before) for before in range(step))
        tiles = pl.ds(first_tile, tiles_of(heads_n, step))
        gather_wait(step, lambda count: pack_ref.at[pl.ds(0, count), tiles], relay)
        for hop, source in hops:
            for h in range(heads_n):
                at = first_tile
                whole = None
                for start, lanes in SEGMENTS[step]:
                    per = HD // lanes
                    piece = shifted(
                        pack_ref[source, at + h // per].astype(F32), h % per * lanes, lanes, start
                    )
                    whole = piece if whole is None else whole + piece
                    at += -(-heads_n // per)
                prob_ref[source, h, rows, :] = whole.astype(BF16)
            for kv in range(local_kv):
                heads = range(kv * group, (kv + 1) * group)
                left = jnp.concatenate(
                    [prob_ref[source, h, rows, pl.ds(0, depth)] for h in heads], axis=0
                )
                mixed = jnp.dot(
                    left, gval_ref[source, pl.ds(0, depth), pl.ds(kv * HD, HD)],
                    preferred_element_type=F32,
                )
                ratio = mixed / stabilize(mixed)
                for at, h in enumerate(heads):
                    ratio_ref[source, rows, h * HD:(h + 1) * HD] = (
                        ratio[at * rows_n:(at + 1) * rows_n, :]
                    )

    length = len_ref[0]
    loads[0].wait()
    loads[1].wait()
    for step in range(CHUNKS):
        rows = rows_of(step)
        hid = hid_ref[rows, :].astype(F32)
        att = att_ref[rows, :].astype(F32)
        totals = hid + att
        inverse = 1.0 / stabilize(totals)
        keep_ref[rows, :] = hid * inverse
        through_ref[rows, :] = att * inverse / stabilize(att)

        @pl.when(is_last)
        def _():
            token = (CHUNKS - 1 - step) * rows_n + lax.broadcasted_iota(
                jnp.int32, (rows_n, half), 0
            )
            inc_ref[rows, :] = jnp.where(token < length, totals, 0.0).astype(BF16)

    loads[2].wait()
    hid_all = hid_ref[...]
    for slot in range(2):
        part = jnp.dot(
            hid_all, vw_ref[:, slot * kv_half:(slot + 1) * kv_half], preferred_element_type=F32
        )
        vsend[slot] = part.astype(BF16)

        @pl.when(core == slot)
        def _():
            val_ref[...] = part

    for load in loads[3:]:
        load.wait()
    bv_ref[...] = jnp.zeros_like(bv_ref)
    barrier_wait()
    value_copy(other).start()

    @pl.when(is_last)
    def _():
        branch_stage(0)

    @pl.when(jnp.logical_not(is_last))
    def _():
        for step in range(DIRECT, CHUNKS):
            through_copy(step, sec + 1).start()

    query_at = lax.broadcasted_iota(jnp.int32, (seq_len, seq_len), 0)
    key_at = lax.broadcasted_iota(jnp.int32, (seq_len, seq_len), 1)
    allowed = (key_at <= query_at) & (key_at < length)
    for h in range(heads_n):
        kv = h // group
        scores = nt_dot(
            que_ref[:, h * HD:(h + 1) * HD], key_ref[:, kv * HD:(kv + 1) * HD]
        ) / math.sqrt(HD)
        scores = jnp.where(allowed, scores, -1000000000.0)
        weights = jnp.exp(scores - jnp.max(scores, axis=1, keepdims=True))
        prob_ref[dp, h] = (weights / jnp.sum(weights, axis=1, keepdims=True)).astype(BF16)

    value_copy(other).wait_recv()
    values = (val_ref[...] + vrecv[...].astype(F32)).astype(BF16)
    gval_ref[dp] = values

    @pl.when(is_last)
    def _():
        for step in range(RAW, CHUNKS):
            pack_stage(step)

    @pl.when(jnp.logical_not(is_last))
    def _():
        for step in range(CHUNKS):
            pack_stage(step)
        for hop, to in (hops[1], hops[0], hops[2]):
            @pl.when(jnp.logical_not(far(to)))
            def _():
                gather_value(0, to, True).start()
                for step in range(CHUNKS):
                    gather_probs(step, to, True).start()

    wide_values = values.astype(F32)
    val_ref[...] = wide_values / stabilize(wide_values)
    for h in range(heads_n):
        kv = h // group
        mixed = jnp.dot(
            prob_ref[dp, h], values[:, kv * HD:(kv + 1) * HD], preferred_element_type=F32
        )
        ratio_ref[dp, :, h * HD:(h + 1) * HD] = mixed / stabilize(mixed)

    for at in range(half // HD):
        flipped = hid_ref[:, at * HD:(at + 1) * HD].astype(F32).T
        hidt_ref[pl.ds(at * HD, HD), :] = flipped.astype(BF16)
    hida_ref[dp] = hidt_ref[pl.ds(pl.multiple_of(dp * block_rows, 16), block_rows), :]

    def branch_next(step):
        section_copy(step, sec + 1).wait_recv()
        branch_stage(step)

    def hidden_stage(step):
        if step == CHUNKS - 1:
            for at in range(DIRECT, CHUNKS):
                for block in range(blocks):
                    direct_copy(at, block).wait_send()
                section_copy(at, sec - 1).start()
        for hop, to in hops:
            hidden_copy(hop, to).start()

    def emit_next(step):
        if step >= DIRECT:
            section_copy(step, sec + 1).wait_recv()
        emit_stage(step)

    def give_stage(step):
        for hop, to in hops:
            if step == RAW:
                gather_value(RAW, to).start()
            gather_probs(step, to).start()

    stages = {
        "give": give_stage, "emit": emit_stage,
        "values": value_wait, "hidden": hidden_stage, "branch": branch_stage, "relay": relay_stage,
        "gather": gather_stage, "part": part_stage, "mix": mix_stage, "head": head_stage,
        "take": branch_next, "linear": linear_stage, "join": join_stage,
    }

    @pl.when(is_last)
    def _():
        for stage, step in LAST_ORDER:
            stages[stage](step)
        for step in range(CHUNKS):
            final_out(step)

    @pl.when(jnp.logical_not(is_last))
    def _():
        stages["values"] = functools.partial(value_wait, relay=True)
        stages["gather"] = functools.partial(gather_stage, relay=True)
        stages["emit"] = emit_next
        for stage, step in NEXT_ORDER:
            if stage == "linear":
                stages[stage] = functools.partial(linear_stage, direct=step >= DIRECT)
            stages[stage](step)

    heat_copy(core).start()
    final_wait()
    for hop, source in hops:
        final_forward(source, core).start()
    hidden_wait()
    block_at = pl.ds(pl.multiple_of(dp * block_rows, 16), block_rows)
    total = None
    for hop in range(peers):
        source = lax.rem(dp + hop, peers)
        if hop == 1:
            forward_wait()
            final_wait_last()
        sens = jnp.concatenate([sv_ref[source, 0], sv_ref[source, 1]], axis=1)
        term = jnp.dot(hida_ref[source], sens, preferred_element_type=F32)
        total = term if total is None else total + term
    rel_ref[...] = vw_ref[block_at, :].astype(F32) * total
    stores = [
        pltpu.make_async_copy(source, target, out_sem.at[at])
        for at, (source, target) in enumerate(((heat_ref, heat_out), (rel_ref, rel_out)))
    ]
    stores[1].start()
    heat_copy(other).wait_recv()
    heat_ref[...] = jnp.sum((heats[0] + heats[1]).T, axis=0, keepdims=True) / DW
    stores[0].start()
    for hop, to in hops:
        for step in range(CHUNKS):
            for side in range(2 if step == CHUNKS - 1 else 1):
                final_copy(step, hop, to, side).wait_send()
    for hop, source in hops:
        final_forward(source, core).wait_send()
    for step in range(CHUNKS):
        for block in range(blocks):
            mine = core * blocks + block != dp

            @pl.when(mine if step < DIRECT else jnp.logical_and(mine, is_last))
            def _():
                branch_copy(step, block).wait_send()

        @pl.when(gets)
        def _():
            for source in range(peers):
                branch_forward(step, source).wait_send()

        sens_copy(step, core).wait_send()

        @pl.when(sec > 0)
        def _():
            section_copy(step, sec - 1).wait_send()

    def sent(first, hop, to):
        gather_value(first, to).wait_send()
        for step in range(first, CHUNKS):
            gather_probs(step, to).wait_send()

    @pl.when(is_last)
    def _():
        for hop, to in hops:
            sent(RAW, hop, to)
            for step in range(RAW, CHUNKS):
                sum_copy(step, hop, to).wait_send()
        for step in range(RAW):
            for turn in range(rounds):
                for at in range(peers >> (turn + 1)):
                    part_copy(step, turn, at).wait_send()

    @pl.when(jnp.logical_not(is_last))
    def _():
        for step in range(DIRECT, CHUNKS):
            through_copy(step, sec + 1).wait_send()
        for hop, to in hops:
            @pl.when(jnp.logical_not(far(to)))
            def _():
                sent(0, hop, to)

            @pl.when(relays(to, dp))
            def _():
                relay_copy(CHUNKS, value_rows(0, to), to).wait_send()
                for step in range(CHUNKS):
                    relay_copy(step, prob_tiles(step, to), to).wait_send()
            for step in range(CHUNKS):
                sum_copy(step, hop, to).wait_send()

    value_copy(other).wait_send()
    heat_copy(core).wait_send()
    for hop, to in hops:
        hidden_copy(hop, to).wait_send()
    for store in stores:
        store.wait()


def on_device_chain(hidden_in, attn_out, queries, keys, value_weight, out_weight, lengths):
    peers = lax.axis_size("dp")
    sections = lax.axis_size("section")
    seq_len, half = hidden_in.shape[2:]
    kv_half = keys.shape[3]
    kv_width = value_weight.shape[2]
    width = out_weight.shape[2]
    heads = half // HD
    rows_n = seq_len // CHUNKS
    packed = sum(tiles_of(heads, step) for step in range(CHUNKS))
    vmem = pltpu.VMEM
    dma = pltpu.SemaphoreType.DMA
    heat, relevance = pl.pallas_call(
        functools.partial(chain_kernel, peers, sections),
        out_shape=(
            jax.ShapeDtypeStruct((1, seq_len), F32),
            jax.ShapeDtypeStruct((half // peers, kv_width), F32),
        ),
        in_specs=[pl.BlockSpec(memory_space=pltpu.SMEM)] + [pl.BlockSpec(memory_space=pl.ANY)] * 6,
        out_specs=(pl.BlockSpec(memory_space=pl.ANY), pl.BlockSpec(memory_space=pl.ANY)),
        scratch_shapes=[
            vmem((seq_len, half), BF16),
            vmem((seq_len, half), BF16),
            vmem((seq_len, half), BF16),
            vmem((seq_len, kv_half), BF16),
            vmem((half, kv_width), BF16),
            vmem((half, width), BF16),
            dma((6,)),
            vmem((seq_len, half), F32),
            vmem((seq_len, half), F32),
            vmem((peers, seq_len, half), F32),
            vmem((seq_len, half), BF16),
            vmem((seq_len, half), BF16),
            vmem((peers, heads, seq_len, seq_len), BF16),
            vmem((peers, packed, rows_n, HD), BF16),
            vmem((peers, seq_len, kv_half), BF16),
            vmem((seq_len, kv_half), F32),
            vmem((peers, seq_len, kv_half), F32),
            vmem((2, seq_len, kv_half), BF16),
            vmem((seq_len, kv_half), BF16),
            vmem((half, seq_len), BF16),
            vmem((peers, half // peers, seq_len), BF16),
            vmem((peers, 2, seq_len, kv_half), BF16),
            vmem((2, seq_len, HD), F32),
            vmem((peers * rows_n, half), BF16),
            vmem((CHUNKS, peers, rows_n, kv_half), BF16),
            vmem((CHUNKS, peers, rows_n, kv_half), BF16),
            vmem((CHUNKS, peers // 2, rows_n, width), BF16),
            vmem((CHUNKS, peers, rows_n, width), BF16),
            vmem((RAW, peers, rows_n, half), BF16),
            vmem((RAW, peers - 1, rows_n, half), BF16),
            vmem((seq_len, half), F32),
            vmem((CHUNKS - DIRECT, peers // 2, rows_n, width), BF16),
            dma((2,)),
            dma((CHUNKS, peers)),
            dma((RAW, peers - 1)),
            dma((CHUNKS,)),
            dma((3,)),
            dma((CHUNKS,)),
            dma((4,)),
            dma((CHUNKS + 1, 2)),
            dma((CHUNKS,)),
            vmem((1, seq_len), F32),
            vmem((half // peers, kv_width), F32),
            dma((2,)),
        ],
        compiler_params=pltpu.CompilerParams(
            collective_id=0, has_side_effects=True, vmem_limit_bytes=40 * 1024 * 1024
        ),
        name="relevance_chain",
    )(
        lengths,
        *(
            pltpu.with_memory_space_constraint(operand, pltpu.MemorySpace.HBM)
            for operand in (
                hidden_in[0, 0], attn_out[0, 0], queries[0, 0], keys[0, 0], value_weight[0], out_weight[0],
            )
        ),
    )
    return heat[None], relevance[None]


def solution(mesh):
    placed = (
        P("section", ("groups", "dp"), None, "mp"),
        P("section", ("groups", "dp"), None, "mp"),
        P("section", ("groups", "dp"), None, "mp"),
        P("section", ("groups", "dp"), None, "mp"),
        P("section", "mp", None),
        P("section", "mp", "dp"),
        P(("groups", "dp")),
    )
    peers = mesh.shape["dp"]
    aligned = peers == 4 and mesh.shape["section"] == 2
    return jax.shard_map(
        on_device_chain if aligned else on_device,
        mesh=mesh,
        in_specs=placed,
        out_specs=(
            P("section", ("groups", "dp"), None),
            P(("groups", "section"), ("mp", "dp"), None),
        ),
        check_vma=False,
    )
```

```python
import functools
import math

import jax
import jax.numpy as jnp
from jax import lax
from jax.experimental import pallas as pl
from jax.experimental.pallas import tpu as pltpu
from jax.sharding import PartitionSpec as P

DW = 2560
HD = 128
QH = 20
KVH = 4


EPS = 0.25


def from_behind(shard, axis, by):
    peers = lax.axis_size(axis)
    pairs = [(i, i + by) for i in range(peers) if 0 <= i + by < peers]
    return lax.ppermute(shard, axis, pairs)


def stabilize(entries):
    return jnp.where(entries >= 0, entries + EPS, entries - EPS)


def gated(active, compute, operand, out_shape, out_type):
    return lax.cond(active, compute, lambda unused: jnp.zeros(out_shape, out_type), operand)


def on_device(hidden_in, attn_out, queries, keys, value_weight, out_weight, lengths):
    inputs = hidden_in[0, 0]
    branch = attn_out[0, 0]
    query_rows = queries[0, 0]
    key_rows = keys[0, 0]
    value_rows = value_weight[0]
    seq_len = inputs.shape[0]
    half_width = inputs.shape[1]
    group_size = QH // KVH
    local_kv = key_rows.shape[1] // HD
    kv_width = value_rows.shape[1]
    sections = lax.axis_size("section")
    section_pos = lax.axis_index("section")
    core_pos = lax.axis_index("mp")
    out_cols = lax.all_gather(out_weight, "dp", axis=2, tiled=True)[0]
    inputs_f = inputs.astype(jnp.float32)
    branch_f = branch.astype(jnp.float32)
    totals = inputs_f + branch_f
    value_part = jnp.dot(inputs, value_rows, preferred_element_type=jnp.float32)
    value_all = lax.psum(value_part.astype(jnp.bfloat16), "mp").astype(jnp.float32)
    value_mine = lax.dynamic_slice_in_dim(value_all, core_pos * local_kv * HD, local_kv * HD, 1)
    values_bf = lax.optimization_barrier(value_mine.astype(jnp.bfloat16))
    values_f = values_bf.astype(jnp.float32)
    query_heads = query_rows.reshape(seq_len, local_kv, group_size, HD)
    key_heads = key_rows.reshape(seq_len, local_kv, HD)
    scores = jnp.einsum(
        "tgjd,sgd->gjts", query_heads, key_heads, preferred_element_type=jnp.float32
    ) / math.sqrt(HD)
    position = lax.iota(jnp.int32, seq_len)
    allowed = (position[None, :] <= position[:, None]) & (position[None, :] < lengths[0])
    scores = jnp.where(allowed, scores, -1000000000.0)
    row_top = jnp.max(scores, axis=-1, keepdims=True)
    weights = jnp.exp(scores - row_top)
    prob_rows = (weights / jnp.sum(weights, axis=-1, keepdims=True)).astype(jnp.bfloat16)
    mixed_heads = jnp.einsum(
        "gjts,sgd->tgjd",
        prob_rows,
        values_bf.reshape(seq_len, local_kv, HD),
        preferred_element_type=jnp.float32,
    ).reshape(seq_len, local_kv * group_size * HD)
    valid_rows = (position < lengths[0]).astype(jnp.float32)
    current = (totals * valid_rows[:, None]).astype(jnp.bfloat16)
    result = jnp.zeros((seq_len, half_width), jnp.bfloat16)
    sens_kept = jnp.zeros((seq_len, kv_width), jnp.bfloat16)
    for turn_index in range(sections):
        active = section_pos == sections - 1 - turn_index
        sens_total = current.astype(jnp.float32) / stabilize(totals)
        sens_branch = (branch_f * sens_total / stabilize(branch_f)).astype(jnp.bfloat16)
        sens_full = lax.all_gather(sens_branch, "mp", axis=1, tiled=True)

        def through_heads(operand):
            back_mixed = lax.dot_general(
                operand, out_cols, (((1,), (1,)), ((), ())), preferred_element_type=jnp.float32
            )
            sens_mixed = (mixed_heads * back_mixed / stabilize(mixed_heads)).astype(jnp.bfloat16)
            back_values = jnp.einsum(
                "gjts,tgjd->sgd",
                prob_rows,
                sens_mixed.reshape(seq_len, local_kv, group_size, HD),
                preferred_element_type=jnp.float32,
            ).reshape(seq_len, local_kv * HD)
            return (values_f * back_values / stabilize(values_f)).astype(jnp.bfloat16)

        sens_values = gated(
            active, through_heads, sens_full, (seq_len, local_kv * HD), jnp.bfloat16
        )
        sens_all = lax.all_gather(sens_values, "mp", axis=1, tiled=True)

        def through_values(operand):
            back_inputs = lax.dot_general(
                operand, value_rows, (((1,), (1,)), ((), ())), preferred_element_type=jnp.float32
            )
            return (inputs_f * sens_total + inputs_f * back_inputs).astype(jnp.bfloat16)

        outgoing = gated(active, through_values, sens_all, (seq_len, half_width), jnp.bfloat16)
        result = jnp.where(active, outgoing, result)
        sens_kept = jnp.where(active, sens_all, sens_kept)
        if turn_index + 1 < sections:
            arrived = from_behind(outgoing, "section", -1)
            current = jnp.where(section_pos == sections - 2 - turn_index, arrived, current)
    heat_part = jnp.sum(result.astype(jnp.float32), axis=1)
    heat_rows = lax.psum(heat_part, "mp") / DW
    block_rows = half_width // lax.axis_size("dp")
    row_start = lax.axis_index("dp") * block_rows
    value_block = lax.dynamic_slice_in_dim(value_rows, row_start, block_rows, 0).astype(jnp.float32)
    summed = lax.psum_scatter(
        lax.dot_general(
            inputs, sens_kept, (((0,), (0,)), ((), ())), preferred_element_type=jnp.float32
        ).astype(jnp.bfloat16),
        "dp",
        scatter_dimension=0,
        tiled=True,
    ).astype(jnp.float32)
    relevance_rows = value_block * summed
    return (heat_rows[None, None, :], relevance_rows[None])


CHUNKS = 4
RAW = 2
SEGMENTS = (((0, 128),), ((0, 64), (64, 32)), ((0, 64),), ((0, 32),))
TILE = 256
MESH_ID = pl.DeviceIdType.MESH
F32 = jnp.float32
BF16 = jnp.bfloat16
DIRECT = 1
LAST_ORDER = (
    ("branch", 1), ("give", 2), ("give", 3), ("branch", 2), ("part", 0), ("branch", 3),
    ("mix", 0), ("part", 1), ("relay", 2), ("relay", 3), ("head", 0), ("emit", 0), ("mix", 1),
    ("values", 2), ("gather", 2), ("gather", 3), ("linear", 2), ("linear", 3), ("head", 1),
    ("emit", 1), ("join", 2), ("join", 3), ("emit", 2), ("emit", 3), ("hidden", 3),
)
NEXT_ORDER = (
    ("relay", 0), ("relay", 1), ("relay", 2), ("relay", 3), ("values", 0), ("gather", 0),
    ("hidden", 0), ("gather", 1), ("take", 0), ("gather", 2), ("gather", 3), ("linear", 0),
    ("join", 0), ("emit", 0), ("linear", 1), ("linear", 2), ("linear", 3), ("join", 1),
    ("join", 2), ("join", 3), ("emit", 1), ("emit", 2), ("emit", 3),
)


def tiles_of(heads, step):
    return sum(-(-heads // (HD // lanes)) for _, lanes in SEGMENTS[step])


def nt_dot(left, right):
    return lax.dot_general(left, right, (((1,), (1,)), ((), ())), preferred_element_type=F32)


def tn_dot(left, right):
    return lax.dot_general(left, right, (((0,), (0,)), ((), ())), preferred_element_type=F32)


def chain_kernel(
    peers, sections, len_ref, hid_in, att_in, que_in, key_in, vw_in, ow_in,
    heat_out, rel_out, hid_ref, att_ref, que_ref, key_ref, vw_ref, ow_ref, load_sem,
    through_ref, keep_ref, ratio_ref, inc_ref, out_ref, prob_ref, pack_ref, gval_ref, val_ref, bv_ref,
    vsend, vrecv, hidt_ref, hida_ref, sv_ref, heats, sm_ref, bvsend, bvbuf,
    asend, abuf, psend, pbuf, below_ref, dsend,
    done, a_recv, p_recv, s_recv, f_recv, x_recv, one_recv, k_recv, b_recv,
    heat_ref, rel_ref, out_sem,
):
    dp = lax.axis_index("dp")
    sec = lax.axis_index("section")
    core = lax.axis_index("mp")
    other = 1 - core
    seq_len, half = hid_ref.shape
    rows_n = seq_len // CHUNKS
    width = ow_ref.shape[1]
    blocks = peers // 2
    local_kv = key_ref.shape[1] // HD
    group = QH // KVH
    heads_n = local_kv * group
    kv_half = local_kv * HD
    block_rows = half // peers
    is_last = sec == sections - 1
    gets = core == dp // blocks
    hops = [(hop, lax.rem(dp + hop, peers)) for hop in range(1, peers)]

    loads = [
        pltpu.make_async_copy(source, target, load_sem.at[at])
        for at, (source, target) in enumerate((
            (hid_in, hid_ref), (att_in, att_ref), (vw_in, vw_ref),
            (que_in, que_ref), (key_in, key_ref), (ow_in, ow_ref),
        ))
    ]
    for load in loads:
        load.start()

    barrier = pltpu.get_barrier_semaphore()
    for hop, to in hops:
        for target in range(2):
            pl.semaphore_signal(
                barrier, inc=1, device_id={"dp": to, "mp": target}, device_id_type=MESH_ID
            )
    pl.semaphore_signal(barrier, inc=1, device_id={"mp": other}, device_id_type=MESH_ID)

    @pl.when(sec > 0)
    def _():
        pl.semaphore_signal(
            barrier, inc=1, device_id={"section": sec - 1}, device_id_type=MESH_ID
        )

    @pl.when(sec < sections - 1)
    def _():
        for at in range(peers):
            pl.semaphore_signal(
                barrier, inc=1, device_id={"dp": at, "section": sec + 1}, device_id_type=MESH_ID
            )

    def barrier_wait():
        greeted = 2 * (peers - 1) + 1

        @pl.when(is_last)
        def _():
            pl.semaphore_wait(barrier, greeted + peers)

        @pl.when(jnp.logical_not(is_last))
        def _():
            pl.semaphore_wait(barrier, greeted + 1)

    def remote(source, target, send, recv, device):
        return pltpu.make_async_remote_copy(
            src_ref=source, dst_ref=target, send_sem=send, recv_sem=recv,
            device_id=device, device_id_type=MESH_ID,
        )

    def rows_of(step):
        return pl.ds((CHUNKS - 1 - step) * rows_n, rows_n)

    def branch_copy(step, block):
        return remote(
            asend.at[step, block], abuf.at[step, dp],
            done.at[0], a_recv.at[step, dp], {"dp": core * blocks + block},
        )

    def direct_copy(step, block):
        return remote(
            dsend.at[step - DIRECT, block], abuf.at[step, dp],
            done.at[1], a_recv.at[step, dp],
            {"dp": core * blocks + block, "section": sec - 1},
        )

    def through_copy(step, target):
        rows = rows_of(step)
        return remote(
            through_ref.at[rows], below_ref.at[rows],
            done.at[0], one_recv.at[3], {"section": target},
        )

    def branch_forward(step, source):
        view = abuf.at[step, source]
        return remote(
            view, view, done.at[0], a_recv.at[step, source], {"mp": other}
        )

    rounds = peers.bit_length() - 1

    def slot_of(turn, target):
        return peers - (peers >> turn) + target // (2 << turn)

    def part_target(turn, at):
        bit = 1 << turn
        return lax.rem(dp, bit) + bit * (2 * at + 1 - lax.rem(dp // bit, 2))

    def part_copy(step, turn, at):
        bit = 1 << turn
        slot = peers - (peers >> turn) + at
        return remote(
            psend.at[step, part_target(turn, at)], pbuf.at[step, slot],
            done.at[0], p_recv.at[step, slot],
            {"dp": dp + bit - 2 * bit * lax.rem(dp // bit, 2)},
        )

    def part_take(step, turn, target):
        slot = slot_of(turn, target)
        view = pbuf.at[step, slot]
        remote(
            view, view, done.at[0], p_recv.at[step, slot], {"mp": other}
        ).wait_recv()
        return pbuf[step, slot].astype(F32)

    def mix_stage(step):
        for turn in range(1, rounds):
            for at in range(peers >> (turn + 1)):
                target = part_target(turn, at)
                running = psend[step, target].astype(F32)
                for before in range(turn):
                    running = running + part_take(step, before, target)
                psend[step, target] = running.astype(BF16)
                part_copy(step, turn, at).start()

    def value_rows(step, source):
        return gval_ref.at[source, pl.ds(0, (CHUNKS - step) * rows_n)]

    def prob_tiles(step, source):
        first = sum(tiles_of(heads_n, before) for before in range(step))
        return pack_ref.at[source, pl.ds(first, tiles_of(heads_n, step))]

    def relays(source, through):
        return jnp.logical_or(
            jnp.logical_and(source == 0, through == peers - 2),
            jnp.logical_and(source == peers - 1, through == 1),
        )

    def lane(source, to):
        return relays(source, to).astype(jnp.int32)

    def gather_value(first, to):
        view = value_rows(first, dp)
        return remote(
            view, view, done.at[0], k_recv.at[CHUNKS, lane(dp, to)], {"dp": to}
        )

    def gather_probs(step, to):
        view = prob_tiles(step, dp)
        return remote(
            view, view, done.at[0], k_recv.at[step, lane(dp, to)], {"dp": to}
        )

    def sum_copy(step, hop, to):
        return remote(
            bvsend.at[step, hop], bvbuf.at[step, dp],
            done.at[0], b_recv.at[step], {"dp": to},
        )

    def sens_copy(step, owner):
        view = sv_ref.at[dp, owner, rows_of(step)]
        return remote(view, view, done.at[0], s_recv.at[step], {"mp": other})

    def final_copy(step, hop, to, side):
        view = sv_ref.at[dp, core, rows_of(step)]
        return remote(
            view, view, done.at[0], f_recv.at[step // (CHUNKS - 1)],
            {"dp": to, "mp": core if side == 0 else other},
        )

    early = pl.ds(rows_n, seq_len - rows_n)

    def final_wait(at, owners, rows):
        view = sv_ref.at[pl.ds(0, peers - 1), owners, rows]
        remote(view, view, done.at[0], f_recv.at[at], {"mp": other}).wait_recv()

    def final_forward(source, owner, rows):
        view = sv_ref.at[source, owner, rows]
        return remote(view, view, done.at[0], f_recv.at[2], {"mp": other})

    def final_out(step):
        for hop, to in hops:
            final_copy(step, hop, to, 0).start()
            if step == CHUNKS - 1:
                @pl.when(jnp.logical_not(is_last))
                def _():
                    final_copy(step, hop, to, 1).start()

    def section_copy(step, target):
        return remote(
            out_ref.at[rows_of(step)], inc_ref.at[rows_of(step)],
            done.at[0], x_recv.at[step], {"section": target},
        )

    def hidden_copy(hop, to):
        return remote(
            hidt_ref.at[pl.ds(pl.multiple_of(to * block_rows, 16), block_rows)], hida_ref.at[dp],
            done.at[0], one_recv.at[2], {"dp": to},
        )

    def hidden_wait():
        view = hida_ref.at[pl.ds(0, peers - 1)]
        remote(view, view, done.at[0], one_recv.at[2], {"mp": other}).wait_recv()

    def value_copy(slot):
        return remote(
            vsend.at[slot], vrecv, done.at[0], one_recv.at[0], {"mp": other}
        )

    def heat_copy(slot):
        return remote(
            heats.at[slot], heats.at[slot], done.at[0], one_recv.at[1], {"mp": other}
        )

    def branch_stage(step):
        rows = rows_of(step)
        sens = (inc_ref[rows, :].astype(F32) * through_ref[rows, :]).astype(BF16)
        for block in range(blocks):
            to = core * blocks + block
            piece = sens[:, block * width:(block + 1) * width]
            asend[step, block] = piece

            @pl.when(to == dp)
            def _():
                abuf[step, dp] = piece
                branch_forward(step, dp).start()

            @pl.when(to != dp)
            def _():
                branch_copy(step, block).start()

    def branch_wait(step, direct):
        @pl.when(gets)
        def _():
            for hop in range(0 if direct else 1, peers):
                source = lax.rem(dp + hop, peers)
                branch_forward(step, source).wait_recv()
                branch_forward(step, source).start()

        @pl.when(jnp.logical_not(gets))
        def _():
            for source in range(peers):
                branch_forward(step, source).wait_recv()

        return abuf[step].reshape(peers * rows_n, width)

    def part_stage(step):
        stacked = branch_wait(step, False)

        def tile(at, unused):
            start = pl.multiple_of(at * TILE, TILE)
            part = nt_dot(stacked, ow_ref[pl.ds(start, TILE), :]).astype(BF16)
            psend[step, :, :, pl.ds(start, TILE)] = part.reshape(peers, rows_n, TILE)
            return unused

        lax.fori_loop(0, half // TILE, tile, 0, unroll=True)
        for at in range(peers // 2):
            part_copy(step, 0, at).start()

    def add_values(seq, rows, mixed):
        for kv in range(local_kv):
            heads = range(kv * group, (kv + 1) * group)
            left = jnp.concatenate([prob_ref[seq, h, rows, :] for h in heads], axis=0)
            right = jnp.concatenate([mixed[:, h * HD:(h + 1) * HD] for h in heads], axis=0)
            columns = pl.ds(kv * HD, HD)
            bv_ref[seq, :, columns] = bv_ref[seq, :, columns] + tn_dot(left, right)

    def head_stage(step):
        rows = rows_of(step)
        back = psend[step, dp].astype(F32)
        for turn in range(rounds):
            back = back + part_take(step, turn, dp)
        add_values(dp, rows, (ratio_ref[dp, rows, :] * back).astype(BF16))
        settle(step, bv_ref[dp, rows, :])

    def linear_stage(step, direct=False):
        rows = rows_of(step)
        stacked = branch_wait(step, direct)
        for at in range(half // TILE):
            columns = pl.ds(at * TILE, TILE)
            part = nt_dot(stacked, ow_ref[columns, :])
            ratio = ratio_ref[:, rows, columns].reshape(peers * rows_n, TILE)
            sm_ref[:, columns] = (ratio * part).astype(BF16)
        for seq in range(peers):
            add_values(seq, rows, sm_ref[seq * rows_n:(seq + 1) * rows_n, :])
        for hop, to in hops:
            bvsend[step, hop] = bv_ref[to, rows, :].astype(BF16)
            sum_copy(step, hop, to).start()

    def join_stage(step):
        total = bv_ref[dp, rows_of(step), :]
        view = bvbuf.at[step, pl.ds(0, peers - 1)]
        remote(view, view, done.at[0], b_recv.at[step], {"mp": other}).wait_recv()
        for hop, source in hops:
            total = total + bvbuf[step, source].astype(F32)
        settle(step, total)

    def settle(step, back_values):
        rows = rows_of(step)
        sv_ref[dp, core, rows, :] = (val_ref[rows, :] * back_values).astype(BF16)
        sens_copy(step, core).start()

        @pl.when(jnp.logical_not(is_last))
        def _():
            final_out(step)

    def emit_stage(step):
        rows = rows_of(step)
        sens_copy(step, other).wait_recv()
        sens = jnp.concatenate([sv_ref[dp, 0, rows, :], sv_ref[dp, 1, rows, :]], axis=1)
        sums = jnp.zeros((rows_n, HD), F32)
        for at in range(half // TILE):
            columns = pl.ds(at * TILE, TILE)
            back_in = nt_dot(sens, vw_ref[columns, :])
            out = (
                inc_ref[rows, columns].astype(F32) * keep_ref[rows, columns]
                + hid_ref[rows, columns].astype(F32) * back_in
            ).astype(BF16)
            out_ref[rows, columns] = out
            wide = out.astype(F32)
            for lane in range(TILE // HD):
                sums = sums + wide[:, lane * HD:(lane + 1) * HD]
        heats[core, rows, :] = sums

        @pl.when(sec > 0)
        def _():
            if step >= DIRECT:
                if step == DIRECT:
                    view = below_ref.at[pl.ds(0, (CHUNKS - DIRECT) * rows_n)]
                    remote(view, view, done.at[0], one_recv.at[3], {"mp": other}).wait_recv()
                below = (out_ref[rows, :].astype(F32) * below_ref[rows, :]).astype(BF16)
                for block in range(blocks):
                    dsend[step - DIRECT, block] = below[:, block * width:(block + 1) * width]
                    direct_copy(step, block).start()
            else:
                section_copy(step, sec - 1).start()

    lane_at = lax.broadcasted_iota(jnp.int32, (rows_n, HD), 1)

    def shifted(tile, start, count, to):
        inside = (lane_at >= start) & (lane_at < start + count)
        kept = jnp.where(inside, tile, 0.0)
        return kept if start == to else pltpu.roll(kept, (to - start) % HD, 1)

    def pack_stage(step):
        at = sum(tiles_of(heads_n, before) for before in range(step))
        for start, lanes in SEGMENTS[step]:
            per = HD // lanes
            for first in range(0, heads_n, per):
                tile = None
                for h in range(first, min(first + per, heads_n)):
                    piece = shifted(
                        prob_ref[dp, h, rows_of(step), :].astype(F32), start, lanes, (h - first) * lanes
                    )
                    tile = piece if tile is None else tile + piece
                pack_ref[dp, at] = tile.astype(BF16)
                at += 1

    def value_wait(first):
        gather_wait(
            CHUNKS, lambda count: gval_ref.at[pl.ds(0, count), pl.ds(0, (CHUNKS - first) * rows_n)]
        )

    def far(to):
        return jnp.logical_and(dp + to == peers - 1, jnp.logical_or(dp == 0, to == 0))

    def relay_copy(step, view, source):
        return remote(
            view, view, done.at[0], k_recv.at[step, 0], {"dp": peers - 1 - source}
        )

    def gather_wait(step, views):
        def wait(view):
            remote(view, view, done.at[0], k_recv.at[step, 0], {"mp": other}).wait_recv()

        inner = jnp.logical_and(dp > 0, dp < peers - 1)

        @pl.when(inner)
        def _():
            wait(views(peers - 2))

        @pl.when(jnp.logical_not(inner))
        def _():
            wait(views(peers - 1))

    def relay_stage(step, first=0):
        for end, through in ((0, peers - 2), (peers - 1, 1)):
            @pl.when(dp == through)
            def _():
                views = [(step, prob_tiles(step, end))]
                if step == first:
                    views.insert(0, (CHUNKS, value_rows(first, end)))
                for at, view in views:
                    remote(view, view, done.at[0], k_recv.at[at, 1], {"mp": other}).wait_recv()
                    relay_copy(at, view, end).start()

    def gather_stage(step):
        rows = rows_of(step)
        depth = (CHUNKS - step) * rows_n
        first_tile = sum(tiles_of(heads_n, before) for before in range(step))
        tiles = pl.ds(first_tile, tiles_of(heads_n, step))
        gather_wait(step, lambda count: pack_ref.at[pl.ds(0, count), tiles])
        for hop, source in hops:
            for h in range(heads_n):
                at = first_tile
                whole = None
                for start, lanes in SEGMENTS[step]:
                    per = HD // lanes
                    piece = shifted(
                        pack_ref[source, at + h // per].astype(F32), h % per * lanes, lanes, start
                    )
                    whole = piece if whole is None else whole + piece
                    at += -(-heads_n // per)
                prob_ref[source, h, rows, :] = whole.astype(BF16)
            for kv in range(local_kv):
                heads = range(kv * group, (kv + 1) * group)
                left = jnp.concatenate(
                    [prob_ref[source, h, rows, pl.ds(0, depth)] for h in heads], axis=0
                )
                mixed = jnp.dot(
                    left, gval_ref[source, pl.ds(0, depth), pl.ds(kv * HD, HD)],
                    preferred_element_type=F32,
                )
                ratio = mixed / stabilize(mixed)
                for at, h in enumerate(heads):
                    ratio_ref[source, rows, h * HD:(h + 1) * HD] = (
                        ratio[at * rows_n:(at + 1) * rows_n, :]
                    )

    length = len_ref[0]
    loads[0].wait()
    loads[1].wait()
    for step in range(CHUNKS):
        rows = rows_of(step)
        hid = hid_ref[rows, :].astype(F32)
        att = att_ref[rows, :].astype(F32)
        totals = hid + att
        inverse = 1.0 / stabilize(totals)
        keep_ref[rows, :] = hid * inverse
        through_ref[rows, :] = att * inverse / stabilize(att)

        @pl.when(is_last)
        def _():
            token = (CHUNKS - 1 - step) * rows_n + lax.broadcasted_iota(
                jnp.int32, (rows_n, half), 0
            )
            inc_ref[rows, :] = jnp.where(token < length, totals, 0.0).astype(BF16)

    loads[2].wait()
    hid_all = hid_ref[...]
    for slot in range(2):
        part = jnp.dot(
            hid_all, vw_ref[:, slot * kv_half:(slot + 1) * kv_half], preferred_element_type=F32
        )
        vsend[slot] = part.astype(BF16)

        @pl.when(core == slot)
        def _():
            val_ref[...] = part

    for load in loads[3:]:
        load.wait()
    bv_ref[...] = jnp.zeros_like(bv_ref)
    barrier_wait()
    value_copy(other).start()

    @pl.when(is_last)
    def _():
        branch_stage(0)

    @pl.when(jnp.logical_not(is_last))
    def _():
        for step in range(DIRECT, CHUNKS):
            through_copy(step, sec + 1).start()

    query_at = lax.broadcasted_iota(jnp.int32, (seq_len, seq_len), 0)
    key_at = lax.broadcasted_iota(jnp.int32, (seq_len, seq_len), 1)
    allowed = (key_at <= query_at) & (key_at < length)
    for h in range(heads_n):
        kv = h // group
        scores = nt_dot(
            que_ref[:, h * HD:(h + 1) * HD], key_ref[:, kv * HD:(kv + 1) * HD]
        ) / math.sqrt(HD)
        scores = jnp.where(allowed, scores, -1000000000.0)
        weights = jnp.exp(scores - jnp.max(scores, axis=1, keepdims=True))
        prob_ref[dp, h] = (weights / jnp.sum(weights, axis=1, keepdims=True)).astype(BF16)

    value_copy(other).wait_recv()
    values = (val_ref[...] + vrecv[...].astype(F32)).astype(BF16)
    gval_ref[dp] = values

    @pl.when(is_last)
    def _():
        for step in range(RAW, CHUNKS):
            pack_stage(step)

    @pl.when(jnp.logical_not(is_last))
    def _():
        for step in range(CHUNKS):
            pack_stage(step)
        for hop, to in (hops[1], hops[0], hops[2]):
            @pl.when(jnp.logical_not(far(to)))
            def _():
                gather_value(0, to).start()
                for step in range(CHUNKS):
                    gather_probs(step, to).start()

    wide_values = values.astype(F32)
    val_ref[...] = wide_values / stabilize(wide_values)
    for h in range(heads_n):
        kv = h // group
        mixed = jnp.dot(
            prob_ref[dp, h], values[:, kv * HD:(kv + 1) * HD], preferred_element_type=F32
        )
        ratio_ref[dp, :, h * HD:(h + 1) * HD] = mixed / stabilize(mixed)

    for at in range(half // HD):
        flipped = hid_ref[:, at * HD:(at + 1) * HD].astype(F32).T
        hidt_ref[pl.ds(at * HD, HD), :] = flipped.astype(BF16)
    hida_ref[dp] = hidt_ref[pl.ds(pl.multiple_of(dp * block_rows, 16), block_rows), :]

    def branch_next(step):
        section_copy(step, sec + 1).wait_recv()
        branch_stage(step)

    def hidden_stage(step):
        if step == CHUNKS - 1:
            for at in range(DIRECT, CHUNKS):
                for block in range(blocks):
                    direct_copy(at, block).wait_send()
                section_copy(at, sec - 1).start()
        for hop, to in hops:
            hidden_copy(hop, to).start()

    def emit_next(step):
        if step >= DIRECT:
            section_copy(step, sec + 1).wait_recv()
        emit_stage(step)

    def give_stage(step):
        for hop, to in (hops[1], hops[0], hops[2]):
            @pl.when(jnp.logical_not(far(to)))
            def _():
                if step == RAW:
                    gather_value(RAW, to).start()
                gather_probs(step, to).start()

    stages = {
        "give": give_stage, "emit": emit_stage,
        "values": value_wait, "hidden": hidden_stage, "branch": branch_stage, "relay": relay_stage,
        "gather": gather_stage, "part": part_stage, "mix": mix_stage, "head": head_stage,
        "take": branch_next, "linear": linear_stage, "join": join_stage,
    }

    @pl.when(is_last)
    def _():
        for stage, step in LAST_ORDER:
            if stage == "relay":
                stages[stage] = functools.partial(relay_stage, first=RAW)
            stages[stage](step)
        for step in range(CHUNKS):
            final_out(step)

    @pl.when(jnp.logical_not(is_last))
    def _():
        stages["emit"] = emit_next
        stages["relay"] = relay_stage
        for stage, step in NEXT_ORDER:
            if stage == "linear":
                stages[stage] = functools.partial(linear_stage, direct=step >= DIRECT)
            stages[stage](step)

    heat_copy(core).start()
    final_wait(0, 0, early)

    @pl.when(is_last)
    def _():
        final_wait(1, 0, rows_of(CHUNKS - 1))
        for hop, source in hops:
            final_forward(source, core, pl.ds(0, seq_len)).start()

    @pl.when(jnp.logical_not(is_last))
    def _():
        for hop, source in hops:
            final_forward(source, core, early).start()

    hidden_wait()

    @pl.when(is_last)
    def _():
        final_wait(2, 0, pl.ds(0, seq_len))

    @pl.when(jnp.logical_not(is_last))
    def _():
        final_wait(2, 0, early)
        final_wait(1, pl.ds(0, 2), rows_of(CHUNKS - 1))

    block_at = pl.ds(pl.multiple_of(dp * block_rows, 16), block_rows)
    total = None
    for hop in range(peers):
        source = lax.rem(dp + hop, peers)
        sens = jnp.concatenate([sv_ref[source, 0], sv_ref[source, 1]], axis=1)
        term = jnp.dot(hida_ref[source], sens, preferred_element_type=F32)
        total = term if total is None else total + term
    rel_ref[...] = vw_ref[block_at, :].astype(F32) * total
    stores = [
        pltpu.make_async_copy(source, target, out_sem.at[at])
        for at, (source, target) in enumerate(((heat_ref, heat_out), (rel_ref, rel_out)))
    ]
    stores[1].start()
    heat_copy(other).wait_recv()
    heat_ref[...] = jnp.sum((heats[0] + heats[1]).T, axis=0, keepdims=True) / DW
    stores[0].start()
    for hop, to in hops:
        for step in range(CHUNKS):
            final_copy(step, hop, to, 0).wait_send()

        @pl.when(is_last)
        def _():
            final_forward(to, core, pl.ds(0, seq_len)).wait_send()

        @pl.when(jnp.logical_not(is_last))
        def _():
            final_copy(CHUNKS - 1, hop, to, 1).wait_send()
            final_forward(to, core, early).wait_send()

    for step in range(CHUNKS):
        for block in range(blocks):
            mine = core * blocks + block != dp

            @pl.when(mine if step < DIRECT else jnp.logical_and(mine, is_last))
            def _():
                branch_copy(step, block).wait_send()

        @pl.when(gets)
        def _():
            for source in range(peers):
                branch_forward(step, source).wait_send()

        sens_copy(step, core).wait_send()

        @pl.when(sec > 0)
        def _():
            section_copy(step, sec - 1).wait_send()

    def sent(first):
        for hop, to in hops:
            @pl.when(jnp.logical_not(far(to)))
            def _():
                gather_value(first, to).wait_send()
                for step in range(first, CHUNKS):
                    gather_probs(step, to).wait_send()

            @pl.when(relays(to, dp))
            def _():
                relay_copy(CHUNKS, value_rows(first, to), to).wait_send()
                for step in range(first, CHUNKS):
                    relay_copy(step, prob_tiles(step, to), to).wait_send()
            for step in range(first, CHUNKS):
                sum_copy(step, hop, to).wait_send()

    @pl.when(is_last)
    def _():
        sent(RAW)
        for step in range(RAW):
            for turn in range(rounds):
                for at in range(peers >> (turn + 1)):
                    part_copy(step, turn, at).wait_send()

    @pl.when(jnp.logical_not(is_last))
    def _():
        sent(0)
        for step in range(DIRECT, CHUNKS):
            through_copy(step, sec + 1).wait_send()

    value_copy(other).wait_send()
    heat_copy(core).wait_send()
    for hop, to in hops:
        hidden_copy(hop, to).wait_send()
    for store in stores:
        store.wait()


def on_device_chain(hidden_in, attn_out, queries, keys, value_weight, out_weight, lengths):
    peers = lax.axis_size("dp")
    sections = lax.axis_size("section")
    seq_len, half = hidden_in.shape[2:]
    kv_half = keys.shape[3]
    kv_width = value_weight.shape[2]
    width = out_weight.shape[2]
    heads = half // HD
    rows_n = seq_len // CHUNKS
    packed = sum(tiles_of(heads, step) for step in range(CHUNKS))
    vmem = pltpu.VMEM
    dma = pltpu.SemaphoreType.DMA
    heat, relevance = pl.pallas_call(
        functools.partial(chain_kernel, peers, sections),
        out_shape=(
            jax.ShapeDtypeStruct((1, seq_len), F32),
            jax.ShapeDtypeStruct((half // peers, kv_width), F32),
        ),
        in_specs=[pl.BlockSpec(memory_space=pltpu.SMEM)] + [pl.BlockSpec(memory_space=pl.ANY)] * 6,
        out_specs=(pl.BlockSpec(memory_space=pl.ANY), pl.BlockSpec(memory_space=pl.ANY)),
        scratch_shapes=[
            vmem((seq_len, half), BF16),
            vmem((seq_len, half), BF16),
            vmem((seq_len, half), BF16),
            vmem((seq_len, kv_half), BF16),
            vmem((half, kv_width), BF16),
            vmem((half, width), BF16),
            dma((6,)),
            vmem((seq_len, half), F32),
            vmem((seq_len, half), F32),
            vmem((peers, seq_len, half), F32),
            vmem((seq_len, half), BF16),
            vmem((seq_len, half), BF16),
            vmem((peers, heads, seq_len, seq_len), BF16),
            vmem((peers, packed, rows_n, HD), BF16),
            vmem((peers, seq_len, kv_half), BF16),
            vmem((seq_len, kv_half), F32),
            vmem((peers, seq_len, kv_half), F32),
            vmem((2, seq_len, kv_half), BF16),
            vmem((seq_len, kv_half), BF16),
            vmem((half, seq_len), BF16),
            vmem((peers, half // peers, seq_len), BF16),
            vmem((peers, 2, seq_len, kv_half), BF16),
            vmem((2, seq_len, HD), F32),
            vmem((peers * rows_n, half), BF16),
            vmem((CHUNKS, peers, rows_n, kv_half), BF16),
            vmem((CHUNKS, peers, rows_n, kv_half), BF16),
            vmem((CHUNKS, peers // 2, rows_n, width), BF16),
            vmem((CHUNKS, peers, rows_n, width), BF16),
            vmem((RAW, peers, rows_n, half), BF16),
            vmem((RAW, peers - 1, rows_n, half), BF16),
            vmem((seq_len, half), F32),
            vmem((CHUNKS - DIRECT, peers // 2, rows_n, width), BF16),
            dma((2,)),
            dma((CHUNKS, peers)),
            dma((RAW, peers - 1)),
            dma((CHUNKS,)),
            dma((3,)),
            dma((CHUNKS,)),
            dma((4,)),
            dma((CHUNKS + 1, 2)),
            dma((CHUNKS,)),
            vmem((1, seq_len), F32),
            vmem((half // peers, kv_width), F32),
            dma((2,)),
        ],
        compiler_params=pltpu.CompilerParams(
            collective_id=0, has_side_effects=True, vmem_limit_bytes=40 * 1024 * 1024
        ),
        name="relevance_chain",
    )(
        lengths,
        *(
            pltpu.with_memory_space_constraint(operand, pltpu.MemorySpace.HBM)
            for operand in (
                hidden_in[0, 0], attn_out[0, 0], queries[0, 0], keys[0, 0], value_weight[0], out_weight[0],
            )
        ),
    )
    return heat[None], relevance[None]


def solution(mesh):
    placed = (
        P("section", ("groups", "dp"), None, "mp"),
        P("section", ("groups", "dp"), None, "mp"),
        P("section", ("groups", "dp"), None, "mp"),
        P("section", ("groups", "dp"), None, "mp"),
        P("section", "mp", None),
        P("section", "mp", "dp"),
        P(("groups", "dp")),
    )
    peers = mesh.shape["dp"]
    aligned = peers == 4 and mesh.shape["section"] == 2
    return jax.shard_map(
        on_device_chain if aligned else on_device,
        mesh=mesh,
        in_specs=placed,
        out_specs=(
            P("section", ("groups", "dp"), None),
            P(("groups", "section"), ("mp", "dp"), None),
        ),
        check_vma=False,
    )
```

```python
import functools
import math

import jax
import jax.numpy as jnp
from jax import lax
from jax.experimental import pallas as pl
from jax.experimental.pallas import tpu as pltpu
from jax.sharding import PartitionSpec as P

DW = 2560
HD = 128
QH = 20
KVH = 4


EPS = 0.25


def from_behind(shard, axis, by):
    peers = lax.axis_size(axis)
    pairs = [(i, i + by) for i in range(peers) if 0 <= i + by < peers]
    return lax.ppermute(shard, axis, pairs)


def stabilize(entries):
    return jnp.where(entries >= 0, entries + EPS, entries - EPS)


def gated(active, compute, operand, out_shape, out_type):
    return lax.cond(active, compute, lambda unused: jnp.zeros(out_shape, out_type), operand)


def on_device(hidden_in, attn_out, queries, keys, value_weight, out_weight, lengths):
    inputs = hidden_in[0, 0]
    branch = attn_out[0, 0]
    query_rows = queries[0, 0]
    key_rows = keys[0, 0]
    value_rows = value_weight[0]
    seq_len = inputs.shape[0]
    half_width = inputs.shape[1]
    group_size = QH // KVH
    local_kv = key_rows.shape[1] // HD
    kv_width = value_rows.shape[1]
    sections = lax.axis_size("section")
    section_pos = lax.axis_index("section")
    core_pos = lax.axis_index("mp")
    out_cols = lax.all_gather(out_weight, "dp", axis=2, tiled=True)[0]
    inputs_f = inputs.astype(jnp.float32)
    branch_f = branch.astype(jnp.float32)
    totals = inputs_f + branch_f
    value_part = jnp.dot(inputs, value_rows, preferred_element_type=jnp.float32)
    value_all = lax.psum(value_part.astype(jnp.bfloat16), "mp").astype(jnp.float32)
    value_mine = lax.dynamic_slice_in_dim(value_all, core_pos * local_kv * HD, local_kv * HD, 1)
    values_bf = lax.optimization_barrier(value_mine.astype(jnp.bfloat16))
    values_f = values_bf.astype(jnp.float32)
    query_heads = query_rows.reshape(seq_len, local_kv, group_size, HD)
    key_heads = key_rows.reshape(seq_len, local_kv, HD)
    scores = jnp.einsum(
        "tgjd,sgd->gjts", query_heads, key_heads, preferred_element_type=jnp.float32
    ) / math.sqrt(HD)
    position = lax.iota(jnp.int32, seq_len)
    allowed = (position[None, :] <= position[:, None]) & (position[None, :] < lengths[0])
    scores = jnp.where(allowed, scores, -1000000000.0)
    row_top = jnp.max(scores, axis=-1, keepdims=True)
    weights = jnp.exp(scores - row_top)
    prob_rows = (weights / jnp.sum(weights, axis=-1, keepdims=True)).astype(jnp.bfloat16)
    mixed_heads = jnp.einsum(
        "gjts,sgd->tgjd",
        prob_rows,
        values_bf.reshape(seq_len, local_kv, HD),
        preferred_element_type=jnp.float32,
    ).reshape(seq_len, local_kv * group_size * HD)
    valid_rows = (position < lengths[0]).astype(jnp.float32)
    current = (totals * valid_rows[:, None]).astype(jnp.bfloat16)
    result = jnp.zeros((seq_len, half_width), jnp.bfloat16)
    sens_kept = jnp.zeros((seq_len, kv_width), jnp.bfloat16)
    for turn_index in range(sections):
        active = section_pos == sections - 1 - turn_index
        sens_total = current.astype(jnp.float32) / stabilize(totals)
        sens_branch = (branch_f * sens_total / stabilize(branch_f)).astype(jnp.bfloat16)
        sens_full = lax.all_gather(sens_branch, "mp", axis=1, tiled=True)

        def through_heads(operand):
            back_mixed = lax.dot_general(
                operand, out_cols, (((1,), (1,)), ((), ())), preferred_element_type=jnp.float32
            )
            sens_mixed = (mixed_heads * back_mixed / stabilize(mixed_heads)).astype(jnp.bfloat16)
            back_values = jnp.einsum(
                "gjts,tgjd->sgd",
                prob_rows,
                sens_mixed.reshape(seq_len, local_kv, group_size, HD),
                preferred_element_type=jnp.float32,
            ).reshape(seq_len, local_kv * HD)
            return (values_f * back_values / stabilize(values_f)).astype(jnp.bfloat16)

        sens_values = gated(
            active, through_heads, sens_full, (seq_len, local_kv * HD), jnp.bfloat16
        )
        sens_all = lax.all_gather(sens_values, "mp", axis=1, tiled=True)

        def through_values(operand):
            back_inputs = lax.dot_general(
                operand, value_rows, (((1,), (1,)), ((), ())), preferred_element_type=jnp.float32
            )
            return (inputs_f * sens_total + inputs_f * back_inputs).astype(jnp.bfloat16)

        outgoing = gated(active, through_values, sens_all, (seq_len, half_width), jnp.bfloat16)
        result = jnp.where(active, outgoing, result)
        sens_kept = jnp.where(active, sens_all, sens_kept)
        if turn_index + 1 < sections:
            arrived = from_behind(outgoing, "section", -1)
            current = jnp.where(section_pos == sections - 2 - turn_index, arrived, current)
    heat_part = jnp.sum(result.astype(jnp.float32), axis=1)
    heat_rows = lax.psum(heat_part, "mp") / DW
    block_rows = half_width // lax.axis_size("dp")
    row_start = lax.axis_index("dp") * block_rows
    value_block = lax.dynamic_slice_in_dim(value_rows, row_start, block_rows, 0).astype(jnp.float32)
    summed = lax.psum_scatter(
        lax.dot_general(
            inputs, sens_kept, (((0,), (0,)), ((), ())), preferred_element_type=jnp.float32
        ).astype(jnp.bfloat16),
        "dp",
        scatter_dimension=0,
        tiled=True,
    ).astype(jnp.float32)
    relevance_rows = value_block * summed
    return (heat_rows[None, None, :], relevance_rows[None])


CHUNKS = 4
RAW = 2
SEGMENTS = (((0, 128),), ((0, 64), (64, 32)), ((0, 64),), ((0, 32),))
TILE = 256
MESH_ID = pl.DeviceIdType.MESH
F32 = jnp.float32
BF16 = jnp.bfloat16
DIRECT = 1
LAST_ORDER = (
    ("branch", 1), ("give", 2), ("give", 3), ("branch", 2), ("part", 0), ("branch", 3),
    ("mix", 0), ("part", 1), ("relay", 2), ("relay", 3), ("head", 0), ("emit", 0), ("mix", 1),
    ("values", 2), ("gather", 2), ("gather", 3), ("linear", 2), ("linear", 3), ("head", 1),
    ("emit", 1), ("join", 2), ("join", 3), ("emit", 2), ("emit", 3), ("hidden", 3),
)
NEXT_ORDER = (
    ("relay", 0), ("relay", 1), ("relay", 2), ("relay", 3), ("values", 0), ("gather", 0),
    ("hidden", 0), ("gather", 1), ("take", 0), ("gather", 2), ("gather", 3), ("linear", 0),
    ("linear", 1), ("join", 0), ("linear", 2), ("join", 1), ("linear", 3), ("emit", 0),
    ("join", 2), ("join", 3), ("emit", 1), ("emit", 2), ("emit", 3),
)


def tiles_of(heads, step):
    return sum(-(-heads // (HD // lanes)) for _, lanes in SEGMENTS[step])


def nt_dot(left, right):
    return lax.dot_general(left, right, (((1,), (1,)), ((), ())), preferred_element_type=F32)


def tn_dot(left, right):
    return lax.dot_general(left, right, (((0,), (0,)), ((), ())), preferred_element_type=F32)


def chain_kernel(
    peers, sections, len_ref, hid_in, att_in, que_in, key_in, vw_in, ow_in,
    heat_out, rel_out, hid_ref, att_ref, que_ref, key_ref, vw_ref, ow_ref, load_sem,
    through_ref, keep_ref, ratio_ref, inc_ref, out_ref, prob_ref, pack_ref, gval_ref, val_ref, bv_ref,
    vsend, vrecv, hidt_ref, hida_ref, sv_ref, heats, sm_ref, bvsend, bvbuf,
    asend, abuf, psend, pbuf, below_ref, dsend,
    done, a_recv, p_recv, s_recv, f_recv, x_recv, one_recv, k_recv, b_recv,
    heat_ref, rel_ref, out_sem,
):
    dp = lax.axis_index("dp")
    sec = lax.axis_index("section")
    core = lax.axis_index("mp")
    other = 1 - core
    seq_len, half = hid_ref.shape
    rows_n = seq_len // CHUNKS
    width = ow_ref.shape[1]
    blocks = peers // 2
    local_kv = key_ref.shape[1] // HD
    group = QH // KVH
    heads_n = local_kv * group
    kv_half = local_kv * HD
    block_rows = half // peers
    is_last = sec == sections - 1
    gets = core == dp // blocks
    hops = [(hop, lax.rem(dp + hop, peers)) for hop in range(1, peers)]

    loads = [
        pltpu.make_async_copy(source, target, load_sem.at[at])
        for at, (source, target) in enumerate((
            (hid_in, hid_ref), (att_in, att_ref), (vw_in, vw_ref),
            (que_in, que_ref), (key_in, key_ref), (ow_in, ow_ref),
        ))
    ]
    for load in loads:
        load.start()

    barrier = pltpu.get_barrier_semaphore()
    for hop, to in hops:
        for target in range(2):
            pl.semaphore_signal(
                barrier, inc=1, device_id={"dp": to, "mp": target}, device_id_type=MESH_ID
            )
    pl.semaphore_signal(barrier, inc=1, device_id={"mp": other}, device_id_type=MESH_ID)

    @pl.when(sec > 0)
    def _():
        pl.semaphore_signal(
            barrier, inc=1, device_id={"section": sec - 1}, device_id_type=MESH_ID
        )

    @pl.when(sec < sections - 1)
    def _():
        for at in range(peers):
            pl.semaphore_signal(
                barrier, inc=1, device_id={"dp": at, "section": sec + 1}, device_id_type=MESH_ID
            )

    def barrier_wait():
        greeted = 2 * (peers - 1) + 1

        @pl.when(is_last)
        def _():
            pl.semaphore_wait(barrier, greeted + peers)

        @pl.when(jnp.logical_not(is_last))
        def _():
            pl.semaphore_wait(barrier, greeted + 1)

    def remote(source, target, send, recv, device):
        return pltpu.make_async_remote_copy(
            src_ref=source, dst_ref=target, send_sem=send, recv_sem=recv,
            device_id=device, device_id_type=MESH_ID,
        )

    def rows_of(step):
        return pl.ds((CHUNKS - 1 - step) * rows_n, rows_n)

    def branch_copy(step, block):
        return remote(
            asend.at[step, block], abuf.at[step, dp],
            done.at[0], a_recv.at[step, dp], {"dp": core * blocks + block},
        )

    def direct_copy(step, block):
        return remote(
            dsend.at[step - DIRECT, block], abuf.at[step, dp],
            done.at[1], a_recv.at[step, dp],
            {"dp": core * blocks + block, "section": sec - 1},
        )

    def through_copy(step, target):
        rows = rows_of(step)
        return remote(
            through_ref.at[rows], below_ref.at[rows],
            done.at[0], one_recv.at[3], {"section": target},
        )

    def branch_forward(step, source):
        view = abuf.at[step, source]
        return remote(
            view, view, done.at[0], a_recv.at[step, source], {"mp": other}
        )

    rounds = peers.bit_length() - 1

    def slot_of(turn, target):
        return peers - (peers >> turn) + target // (2 << turn)

    def part_target(turn, at):
        bit = 1 << turn
        return lax.rem(dp, bit) + bit * (2 * at + 1 - lax.rem(dp // bit, 2))

    def part_copy(step, turn, at):
        bit = 1 << turn
        slot = peers - (peers >> turn) + at
        return remote(
            psend.at[step, part_target(turn, at)], pbuf.at[step, slot],
            done.at[0], p_recv.at[step, slot],
            {"dp": dp + bit - 2 * bit * lax.rem(dp // bit, 2)},
        )

    def part_take(step, turn, target):
        slot = slot_of(turn, target)
        view = pbuf.at[step, slot]
        remote(
            view, view, done.at[0], p_recv.at[step, slot], {"mp": other}
        ).wait_recv()
        return pbuf[step, slot].astype(F32)

    def mix_stage(step):
        for turn in range(1, rounds):
            for at in range(peers >> (turn + 1)):
                target = part_target(turn, at)
                running = psend[step, target].astype(F32)
                for before in range(turn):
                    running = running + part_take(step, before, target)
                psend[step, target] = running.astype(BF16)
                part_copy(step, turn, at).start()

    def value_rows(step, source):
        return gval_ref.at[source, pl.ds(0, (CHUNKS - step) * rows_n)]

    def prob_tiles(step, source):
        first = sum(tiles_of(heads_n, before) for before in range(step))
        return pack_ref.at[source, pl.ds(first, tiles_of(heads_n, step))]

    def relays(source, through):
        return jnp.logical_or(
            jnp.logical_and(source == 0, through == peers - 2),
            jnp.logical_and(source == peers - 1, through == 1),
        )

    def lane(source, to):
        return relays(source, to).astype(jnp.int32)

    def gather_value(first, to):
        view = value_rows(first, dp)
        return remote(
            view, view, done.at[0], k_recv.at[CHUNKS, lane(dp, to)], {"dp": to}
        )

    def gather_probs(step, to):
        view = prob_tiles(step, dp)
        return remote(
            view, view, done.at[0], k_recv.at[step, lane(dp, to)], {"dp": to}
        )

    def sum_copy(step, hop, to):
        return remote(
            bvsend.at[step, hop], bvbuf.at[step, dp],
            done.at[0], b_recv.at[step], {"dp": to},
        )

    def sens_copy(step, owner):
        view = sv_ref.at[dp, owner, rows_of(step)]
        return remote(view, view, done.at[0], s_recv.at[step], {"mp": other})

    def final_copy(step, hop, to, side):
        view = sv_ref.at[dp, core, rows_of(step)]
        return remote(
            view, view, done.at[0], f_recv.at[step // (CHUNKS - 1)],
            {"dp": to, "mp": core if side == 0 else other},
        )

    early = pl.ds(rows_n, seq_len - rows_n)

    def final_wait(at, owners, rows):
        view = sv_ref.at[pl.ds(0, peers - 1), owners, rows]
        remote(view, view, done.at[0], f_recv.at[at], {"mp": other}).wait_recv()

    def final_forward(source, owner, at):
        rows = rows_of(CHUNKS - 1) if at else early
        view = sv_ref.at[source, owner, rows]
        return remote(view, view, done.at[0], f_recv.at[2 + at], {"mp": other})

    def final_out(step):
        for hop, to in hops:
            final_copy(step, hop, to, 0).start()

    def section_copy(step, target):
        return remote(
            out_ref.at[rows_of(step)], inc_ref.at[rows_of(step)],
            done.at[0], x_recv.at[step], {"section": target},
        )

    def hidden_copy(hop, to):
        return remote(
            hidt_ref.at[pl.ds(pl.multiple_of(to * block_rows, 16), block_rows)], hida_ref.at[dp],
            done.at[0], one_recv.at[2], {"dp": to},
        )

    def hidden_wait():
        view = hida_ref.at[pl.ds(0, peers - 1)]
        remote(view, view, done.at[0], one_recv.at[2], {"mp": other}).wait_recv()

    def value_copy(slot):
        return remote(
            vsend.at[slot], vrecv, done.at[0], one_recv.at[0], {"mp": other}
        )

    def heat_copy(slot):
        return remote(
            heats.at[slot], heats.at[slot], done.at[0], one_recv.at[1], {"mp": other}
        )

    def branch_stage(step):
        rows = rows_of(step)
        sens = (inc_ref[rows, :].astype(F32) * through_ref[rows, :]).astype(BF16)
        for block in range(blocks):
            to = core * blocks + block
            piece = sens[:, block * width:(block + 1) * width]
            asend[step, block] = piece

            @pl.when(to == dp)
            def _():
                abuf[step, dp] = piece
                branch_forward(step, dp).start()

            @pl.when(to != dp)
            def _():
                branch_copy(step, block).start()

    def branch_wait(step, direct):
        @pl.when(gets)
        def _():
            for hop in range(0 if direct else 1, peers):
                source = lax.rem(dp + hop, peers)
                branch_forward(step, source).wait_recv()
                branch_forward(step, source).start()

        @pl.when(jnp.logical_not(gets))
        def _():
            for source in range(peers):
                branch_forward(step, source).wait_recv()

        return abuf[step].reshape(peers * rows_n, width)

    def part_stage(step):
        stacked = branch_wait(step, False)

        def tile(at, unused):
            start = pl.multiple_of(at * TILE, TILE)
            part = nt_dot(stacked, ow_ref[pl.ds(start, TILE), :]).astype(BF16)
            psend[step, :, :, pl.ds(start, TILE)] = part.reshape(peers, rows_n, TILE)
            return unused

        lax.fori_loop(0, half // TILE, tile, 0, unroll=True)
        for at in range(peers // 2):
            part_copy(step, 0, at).start()

    def add_values(seq, rows, mixed):
        for kv in range(local_kv):
            heads = range(kv * group, (kv + 1) * group)
            left = jnp.concatenate([prob_ref[seq, h, rows, :] for h in heads], axis=0)
            right = jnp.concatenate([mixed[:, h * HD:(h + 1) * HD] for h in heads], axis=0)
            columns = pl.ds(kv * HD, HD)
            bv_ref[seq, :, columns] = bv_ref[seq, :, columns] + tn_dot(left, right)

    def head_stage(step):
        rows = rows_of(step)
        back = psend[step, dp].astype(F32)
        for turn in range(rounds):
            back = back + part_take(step, turn, dp)
        add_values(dp, rows, (ratio_ref[dp, rows, :] * back).astype(BF16))
        settle(step, bv_ref[dp, rows, :])

    def linear_stage(step, direct=False):
        rows = rows_of(step)
        stacked = branch_wait(step, direct)
        for at in range(half // TILE):
            columns = pl.ds(at * TILE, TILE)
            part = nt_dot(stacked, ow_ref[columns, :])
            ratio = ratio_ref[:, rows, columns].reshape(peers * rows_n, TILE)
            sm_ref[:, columns] = (ratio * part).astype(BF16)
        for seq in range(peers):
            add_values(seq, rows, sm_ref[seq * rows_n:(seq + 1) * rows_n, :])
        for hop, to in hops:
            bvsend[step, hop] = bv_ref[to, rows, :].astype(BF16)
            sum_copy(step, hop, to).start()

    def join_stage(step):
        total = bv_ref[dp, rows_of(step), :]
        view = bvbuf.at[step, pl.ds(0, peers - 1)]
        remote(view, view, done.at[0], b_recv.at[step], {"mp": other}).wait_recv()
        for hop, source in hops:
            total = total + bvbuf[step, source].astype(F32)
        settle(step, total)

    def settle(step, back_values):
        rows = rows_of(step)
        sv_ref[dp, core, rows, :] = (val_ref[rows, :] * back_values).astype(BF16)
        sens_copy(step, core).start()

        @pl.when(jnp.logical_not(is_last))
        def _():
            final_out(step)

    def emit_stage(step):
        rows = rows_of(step)
        sens_copy(step, other).wait_recv()
        sens = jnp.concatenate([sv_ref[dp, 0, rows, :], sv_ref[dp, 1, rows, :]], axis=1)
        sums = jnp.zeros((rows_n, HD), F32)
        for at in range(half // TILE):
            columns = pl.ds(at * TILE, TILE)
            back_in = nt_dot(sens, vw_ref[columns, :])
            out = (
                inc_ref[rows, columns].astype(F32) * keep_ref[rows, columns]
                + hid_ref[rows, columns].astype(F32) * back_in
            ).astype(BF16)
            out_ref[rows, columns] = out
            wide = out.astype(F32)
            for lane in range(TILE // HD):
                sums = sums + wide[:, lane * HD:(lane + 1) * HD]
        heats[core, rows, :] = sums

        @pl.when(sec > 0)
        def _():
            if step >= DIRECT:
                if step == DIRECT:
                    view = below_ref.at[pl.ds(0, (CHUNKS - DIRECT) * rows_n)]
                    remote(view, view, done.at[0], one_recv.at[3], {"mp": other}).wait_recv()
                below = (out_ref[rows, :].astype(F32) * below_ref[rows, :]).astype(BF16)
                for block in range(blocks):
                    dsend[step - DIRECT, block] = below[:, block * width:(block + 1) * width]
                    direct_copy(step, block).start()
            else:
                section_copy(step, sec - 1).start()

    lane_at = lax.broadcasted_iota(jnp.int32, (rows_n, HD), 1)

    def shifted(tile, start, count, to):
        inside = (lane_at >= start) & (lane_at < start + count)
        kept = jnp.where(inside, tile, 0.0)
        return kept if start == to else pltpu.roll(kept, (to - start) % HD, 1)

    def pack_stage(step):
        at = sum(tiles_of(heads_n, before) for before in range(step))
        for start, lanes in SEGMENTS[step]:
            per = HD // lanes
            for first in range(0, heads_n, per):
                tile = None
                for h in range(first, min(first + per, heads_n)):
                    piece = shifted(
                        prob_ref[dp, h, rows_of(step), :].astype(F32), start, lanes, (h - first) * lanes
                    )
                    tile = piece if tile is None else tile + piece
                pack_ref[dp, at] = tile.astype(BF16)
                at += 1

    def value_wait(first):
        gather_wait(
            CHUNKS, lambda count: gval_ref.at[pl.ds(0, count), pl.ds(0, (CHUNKS - first) * rows_n)]
        )

    def far(to):
        return jnp.logical_and(dp + to == peers - 1, jnp.logical_or(dp == 0, to == 0))

    def relay_copy(step, view, source):
        return remote(
            view, view, done.at[0], k_recv.at[step, 0], {"dp": peers - 1 - source}
        )

    def gather_wait(step, views):
        def wait(view):
            remote(view, view, done.at[0], k_recv.at[step, 0], {"mp": other}).wait_recv()

        inner = jnp.logical_and(dp > 0, dp < peers - 1)

        @pl.when(inner)
        def _():
            wait(views(peers - 2))

        @pl.when(jnp.logical_not(inner))
        def _():
            wait(views(peers - 1))

    def relay_stage(step, first=0):
        for end, through in ((0, peers - 2), (peers - 1, 1)):
            @pl.when(dp == through)
            def _():
                views = [(step, prob_tiles(step, end))]
                if step == first:
                    views.insert(0, (CHUNKS, value_rows(first, end)))
                for at, view in views:
                    remote(view, view, done.at[0], k_recv.at[at, 1], {"mp": other}).wait_recv()
                    relay_copy(at, view, end).start()

    def gather_stage(step):
        rows = rows_of(step)
        depth = (CHUNKS - step) * rows_n
        first_tile = sum(tiles_of(heads_n, before) for before in range(step))
        tiles = pl.ds(first_tile, tiles_of(heads_n, step))
        gather_wait(step, lambda count: pack_ref.at[pl.ds(0, count), tiles])
        for hop, source in hops:
            for h in range(heads_n):
                at = first_tile
                whole = None
                for start, lanes in SEGMENTS[step]:
                    per = HD // lanes
                    piece = shifted(
                        pack_ref[source, at + h // per].astype(F32), h % per * lanes, lanes, start
                    )
                    whole = piece if whole is None else whole + piece
                    at += -(-heads_n // per)
                prob_ref[source, h, rows, :] = whole.astype(BF16)
            for kv in range(local_kv):
                heads = range(kv * group, (kv + 1) * group)
                left = jnp.concatenate(
                    [prob_ref[source, h, rows, pl.ds(0, depth)] for h in heads], axis=0
                )
                mixed = jnp.dot(
                    left, gval_ref[source, pl.ds(0, depth), pl.ds(kv * HD, HD)],
                    preferred_element_type=F32,
                )
                ratio = mixed / stabilize(mixed)
                for at, h in enumerate(heads):
                    ratio_ref[source, rows, h * HD:(h + 1) * HD] = (
                        ratio[at * rows_n:(at + 1) * rows_n, :]
                    )

    length = len_ref[0]
    loads[0].wait()
    loads[1].wait()
    for step in range(CHUNKS):
        rows = rows_of(step)
        hid = hid_ref[rows, :].astype(F32)
        att = att_ref[rows, :].astype(F32)
        totals = hid + att
        inverse = 1.0 / stabilize(totals)
        keep_ref[rows, :] = hid * inverse
        through_ref[rows, :] = att * inverse / stabilize(att)

        @pl.when(is_last)
        def _():
            token = (CHUNKS - 1 - step) * rows_n + lax.broadcasted_iota(
                jnp.int32, (rows_n, half), 0
            )
            inc_ref[rows, :] = jnp.where(token < length, totals, 0.0).astype(BF16)

    loads[2].wait()
    hid_all = hid_ref[...]
    for slot in range(2):
        part = jnp.dot(
            hid_all, vw_ref[:, slot * kv_half:(slot + 1) * kv_half], preferred_element_type=F32
        )
        vsend[slot] = part.astype(BF16)

        @pl.when(core == slot)
        def _():
            val_ref[...] = part

    for load in loads[3:]:
        load.wait()
    bv_ref[...] = jnp.zeros_like(bv_ref)
    barrier_wait()
    value_copy(other).start()

    @pl.when(is_last)
    def _():
        branch_stage(0)

    @pl.when(jnp.logical_not(is_last))
    def _():
        for step in range(DIRECT, CHUNKS):
            through_copy(step, sec + 1).start()

    query_at = lax.broadcasted_iota(jnp.int32, (seq_len, seq_len), 0)
    key_at = lax.broadcasted_iota(jnp.int32, (seq_len, seq_len), 1)
    allowed = (key_at <= query_at) & (key_at < length)
    for h in range(heads_n):
        kv = h // group
        scores = nt_dot(
            que_ref[:, h * HD:(h + 1) * HD], key_ref[:, kv * HD:(kv + 1) * HD]
        ) / math.sqrt(HD)
        scores = jnp.where(allowed, scores, -1000000000.0)
        weights = jnp.exp(scores - jnp.max(scores, axis=1, keepdims=True))
        prob_ref[dp, h] = (weights / jnp.sum(weights, axis=1, keepdims=True)).astype(BF16)

    value_copy(other).wait_recv()
    values = (val_ref[...] + vrecv[...].astype(F32)).astype(BF16)
    gval_ref[dp] = values

    @pl.when(is_last)
    def _():
        for step in range(RAW, CHUNKS):
            pack_stage(step)

    @pl.when(jnp.logical_not(is_last))
    def _():
        for step in range(CHUNKS):
            pack_stage(step)
        for hop, to in (hops[1], hops[0], hops[2]):
            @pl.when(jnp.logical_not(far(to)))
            def _():
                gather_value(0, to).start()
                for step in range(CHUNKS):
                    gather_probs(step, to).start()

    wide_values = values.astype(F32)
    val_ref[...] = wide_values / stabilize(wide_values)
    for h in range(heads_n):
        kv = h // group
        mixed = jnp.dot(
            prob_ref[dp, h], values[:, kv * HD:(kv + 1) * HD], preferred_element_type=F32
        )
        ratio_ref[dp, :, h * HD:(h + 1) * HD] = mixed / stabilize(mixed)

    for at in range(half // HD):
        flipped = hid_ref[:, at * HD:(at + 1) * HD].astype(F32).T
        hidt_ref[pl.ds(at * HD, HD), :] = flipped.astype(BF16)
    hida_ref[dp] = hidt_ref[pl.ds(pl.multiple_of(dp * block_rows, 16), block_rows), :]

    def branch_next(step):
        section_copy(step, sec + 1).wait_recv()
        branch_stage(step)

    def hidden_stage(step):
        if step == CHUNKS - 1:
            for at in range(DIRECT, CHUNKS):
                for block in range(blocks):
                    direct_copy(at, block).wait_send()
                section_copy(at, sec - 1).start()
        for hop, to in hops:
            hidden_copy(hop, to).start()

    def emit_next(step):
        if step >= DIRECT:
            section_copy(step, sec + 1).wait_recv()
        emit_stage(step)

    def give_stage(step):
        for hop, to in (hops[1], hops[0], hops[2]):
            @pl.when(jnp.logical_not(far(to)))
            def _():
                if step == RAW:
                    gather_value(RAW, to).start()
                gather_probs(step, to).start()

    stages = {
        "give": give_stage, "emit": emit_stage,
        "values": value_wait, "hidden": hidden_stage, "branch": branch_stage, "relay": relay_stage,
        "gather": gather_stage, "part": part_stage, "mix": mix_stage, "head": head_stage,
        "take": branch_next, "linear": linear_stage, "join": join_stage,
    }

    @pl.when(is_last)
    def _():
        for stage, step in LAST_ORDER:
            if stage == "relay":
                stages[stage] = functools.partial(relay_stage, first=RAW)
            stages[stage](step)
        for step in range(CHUNKS):
            final_out(step)

    @pl.when(jnp.logical_not(is_last))
    def _():
        stages["emit"] = emit_next
        stages["relay"] = relay_stage
        for stage, step in NEXT_ORDER:
            if stage == "linear":
                stages[stage] = functools.partial(linear_stage, direct=step >= DIRECT)
            stages[stage](step)

    heat_copy(core).start()
    last = rows_of(CHUNKS - 1)
    for at, rows in enumerate((early, last)):
        final_wait(at, 0, rows)
        for hop, source in hops:
            final_forward(source, core, at).start()
    hidden_wait()
    final_wait(2, 0, early)
    final_wait(3, 0, last)
    block_at = pl.ds(pl.multiple_of(dp * block_rows, 16), block_rows)
    total = None
    for hop in range(peers):
        source = lax.rem(dp + hop, peers)
        sens = jnp.concatenate([sv_ref[source, 0], sv_ref[source, 1]], axis=1)
        term = jnp.dot(hida_ref[source], sens, preferred_element_type=F32)
        total = term if total is None else total + term
    rel_ref[...] = vw_ref[block_at, :].astype(F32) * total
    stores = [
        pltpu.make_async_copy(source, target, out_sem.at[at])
        for at, (source, target) in enumerate(((heat_ref, heat_out), (rel_ref, rel_out)))
    ]
    stores[1].start()
    heat_copy(other).wait_recv()
    heat_ref[...] = jnp.sum((heats[0] + heats[1]).T, axis=0, keepdims=True) / DW
    stores[0].start()
    for hop, to in hops:
        for step in range(CHUNKS):
            final_copy(step, hop, to, 0).wait_send()

        for at in range(2):
            final_forward(to, core, at).wait_send()
    for step in range(CHUNKS):
        for block in range(blocks):
            mine = core * blocks + block != dp

            @pl.when(mine if step < DIRECT else jnp.logical_and(mine, is_last))
            def _():
                branch_copy(step, block).wait_send()

        @pl.when(gets)
        def _():
            for source in range(peers):
                branch_forward(step, source).wait_send()

        sens_copy(step, core).wait_send()

        @pl.when(sec > 0)
        def _():
            section_copy(step, sec - 1).wait_send()

    def sent(first):
        for hop, to in hops:
            @pl.when(jnp.logical_not(far(to)))
            def _():
                gather_value(first, to).wait_send()
                for step in range(first, CHUNKS):
                    gather_probs(step, to).wait_send()

            @pl.when(relays(to, dp))
            def _():
                relay_copy(CHUNKS, value_rows(first, to), to).wait_send()
                for step in range(first, CHUNKS):
                    relay_copy(step, prob_tiles(step, to), to).wait_send()
            for step in range(first, CHUNKS):
                sum_copy(step, hop, to).wait_send()

    @pl.when(is_last)
    def _():
        sent(RAW)
        for step in range(RAW):
            for turn in range(rounds):
                for at in range(peers >> (turn + 1)):
                    part_copy(step, turn, at).wait_send()

    @pl.when(jnp.logical_not(is_last))
    def _():
        sent(0)
        for step in range(DIRECT, CHUNKS):
            through_copy(step, sec + 1).wait_send()

    value_copy(other).wait_send()
    heat_copy(core).wait_send()
    for hop, to in hops:
        hidden_copy(hop, to).wait_send()
    for store in stores:
        store.wait()


def on_device_chain(hidden_in, attn_out, queries, keys, value_weight, out_weight, lengths):
    peers = lax.axis_size("dp")
    sections = lax.axis_size("section")
    seq_len, half = hidden_in.shape[2:]
    kv_half = keys.shape[3]
    kv_width = value_weight.shape[2]
    width = out_weight.shape[2]
    heads = half // HD
    rows_n = seq_len // CHUNKS
    packed = sum(tiles_of(heads, step) for step in range(CHUNKS))
    vmem = pltpu.VMEM
    dma = pltpu.SemaphoreType.DMA
    heat, relevance = pl.pallas_call(
        functools.partial(chain_kernel, peers, sections),
        out_shape=(
            jax.ShapeDtypeStruct((1, seq_len), F32),
            jax.ShapeDtypeStruct((half // peers, kv_width), F32),
        ),
        in_specs=[pl.BlockSpec(memory_space=pltpu.SMEM)] + [pl.BlockSpec(memory_space=pl.ANY)] * 6,
        out_specs=(pl.BlockSpec(memory_space=pl.ANY), pl.BlockSpec(memory_space=pl.ANY)),
        scratch_shapes=[
            vmem((seq_len, half), BF16),
            vmem((seq_len, half), BF16),
            vmem((seq_len, half), BF16),
            vmem((seq_len, kv_half), BF16),
            vmem((half, kv_width), BF16),
            vmem((half, width), BF16),
            dma((6,)),
            vmem((seq_len, half), F32),
            vmem((seq_len, half), F32),
            vmem((peers, seq_len, half), F32),
            vmem((seq_len, half), BF16),
            vmem((seq_len, half), BF16),
            vmem((peers, heads, seq_len, seq_len), BF16),
            vmem((peers, packed, rows_n, HD), BF16),
            vmem((peers, seq_len, kv_half), BF16),
            vmem((seq_len, kv_half), F32),
            vmem((peers, seq_len, kv_half), F32),
            vmem((2, seq_len, kv_half), BF16),
            vmem((seq_len, kv_half), BF16),
            vmem((half, seq_len), BF16),
            vmem((peers, half // peers, seq_len), BF16),
            vmem((peers, 2, seq_len, kv_half), BF16),
            vmem((2, seq_len, HD), F32),
            vmem((peers * rows_n, half), BF16),
            vmem((CHUNKS, peers, rows_n, kv_half), BF16),
            vmem((CHUNKS, peers, rows_n, kv_half), BF16),
            vmem((CHUNKS, peers // 2, rows_n, width), BF16),
            vmem((CHUNKS, peers, rows_n, width), BF16),
            vmem((RAW, peers, rows_n, half), BF16),
            vmem((RAW, peers - 1, rows_n, half), BF16),
            vmem((seq_len, half), F32),
            vmem((CHUNKS - DIRECT, peers // 2, rows_n, width), BF16),
            dma((2,)),
            dma((CHUNKS, peers)),
            dma((RAW, peers - 1)),
            dma((CHUNKS,)),
            dma((4,)),
            dma((CHUNKS,)),
            dma((4,)),
            dma((CHUNKS + 1, 2)),
            dma((CHUNKS,)),
            vmem((1, seq_len), F32),
            vmem((half // peers, kv_width), F32),
            dma((2,)),
        ],
        compiler_params=pltpu.CompilerParams(
            collective_id=0, has_side_effects=True, vmem_limit_bytes=40 * 1024 * 1024
        ),
        name="relevance_chain",
    )(
        lengths,
        *(
            pltpu.with_memory_space_constraint(operand, pltpu.MemorySpace.HBM)
            for operand in (
                hidden_in[0, 0], attn_out[0, 0], queries[0, 0], keys[0, 0], value_weight[0], out_weight[0],
            )
        ),
    )
    return heat[None], relevance[None]


def solution(mesh):
    placed = (
        P("section", ("groups", "dp"), None, "mp"),
        P("section", ("groups", "dp"), None, "mp"),
        P("section", ("groups", "dp"), None, "mp"),
        P("section", ("groups", "dp"), None, "mp"),
        P("section", "mp", None),
        P("section", "mp", "dp"),
        P(("groups", "dp")),
    )
    peers = mesh.shape["dp"]
    aligned = peers == 4 and mesh.shape["section"] == 2
    return jax.shard_map(
        on_device_chain if aligned else on_device,
        mesh=mesh,
        in_specs=placed,
        out_specs=(
            P("section", ("groups", "dp"), None),
            P(("groups", "section"), ("mp", "dp"), None),
        ),
        check_vma=False,
    )
```

```python
import functools
import math

import jax
import jax.numpy as jnp
from jax import lax
from jax.experimental import pallas as pl
from jax.experimental.pallas import tpu as pltpu
from jax.sharding import PartitionSpec as P

DW = 2560
HD = 128
QH = 20
KVH = 4


EPS = 0.25


def from_behind(shard, axis, by):
    peers = lax.axis_size(axis)
    pairs = [(i, i + by) for i in range(peers) if 0 <= i + by < peers]
    return lax.ppermute(shard, axis, pairs)


def stabilize(entries):
    return jnp.where(entries >= 0, entries + EPS, entries - EPS)


def gated(active, compute, operand, out_shape, out_type):
    return lax.cond(active, compute, lambda unused: jnp.zeros(out_shape, out_type), operand)


def on_device(hidden_in, attn_out, queries, keys, value_weight, out_weight, lengths):
    inputs = hidden_in[0, 0]
    branch = attn_out[0, 0]
    query_rows = queries[0, 0]
    key_rows = keys[0, 0]
    value_rows = value_weight[0]
    seq_len = inputs.shape[0]
    half_width = inputs.shape[1]
    group_size = QH // KVH
    local_kv = key_rows.shape[1] // HD
    kv_width = value_rows.shape[1]
    sections = lax.axis_size("section")
    section_pos = lax.axis_index("section")
    core_pos = lax.axis_index("mp")
    out_cols = lax.all_gather(out_weight, "dp", axis=2, tiled=True)[0]
    inputs_f = inputs.astype(jnp.float32)
    branch_f = branch.astype(jnp.float32)
    totals = inputs_f + branch_f
    value_part = jnp.dot(inputs, value_rows, preferred_element_type=jnp.float32)
    value_all = lax.psum(value_part.astype(jnp.bfloat16), "mp").astype(jnp.float32)
    value_mine = lax.dynamic_slice_in_dim(value_all, core_pos * local_kv * HD, local_kv * HD, 1)
    values_bf = lax.optimization_barrier(value_mine.astype(jnp.bfloat16))
    values_f = values_bf.astype(jnp.float32)
    query_heads = query_rows.reshape(seq_len, local_kv, group_size, HD)
    key_heads = key_rows.reshape(seq_len, local_kv, HD)
    scores = jnp.einsum(
        "tgjd,sgd->gjts", query_heads, key_heads, preferred_element_type=jnp.float32
    ) / math.sqrt(HD)
    position = lax.iota(jnp.int32, seq_len)
    allowed = (position[None, :] <= position[:, None]) & (position[None, :] < lengths[0])
    scores = jnp.where(allowed, scores, -1000000000.0)
    row_top = jnp.max(scores, axis=-1, keepdims=True)
    weights = jnp.exp(scores - row_top)
    prob_rows = (weights / jnp.sum(weights, axis=-1, keepdims=True)).astype(jnp.bfloat16)
    mixed_heads = jnp.einsum(
        "gjts,sgd->tgjd",
        prob_rows,
        values_bf.reshape(seq_len, local_kv, HD),
        preferred_element_type=jnp.float32,
    ).reshape(seq_len, local_kv * group_size * HD)
    valid_rows = (position < lengths[0]).astype(jnp.float32)
    current = (totals * valid_rows[:, None]).astype(jnp.bfloat16)
    result = jnp.zeros((seq_len, half_width), jnp.bfloat16)
    sens_kept = jnp.zeros((seq_len, kv_width), jnp.bfloat16)
    for turn_index in range(sections):
        active = section_pos == sections - 1 - turn_index
        sens_total = current.astype(jnp.float32) / stabilize(totals)
        sens_branch = (branch_f * sens_total / stabilize(branch_f)).astype(jnp.bfloat16)
        sens_full = lax.all_gather(sens_branch, "mp", axis=1, tiled=True)

        def through_heads(operand):
            back_mixed = lax.dot_general(
                operand, out_cols, (((1,), (1,)), ((), ())), preferred_element_type=jnp.float32
            )
            sens_mixed = (mixed_heads * back_mixed / stabilize(mixed_heads)).astype(jnp.bfloat16)
            back_values = jnp.einsum(
                "gjts,tgjd->sgd",
                prob_rows,
                sens_mixed.reshape(seq_len, local_kv, group_size, HD),
                preferred_element_type=jnp.float32,
            ).reshape(seq_len, local_kv * HD)
            return (values_f * back_values / stabilize(values_f)).astype(jnp.bfloat16)

        sens_values = gated(
            active, through_heads, sens_full, (seq_len, local_kv * HD), jnp.bfloat16
        )
        sens_all = lax.all_gather(sens_values, "mp", axis=1, tiled=True)

        def through_values(operand):
            back_inputs = lax.dot_general(
                operand, value_rows, (((1,), (1,)), ((), ())), preferred_element_type=jnp.float32
            )
            return (inputs_f * sens_total + inputs_f * back_inputs).astype(jnp.bfloat16)

        outgoing = gated(active, through_values, sens_all, (seq_len, half_width), jnp.bfloat16)
        result = jnp.where(active, outgoing, result)
        sens_kept = jnp.where(active, sens_all, sens_kept)
        if turn_index + 1 < sections:
            arrived = from_behind(outgoing, "section", -1)
            current = jnp.where(section_pos == sections - 2 - turn_index, arrived, current)
    heat_part = jnp.sum(result.astype(jnp.float32), axis=1)
    heat_rows = lax.psum(heat_part, "mp") / DW
    block_rows = half_width // lax.axis_size("dp")
    row_start = lax.axis_index("dp") * block_rows
    value_block = lax.dynamic_slice_in_dim(value_rows, row_start, block_rows, 0).astype(jnp.float32)
    summed = lax.psum_scatter(
        lax.dot_general(
            inputs, sens_kept, (((0,), (0,)), ((), ())), preferred_element_type=jnp.float32
        ).astype(jnp.bfloat16),
        "dp",
        scatter_dimension=0,
        tiled=True,
    ).astype(jnp.float32)
    relevance_rows = value_block * summed
    return (heat_rows[None, None, :], relevance_rows[None])


CHUNKS = 4
RAW = 2
EARLY = (1,)
SEGMENTS = (((0, 128),), ((0, 64), (64, 32)), ((0, 64),), ((0, 32),))
TILE = 256
MESH_ID = pl.DeviceIdType.MESH
F32 = jnp.float32
BF16 = jnp.bfloat16
DIRECT = 1
LAST_ORDER = (
    ("branch", 1), ("give", 2), ("give", 3), ("branch", 2), ("part", 0), ("branch", 3),
    ("mix", 0), ("part", 1), ("relay", 2), ("relay", 3), ("head", 0), ("emit", 0), ("mix", 1),
    ("ahead", 0), ("values", 2), ("gather", 2), ("gather", 3), ("linear", 2), ("linear", 3),
    ("head", 1), ("emit", 1), ("join", 2), ("join", 3), ("emit", 2), ("emit", 3), ("hidden", 3),
)
NEXT_ORDER = (
    ("relay", 0), ("relay", 1), ("relay", 2), ("relay", 3), ("values", 0), ("gather", 0),
    ("hidden", 0), ("gather", 1), ("take", 0), ("gather", 2), ("gather", 3), ("linear", 0),
    ("linear", 1), ("join", 0), ("emit", 0), ("linear", 2), ("linear", 3), ("join", 1),
    ("join", 2), ("join", 3), ("emit", 1), ("emit", 2), ("emit", 3),
)


def tiles_of(heads, step):
    return sum(-(-heads // (HD // lanes)) for _, lanes in SEGMENTS[step])


def nt_dot(left, right):
    return lax.dot_general(left, right, (((1,), (1,)), ((), ())), preferred_element_type=F32)


def tn_dot(left, right):
    return lax.dot_general(left, right, (((0,), (0,)), ((), ())), preferred_element_type=F32)


def chain_kernel(
    peers, sections, len_ref, hid_in, att_in, que_in, key_in, vw_in, ow_in,
    heat_out, rel_out, hid_ref, att_ref, que_ref, key_ref, vw_ref, ow_ref, load_sem,
    through_ref, keep_ref, ratio_ref, inc_ref, out_ref, prob_ref, pack_ref, gval_ref, val_ref, bv_ref,
    vsend, vrecv, hidt_ref, hida_ref, sv_ref, heats, sm_ref, bvsend, bvbuf,
    asend, abuf, psend, pbuf, below_ref, dsend,
    done, a_recv, p_recv, s_recv, f_recv, x_recv, one_recv, k_recv, b_recv,
    heat_ref, rel_ref, out_sem,
):
    dp = lax.axis_index("dp")
    sec = lax.axis_index("section")
    core = lax.axis_index("mp")
    other = 1 - core
    seq_len, half = hid_ref.shape
    rows_n = seq_len // CHUNKS
    width = ow_ref.shape[1]
    blocks = peers // 2
    local_kv = key_ref.shape[1] // HD
    group = QH // KVH
    heads_n = local_kv * group
    kv_half = local_kv * HD
    block_rows = half // peers
    is_last = sec == sections - 1
    gets = core == dp // blocks
    hops = [(hop, lax.rem(dp + hop, peers)) for hop in range(1, peers)]

    loads = [
        pltpu.make_async_copy(source, target, load_sem.at[at])
        for at, (source, target) in enumerate((
            (hid_in, hid_ref), (att_in, att_ref), (vw_in, vw_ref),
            (que_in, que_ref), (key_in, key_ref), (ow_in, ow_ref),
        ))
    ]
    for load in loads:
        load.start()

    barrier = pltpu.get_barrier_semaphore()
    for hop, to in hops:
        for target in range(2):
            pl.semaphore_signal(
                barrier, inc=1, device_id={"dp": to, "mp": target}, device_id_type=MESH_ID
            )
    pl.semaphore_signal(barrier, inc=1, device_id={"mp": other}, device_id_type=MESH_ID)

    @pl.when(sec > 0)
    def _():
        pl.semaphore_signal(
            barrier, inc=1, device_id={"section": sec - 1}, device_id_type=MESH_ID
        )

    @pl.when(sec < sections - 1)
    def _():
        for at in range(peers):
            pl.semaphore_signal(
                barrier, inc=1, device_id={"dp": at, "section": sec + 1}, device_id_type=MESH_ID
            )

    def barrier_wait():
        greeted = 2 * (peers - 1) + 1

        @pl.when(is_last)
        def _():
            pl.semaphore_wait(barrier, greeted + peers)

        @pl.when(jnp.logical_not(is_last))
        def _():
            pl.semaphore_wait(barrier, greeted + 1)

    def remote(source, target, send, recv, device):
        return pltpu.make_async_remote_copy(
            src_ref=source, dst_ref=target, send_sem=send, recv_sem=recv,
            device_id=device, device_id_type=MESH_ID,
        )

    def rows_of(step):
        return pl.ds((CHUNKS - 1 - step) * rows_n, rows_n)

    def branch_copy(step, block):
        return remote(
            asend.at[step, block], abuf.at[step, dp],
            done.at[0], a_recv.at[step, dp], {"dp": core * blocks + block},
        )

    def direct_copy(step, block):
        return remote(
            dsend.at[step - DIRECT, block], abuf.at[step, dp],
            done.at[1], a_recv.at[step, dp],
            {"dp": core * blocks + block, "section": sec - 1},
        )

    def through_copy(step, target):
        rows = rows_of(step)
        return remote(
            through_ref.at[rows], below_ref.at[rows],
            done.at[0], one_recv.at[3], {"section": target},
        )

    def branch_forward(step, source):
        view = abuf.at[step, source]
        return remote(
            view, view, done.at[0], a_recv.at[step, source], {"mp": other}
        )

    rounds = peers.bit_length() - 1

    def slot_of(turn, target):
        return peers - (peers >> turn) + target // (2 << turn)

    def part_target(turn, at):
        bit = 1 << turn
        return lax.rem(dp, bit) + bit * (2 * at + 1 - lax.rem(dp // bit, 2))

    def part_copy(step, turn, at):
        bit = 1 << turn
        slot = peers - (peers >> turn) + at
        return remote(
            psend.at[step, part_target(turn, at)], pbuf.at[step, slot],
            done.at[0], p_recv.at[step, slot],
            {"dp": dp + bit - 2 * bit * lax.rem(dp // bit, 2)},
        )

    def part_take(step, turn, target):
        slot = slot_of(turn, target)
        view = pbuf.at[step, slot]
        remote(
            view, view, done.at[0], p_recv.at[step, slot], {"mp": other}
        ).wait_recv()
        return pbuf[step, slot].astype(F32)

    def mix_stage(step):
        for turn in range(1, rounds):
            for at in range(peers >> (turn + 1)):
                target = part_target(turn, at)
                running = psend[step, target].astype(F32)
                for before in range(turn):
                    running = running + part_take(step, before, target)
                psend[step, target] = running.astype(BF16)
                part_copy(step, turn, at).start()

    def value_rows(step, source):
        return gval_ref.at[source, pl.ds(0, (CHUNKS - step) * rows_n)]

    def prob_tiles(step, source):
        first = sum(tiles_of(heads_n, before) for before in range(step))
        return pack_ref.at[source, pl.ds(first, tiles_of(heads_n, step))]

    def relays(source, through):
        return jnp.logical_or(
            jnp.logical_and(source == 0, through == peers - 2),
            jnp.logical_and(source == peers - 1, through == 1),
        )

    def lane(source, to):
        return relays(source, to).astype(jnp.int32)

    def gather_value(first, to):
        view = value_rows(first, dp)
        return remote(
            view, view, done.at[0], k_recv.at[CHUNKS, lane(dp, to)], {"dp": to}
        )

    def gather_probs(step, to):
        view = prob_tiles(step, dp)
        return remote(
            view, view, done.at[0], k_recv.at[step, lane(dp, to)], {"dp": to}
        )

    def sum_copy(step, hop, to):
        return remote(
            bvsend.at[step, hop], bvbuf.at[step, dp],
            done.at[0], b_recv.at[step], {"dp": to},
        )

    def sens_copy(step, owner):
        view = sv_ref.at[dp, owner, rows_of(step)]
        return remote(view, view, done.at[0], s_recv.at[step], {"mp": other})

    def final_copy(step, hop, to, side):
        view = sv_ref.at[dp, core, rows_of(step)]
        return remote(
            view, view, done.at[0], f_recv.at[step // (CHUNKS - 1)],
            {"dp": to, "mp": core if side == 0 else other},
        )

    early = pl.ds(rows_n, seq_len - rows_n)

    def final_wait(at, owners, rows):
        view = sv_ref.at[pl.ds(0, peers - 1), owners, rows]
        remote(view, view, done.at[0], f_recv.at[at], {"mp": other}).wait_recv()

    def final_forward(source, owner, at):
        rows = rows_of(CHUNKS - 1) if at else early
        view = sv_ref.at[source, owner, rows]
        return remote(view, view, done.at[0], f_recv.at[2 + at], {"mp": other})

    def final_out(step):
        for hop, to in hops:
            final_copy(step, hop, to, 0).start()

    def section_copy(step, target):
        return remote(
            out_ref.at[rows_of(step)], inc_ref.at[rows_of(step)],
            done.at[0], x_recv.at[step], {"section": target},
        )

    def hidden_copy(hop, to):
        return remote(
            hidt_ref.at[pl.ds(pl.multiple_of(to * block_rows, 16), block_rows)], hida_ref.at[dp],
            done.at[0], one_recv.at[2], {"dp": to},
        )

    def hidden_wait():
        view = hida_ref.at[pl.ds(0, peers - 1)]
        remote(view, view, done.at[0], one_recv.at[2], {"mp": other}).wait_recv()

    def value_copy(slot):
        return remote(
            vsend.at[slot], vrecv, done.at[0], one_recv.at[0], {"mp": other}
        )

    def heat_copy(slot):
        return remote(
            heats.at[slot], heats.at[slot], done.at[0], one_recv.at[1], {"mp": other}
        )

    def branch_stage(step):
        rows = rows_of(step)
        sens = (inc_ref[rows, :].astype(F32) * through_ref[rows, :]).astype(BF16)
        for block in range(blocks):
            to = core * blocks + block
            piece = sens[:, block * width:(block + 1) * width]
            asend[step, block] = piece

            @pl.when(to == dp)
            def _():
                abuf[step, dp] = piece
                branch_forward(step, dp).start()

            @pl.when(to != dp)
            def _():
                branch_copy(step, block).start()

    def branch_wait(step, direct):
        @pl.when(gets)
        def _():
            for hop in range(0 if direct else 1, peers):
                source = lax.rem(dp + hop, peers)
                branch_forward(step, source).wait_recv()
                branch_forward(step, source).start()

        @pl.when(jnp.logical_not(gets))
        def _():
            for source in range(peers):
                branch_forward(step, source).wait_recv()

        return abuf[step].reshape(peers * rows_n, width)

    def part_stage(step):
        stacked = branch_wait(step, False)

        def tile(at, unused):
            start = pl.multiple_of(at * TILE, TILE)
            part = nt_dot(stacked, ow_ref[pl.ds(start, TILE), :]).astype(BF16)
            psend[step, :, :, pl.ds(start, TILE)] = part.reshape(peers, rows_n, TILE)
            return unused

        lax.fori_loop(0, half // TILE, tile, 0, unroll=True)
        for at in range(peers // 2):
            part_copy(step, 0, at).start()

    def add_values(seq, rows, mixed):
        for kv in range(local_kv):
            heads = range(kv * group, (kv + 1) * group)
            left = jnp.concatenate([prob_ref[seq, h, rows, :] for h in heads], axis=0)
            right = jnp.concatenate([mixed[:, h * HD:(h + 1) * HD] for h in heads], axis=0)
            columns = pl.ds(kv * HD, HD)
            bv_ref[seq, :, columns] = bv_ref[seq, :, columns] + tn_dot(left, right)

    def head_stage(step):
        rows = rows_of(step)
        back = psend[step, dp].astype(F32)
        for turn in range(rounds):
            back = back + part_take(step, turn, dp)
        add_values(dp, rows, (ratio_ref[dp, rows, :] * back).astype(BF16))
        settle(step, bv_ref[dp, rows, :])

    def linear_stage(step, direct=False):
        rows = rows_of(step)
        stacked = branch_wait(step, direct)
        for at in range(half // TILE):
            columns = pl.ds(at * TILE, TILE)
            part = nt_dot(stacked, ow_ref[columns, :])
            ratio = ratio_ref[:, rows, columns].reshape(peers * rows_n, TILE)
            sm_ref[:, columns] = (ratio * part).astype(BF16)
        for seq in range(peers):
            add_values(seq, rows, sm_ref[seq * rows_n:(seq + 1) * rows_n, :])
        for hop, to in hops:
            bvsend[step, hop] = bv_ref[to, rows, :].astype(BF16)
            sum_copy(step, hop, to).start()

    def join_stage(step):
        total = bv_ref[dp, rows_of(step), :]
        view = bvbuf.at[step, pl.ds(0, peers - 1)]
        remote(view, view, done.at[0], b_recv.at[step], {"mp": other}).wait_recv()
        for hop, source in hops:
            total = total + bvbuf[step, source].astype(F32)
        settle(step, total)

    def settle(step, back_values):
        rows = rows_of(step)
        sv_ref[dp, core, rows, :] = (val_ref[rows, :] * back_values).astype(BF16)
        sens_copy(step, core).start()

        @pl.when(jnp.logical_not(is_last))
        def _():
            final_out(step)

    def emit_stage(step):
        rows = rows_of(step)
        sens_copy(step, other).wait_recv()
        sens = jnp.concatenate([sv_ref[dp, 0, rows, :], sv_ref[dp, 1, rows, :]], axis=1)
        sums = jnp.zeros((rows_n, HD), F32)
        for at in range(half // TILE):
            columns = pl.ds(at * TILE, TILE)
            back_in = nt_dot(sens, vw_ref[columns, :])
            out = (
                inc_ref[rows, columns].astype(F32) * keep_ref[rows, columns]
                + hid_ref[rows, columns].astype(F32) * back_in
            ).astype(BF16)
            out_ref[rows, columns] = out
            wide = out.astype(F32)
            for lane in range(TILE // HD):
                sums = sums + wide[:, lane * HD:(lane + 1) * HD]
        heats[core, rows, :] = sums

        @pl.when(sec > 0)
        def _():
            if step >= DIRECT:
                if step == DIRECT:
                    view = below_ref.at[pl.ds(0, (CHUNKS - DIRECT) * rows_n)]
                    remote(view, view, done.at[0], one_recv.at[3], {"mp": other}).wait_recv()
                below = (out_ref[rows, :].astype(F32) * below_ref[rows, :]).astype(BF16)
                for block in range(blocks):
                    dsend[step - DIRECT, block] = below[:, block * width:(block + 1) * width]
                    direct_copy(step, block).start()
            else:
                section_copy(step, sec - 1).start()

    lane_at = lax.broadcasted_iota(jnp.int32, (rows_n, HD), 1)

    def shifted(tile, start, count, to):
        inside = (lane_at >= start) & (lane_at < start + count)
        kept = jnp.where(inside, tile, 0.0)
        return kept if start == to else pltpu.roll(kept, (to - start) % HD, 1)

    def pack_stage(step):
        at = sum(tiles_of(heads_n, before) for before in range(step))
        for start, lanes in SEGMENTS[step]:
            per = HD // lanes
            for first in range(0, heads_n, per):
                tile = None
                for h in range(first, min(first + per, heads_n)):
                    piece = shifted(
                        prob_ref[dp, h, rows_of(step), :].astype(F32), start, lanes, (h - first) * lanes
                    )
                    tile = piece if tile is None else tile + piece
                pack_ref[dp, at] = tile.astype(BF16)
                at += 1

    def value_wait(first):
        gather_wait(
            CHUNKS, lambda count: gval_ref.at[pl.ds(0, count), pl.ds(0, (CHUNKS - first) * rows_n)]
        )

    def far(to):
        return jnp.logical_and(dp + to == peers - 1, jnp.logical_or(dp == 0, to == 0))

    def relay_copy(step, view, source):
        return remote(
            view, view, done.at[0], k_recv.at[step, 0], {"dp": peers - 1 - source}
        )

    def gather_wait(step, views):
        def wait(view):
            remote(view, view, done.at[0], k_recv.at[step, 0], {"mp": other}).wait_recv()

        inner = jnp.logical_and(dp > 0, dp < peers - 1)

        @pl.when(inner)
        def _():
            wait(views(peers - 2))

        @pl.when(jnp.logical_not(inner))
        def _():
            wait(views(peers - 1))

    def relay_stage(step, first=0):
        for end, through in ((0, peers - 2), (peers - 1, 1)):
            @pl.when(dp == through)
            def _():
                views = [(step, prob_tiles(step, end))]
                if step == first:
                    views.insert(0, (CHUNKS, value_rows(first, end)))
                for at, view in views:
                    remote(view, view, done.at[0], k_recv.at[at, 1], {"mp": other}).wait_recv()
                    relay_copy(at, view, end).start()

    def gather_stage(step):
        rows = rows_of(step)
        depth = (CHUNKS - step) * rows_n
        first_tile = sum(tiles_of(heads_n, before) for before in range(step))
        tiles = pl.ds(first_tile, tiles_of(heads_n, step))
        gather_wait(step, lambda count: pack_ref.at[pl.ds(0, count), tiles])
        for hop, source in hops:
            for h in range(heads_n):
                at = first_tile
                whole = None
                for start, lanes in SEGMENTS[step]:
                    per = HD // lanes
                    piece = shifted(
                        pack_ref[source, at + h // per].astype(F32), h % per * lanes, lanes, start
                    )
                    whole = piece if whole is None else whole + piece
                    at += -(-heads_n // per)
                prob_ref[source, h, rows, :] = whole.astype(BF16)
            for kv in range(local_kv):
                heads = range(kv * group, (kv + 1) * group)
                left = jnp.concatenate(
                    [prob_ref[source, h, rows, pl.ds(0, depth)] for h in heads], axis=0
                )
                mixed = jnp.dot(
                    left, gval_ref[source, pl.ds(0, depth), pl.ds(kv * HD, HD)],
                    preferred_element_type=F32,
                )
                ratio = mixed / stabilize(mixed)
                for at, h in enumerate(heads):
                    ratio_ref[source, rows, h * HD:(h + 1) * HD] = (
                        ratio[at * rows_n:(at + 1) * rows_n, :]
                    )

    length = len_ref[0]
    loads[0].wait()
    loads[1].wait()
    for step in range(CHUNKS):
        rows = rows_of(step)
        hid = hid_ref[rows, :].astype(F32)
        att = att_ref[rows, :].astype(F32)
        totals = hid + att
        inverse = 1.0 / stabilize(totals)
        keep_ref[rows, :] = hid * inverse
        through_ref[rows, :] = att * inverse / stabilize(att)

        @pl.when(is_last)
        def _():
            token = (CHUNKS - 1 - step) * rows_n + lax.broadcasted_iota(
                jnp.int32, (rows_n, half), 0
            )
            inc_ref[rows, :] = jnp.where(token < length, totals, 0.0).astype(BF16)

    loads[2].wait()
    hid_all = hid_ref[...]
    for slot in range(2):
        part = jnp.dot(
            hid_all, vw_ref[:, slot * kv_half:(slot + 1) * kv_half], preferred_element_type=F32
        )
        vsend[slot] = part.astype(BF16)

        @pl.when(core == slot)
        def _():
            val_ref[...] = part

    for load in loads[3:]:
        load.wait()
    bv_ref[...] = jnp.zeros_like(bv_ref)
    barrier_wait()
    value_copy(other).start()

    @pl.when(is_last)
    def _():
        branch_stage(0)

    @pl.when(jnp.logical_not(is_last))
    def _():
        for step in range(DIRECT, CHUNKS):
            through_copy(step, sec + 1).start()

    query_at = lax.broadcasted_iota(jnp.int32, (seq_len, seq_len), 0)
    key_at = lax.broadcasted_iota(jnp.int32, (seq_len, seq_len), 1)
    allowed = (key_at <= query_at) & (key_at < length)
    for h in range(heads_n):
        kv = h // group
        scores = nt_dot(
            que_ref[:, h * HD:(h + 1) * HD], key_ref[:, kv * HD:(kv + 1) * HD]
        ) / math.sqrt(HD)
        scores = jnp.where(allowed, scores, -1000000000.0)
        weights = jnp.exp(scores - jnp.max(scores, axis=1, keepdims=True))
        prob_ref[dp, h] = (weights / jnp.sum(weights, axis=1, keepdims=True)).astype(BF16)

    value_copy(other).wait_recv()
    values = (val_ref[...] + vrecv[...].astype(F32)).astype(BF16)
    gval_ref[dp] = values

    @pl.when(is_last)
    def _():
        for step in range(RAW, CHUNKS):
            pack_stage(step)

    @pl.when(jnp.logical_not(is_last))
    def _():
        for step in range(CHUNKS):
            pack_stage(step)
        for hop, to in (hops[1], hops[0], hops[2]):
            @pl.when(jnp.logical_not(far(to)))
            def _():
                gather_value(0, to).start()
                for step in range(CHUNKS):
                    gather_probs(step, to).start()

    wide_values = values.astype(F32)
    val_ref[...] = wide_values / stabilize(wide_values)
    for h in range(heads_n):
        kv = h // group
        mixed = jnp.dot(
            prob_ref[dp, h], values[:, kv * HD:(kv + 1) * HD], preferred_element_type=F32
        )
        ratio_ref[dp, :, h * HD:(h + 1) * HD] = mixed / stabilize(mixed)

    for at in range(half // HD):
        flipped = hid_ref[:, at * HD:(at + 1) * HD].astype(F32).T
        hidt_ref[pl.ds(at * HD, HD), :] = flipped.astype(BF16)
    hida_ref[dp] = hidt_ref[pl.ds(pl.multiple_of(dp * block_rows, 16), block_rows), :]

    def branch_next(step):
        section_copy(step, sec + 1).wait_recv()
        branch_stage(step)

    def hidden_stage(step):
        if step == CHUNKS - 1:
            for at in range(DIRECT, CHUNKS):
                for block in range(blocks):
                    direct_copy(at, block).wait_send()
                section_copy(at, sec - 1).start()
        for hop, to in hops:
            if step == 0 or hop not in EARLY:
                hidden_copy(hop, to).start()

    def ahead_stage(step):
        hop, to = hops[step]
        hidden_copy(hop, to).start()

    def emit_next(step):
        if step >= DIRECT:
            section_copy(step, sec + 1).wait_recv()
        emit_stage(step)

    def give_stage(step):
        for hop, to in (hops[1], hops[0], hops[2]):
            @pl.when(jnp.logical_not(far(to)))
            def _():
                if step == RAW:
                    gather_value(RAW, to).start()
                gather_probs(step, to).start()

    stages = {
        "ahead": ahead_stage, "give": give_stage, "emit": emit_stage,
        "values": value_wait, "hidden": hidden_stage, "branch": branch_stage, "relay": relay_stage,
        "gather": gather_stage, "part": part_stage, "mix": mix_stage, "head": head_stage,
        "take": branch_next, "linear": linear_stage, "join": join_stage,
    }

    @pl.when(is_last)
    def _():
        for stage, step in LAST_ORDER:
            if stage == "relay":
                stages[stage] = functools.partial(relay_stage, first=RAW)
            stages[stage](step)
        for step in range(CHUNKS):
            final_out(step)

    @pl.when(jnp.logical_not(is_last))
    def _():
        stages["emit"] = emit_next
        stages["relay"] = relay_stage
        for stage, step in NEXT_ORDER:
            if stage == "linear":
                stages[stage] = functools.partial(linear_stage, direct=step >= DIRECT)
            stages[stage](step)

    heat_copy(core).start()
    last = rows_of(CHUNKS - 1)
    for at, rows in enumerate((early, last)):
        final_wait(at, 0, rows)
        for hop, source in hops:
            final_forward(source, core, at).start()
    hidden_wait()
    final_wait(2, 0, early)
    final_wait(3, 0, last)
    block_at = pl.ds(pl.multiple_of(dp * block_rows, 16), block_rows)
    total = None
    for hop in range(peers):
        source = lax.rem(dp + hop, peers)
        sens = jnp.concatenate([sv_ref[source, 0], sv_ref[source, 1]], axis=1)
        term = jnp.dot(hida_ref[source], sens, preferred_element_type=F32)
        total = term if total is None else total + term
    rel_ref[...] = vw_ref[block_at, :].astype(F32) * total
    stores = [
        pltpu.make_async_copy(source, target, out_sem.at[at])
        for at, (source, target) in enumerate(((heat_ref, heat_out), (rel_ref, rel_out)))
    ]
    stores[1].start()
    heat_copy(other).wait_recv()
    heat_ref[...] = jnp.sum((heats[0] + heats[1]).T, axis=0, keepdims=True) / DW
    stores[0].start()
    for hop, to in hops:
        for step in range(CHUNKS):
            final_copy(step, hop, to, 0).wait_send()

        for at in range(2):
            final_forward(to, core, at).wait_send()
    for step in range(CHUNKS):
        for block in range(blocks):
            mine = core * blocks + block != dp

            @pl.when(mine if step < DIRECT else jnp.logical_and(mine, is_last))
            def _():
                branch_copy(step, block).wait_send()

        @pl.when(gets)
        def _():
            for source in range(peers):
                branch_forward(step, source).wait_send()

        sens_copy(step, core).wait_send()

        @pl.when(sec > 0)
        def _():
            section_copy(step, sec - 1).wait_send()

    def sent(first):
        for hop, to in hops:
            @pl.when(jnp.logical_not(far(to)))
            def _():
                gather_value(first, to).wait_send()
                for step in range(first, CHUNKS):
                    gather_probs(step, to).wait_send()

            @pl.when(relays(to, dp))
            def _():
                relay_copy(CHUNKS, value_rows(first, to), to).wait_send()
                for step in range(first, CHUNKS):
                    relay_copy(step, prob_tiles(step, to), to).wait_send()
            for step in range(first, CHUNKS):
                sum_copy(step, hop, to).wait_send()

    @pl.when(is_last)
    def _():
        sent(RAW)
        for step in range(RAW):
            for turn in range(rounds):
                for at in range(peers >> (turn + 1)):
                    part_copy(step, turn, at).wait_send()

    @pl.when(jnp.logical_not(is_last))
    def _():
        sent(0)
        for step in range(DIRECT, CHUNKS):
            through_copy(step, sec + 1).wait_send()

    value_copy(other).wait_send()
    heat_copy(core).wait_send()
    for hop, to in hops:
        hidden_copy(hop, to).wait_send()
    for store in stores:
        store.wait()


def on_device_chain(hidden_in, attn_out, queries, keys, value_weight, out_weight, lengths):
    peers = lax.axis_size("dp")
    sections = lax.axis_size("section")
    seq_len, half = hidden_in.shape[2:]
    kv_half = keys.shape[3]
    kv_width = value_weight.shape[2]
    width = out_weight.shape[2]
    heads = half // HD
    rows_n = seq_len // CHUNKS
    packed = sum(tiles_of(heads, step) for step in range(CHUNKS))
    vmem = pltpu.VMEM
    dma = pltpu.SemaphoreType.DMA
    heat, relevance = pl.pallas_call(
        functools.partial(chain_kernel, peers, sections),
        out_shape=(
            jax.ShapeDtypeStruct((1, seq_len), F32),
            jax.ShapeDtypeStruct((half // peers, kv_width), F32),
        ),
        in_specs=[pl.BlockSpec(memory_space=pltpu.SMEM)] + [pl.BlockSpec(memory_space=pl.ANY)] * 6,
        out_specs=(pl.BlockSpec(memory_space=pl.ANY), pl.BlockSpec(memory_space=pl.ANY)),
        scratch_shapes=[
            vmem((seq_len, half), BF16),
            vmem((seq_len, half), BF16),
            vmem((seq_len, half), BF16),
            vmem((seq_len, kv_half), BF16),
            vmem((half, kv_width), BF16),
            vmem((half, width), BF16),
            dma((6,)),
            vmem((seq_len, half), F32),
            vmem((seq_len, half), F32),
            vmem((peers, seq_len, half), F32),
            vmem((seq_len, half), BF16),
            vmem((seq_len, half), BF16),
            vmem((peers, heads, seq_len, seq_len), BF16),
            vmem((peers, packed, rows_n, HD), BF16),
            vmem((peers, seq_len, kv_half), BF16),
            vmem((seq_len, kv_half), F32),
            vmem((peers, seq_len, kv_half), F32),
            vmem((2, seq_len, kv_half), BF16),
            vmem((seq_len, kv_half), BF16),
            vmem((half, seq_len), BF16),
            vmem((peers, half // peers, seq_len), BF16),
            vmem((peers, 2, seq_len, kv_half), BF16),
            vmem((2, seq_len, HD), F32),
            vmem((peers * rows_n, half), BF16),
            vmem((CHUNKS, peers, rows_n, kv_half), BF16),
            vmem((CHUNKS, peers, rows_n, kv_half), BF16),
            vmem((CHUNKS, peers // 2, rows_n, width), BF16),
            vmem((CHUNKS, peers, rows_n, width), BF16),
            vmem((RAW, peers, rows_n, half), BF16),
            vmem((RAW, peers - 1, rows_n, half), BF16),
            vmem((seq_len, half), F32),
            vmem((CHUNKS - DIRECT, peers // 2, rows_n, width), BF16),
            dma((2,)),
            dma((CHUNKS, peers)),
            dma((RAW, peers - 1)),
            dma((CHUNKS,)),
            dma((4,)),
            dma((CHUNKS,)),
            dma((4,)),
            dma((CHUNKS + 1, 2)),
            dma((CHUNKS,)),
            vmem((1, seq_len), F32),
            vmem((half // peers, kv_width), F32),
            dma((2,)),
        ],
        compiler_params=pltpu.CompilerParams(
            collective_id=0, has_side_effects=True, vmem_limit_bytes=40 * 1024 * 1024
        ),
        name="relevance_chain",
    )(
        lengths,
        *(
            pltpu.with_memory_space_constraint(operand, pltpu.MemorySpace.HBM)
            for operand in (
                hidden_in[0, 0], attn_out[0, 0], queries[0, 0], keys[0, 0], value_weight[0], out_weight[0],
            )
        ),
    )
    return heat[None], relevance[None]


def solution(mesh):
    placed = (
        P("section", ("groups", "dp"), None, "mp"),
        P("section", ("groups", "dp"), None, "mp"),
        P("section", ("groups", "dp"), None, "mp"),
        P("section", ("groups", "dp"), None, "mp"),
        P("section", "mp", None),
        P("section", "mp", "dp"),
        P(("groups", "dp")),
    )
    peers = mesh.shape["dp"]
    aligned = peers == 4 and mesh.shape["section"] == 2
    return jax.shard_map(
        on_device_chain if aligned else on_device,
        mesh=mesh,
        in_specs=placed,
        out_specs=(
            P("section", ("groups", "dp"), None),
            P(("groups", "section"), ("mp", "dp"), None),
        ),
        check_vma=False,
    )
```

```python
import functools
import math

import jax
import jax.numpy as jnp
from jax import lax
from jax.experimental import pallas as pl
from jax.experimental.pallas import tpu as pltpu
from jax.sharding import PartitionSpec as P

DW = 2560
HD = 128
QH = 20
KVH = 4


EPS = 0.25


def from_behind(shard, axis, by):
    peers = lax.axis_size(axis)
    pairs = [(i, i + by) for i in range(peers) if 0 <= i + by < peers]
    return lax.ppermute(shard, axis, pairs)


def stabilize(entries):
    return jnp.where(entries >= 0, entries + EPS, entries - EPS)


def gated(active, compute, operand, out_shape, out_type):
    return lax.cond(active, compute, lambda unused: jnp.zeros(out_shape, out_type), operand)


def on_device(hidden_in, attn_out, queries, keys, value_weight, out_weight, lengths):
    inputs = hidden_in[0, 0]
    branch = attn_out[0, 0]
    query_rows = queries[0, 0]
    key_rows = keys[0, 0]
    value_rows = value_weight[0]
    seq_len = inputs.shape[0]
    half_width = inputs.shape[1]
    group_size = QH // KVH
    local_kv = key_rows.shape[1] // HD
    kv_width = value_rows.shape[1]
    sections = lax.axis_size("section")
    section_pos = lax.axis_index("section")
    core_pos = lax.axis_index("mp")
    out_cols = lax.all_gather(out_weight, "dp", axis=2, tiled=True)[0]
    inputs_f = inputs.astype(jnp.float32)
    branch_f = branch.astype(jnp.float32)
    totals = inputs_f + branch_f
    value_part = jnp.dot(inputs, value_rows, preferred_element_type=jnp.float32)
    value_all = lax.psum(value_part.astype(jnp.bfloat16), "mp").astype(jnp.float32)
    value_mine = lax.dynamic_slice_in_dim(value_all, core_pos * local_kv * HD, local_kv * HD, 1)
    values_bf = lax.optimization_barrier(value_mine.astype(jnp.bfloat16))
    values_f = values_bf.astype(jnp.float32)
    query_heads = query_rows.reshape(seq_len, local_kv, group_size, HD)
    key_heads = key_rows.reshape(seq_len, local_kv, HD)
    scores = jnp.einsum(
        "tgjd,sgd->gjts", query_heads, key_heads, preferred_element_type=jnp.float32
    ) / math.sqrt(HD)
    position = lax.iota(jnp.int32, seq_len)
    allowed = (position[None, :] <= position[:, None]) & (position[None, :] < lengths[0])
    scores = jnp.where(allowed, scores, -1000000000.0)
    row_top = jnp.max(scores, axis=-1, keepdims=True)
    weights = jnp.exp(scores - row_top)
    prob_rows = (weights / jnp.sum(weights, axis=-1, keepdims=True)).astype(jnp.bfloat16)
    mixed_heads = jnp.einsum(
        "gjts,sgd->tgjd",
        prob_rows,
        values_bf.reshape(seq_len, local_kv, HD),
        preferred_element_type=jnp.float32,
    ).reshape(seq_len, local_kv * group_size * HD)
    valid_rows = (position < lengths[0]).astype(jnp.float32)
    current = (totals * valid_rows[:, None]).astype(jnp.bfloat16)
    result = jnp.zeros((seq_len, half_width), jnp.bfloat16)
    sens_kept = jnp.zeros((seq_len, kv_width), jnp.bfloat16)
    for turn_index in range(sections):
        active = section_pos == sections - 1 - turn_index
        sens_total = current.astype(jnp.float32) / stabilize(totals)
        sens_branch = (branch_f * sens_total / stabilize(branch_f)).astype(jnp.bfloat16)
        sens_full = lax.all_gather(sens_branch, "mp", axis=1, tiled=True)

        def through_heads(operand):
            back_mixed = lax.dot_general(
                operand, out_cols, (((1,), (1,)), ((), ())), preferred_element_type=jnp.float32
            )
            sens_mixed = (mixed_heads * back_mixed / stabilize(mixed_heads)).astype(jnp.bfloat16)
            back_values = jnp.einsum(
                "gjts,tgjd->sgd",
                prob_rows,
                sens_mixed.reshape(seq_len, local_kv, group_size, HD),
                preferred_element_type=jnp.float32,
            ).reshape(seq_len, local_kv * HD)
            return (values_f * back_values / stabilize(values_f)).astype(jnp.bfloat16)

        sens_values = gated(
            active, through_heads, sens_full, (seq_len, local_kv * HD), jnp.bfloat16
        )
        sens_all = lax.all_gather(sens_values, "mp", axis=1, tiled=True)

        def through_values(operand):
            back_inputs = lax.dot_general(
                operand, value_rows, (((1,), (1,)), ((), ())), preferred_element_type=jnp.float32
            )
            return (inputs_f * sens_total + inputs_f * back_inputs).astype(jnp.bfloat16)

        outgoing = gated(active, through_values, sens_all, (seq_len, half_width), jnp.bfloat16)
        result = jnp.where(active, outgoing, result)
        sens_kept = jnp.where(active, sens_all, sens_kept)
        if turn_index + 1 < sections:
            arrived = from_behind(outgoing, "section", -1)
            current = jnp.where(section_pos == sections - 2 - turn_index, arrived, current)
    heat_part = jnp.sum(result.astype(jnp.float32), axis=1)
    heat_rows = lax.psum(heat_part, "mp") / DW
    block_rows = half_width // lax.axis_size("dp")
    row_start = lax.axis_index("dp") * block_rows
    value_block = lax.dynamic_slice_in_dim(value_rows, row_start, block_rows, 0).astype(jnp.float32)
    summed = lax.psum_scatter(
        lax.dot_general(
            inputs, sens_kept, (((0,), (0,)), ((), ())), preferred_element_type=jnp.float32
        ).astype(jnp.bfloat16),
        "dp",
        scatter_dimension=0,
        tiled=True,
    ).astype(jnp.float32)
    relevance_rows = value_block * summed
    return (heat_rows[None, None, :], relevance_rows[None])


CHUNKS = 4
RAW = 2
EARLY = (1,)
SEGMENTS = (((0, 128),), ((0, 64), (64, 32)), ((0, 64),), ((0, 32),))
TILE = 256
MESH_ID = pl.DeviceIdType.MESH
F32 = jnp.float32
BF16 = jnp.bfloat16
DIRECT = 1
LAST_ORDER = (
    ("branch", 1), ("give", 2), ("give", 3), ("branch", 2), ("part", 0), ("branch", 3),
    ("mix", 0), ("part", 1), ("relay", 2), ("relay", 3), ("head", 0), ("mix", 1), ("emit", 0),
    ("ahead", 0), ("values", 2), ("gather", 2), ("gather", 3), ("linear", 2), ("linear", 3),
    ("head", 1), ("emit", 1), ("join", 2), ("join", 3), ("emit", 2), ("emit", 3), ("hidden", 3),
)
NEXT_ORDER = (
    ("relay", 0), ("relay", 1), ("relay", 2), ("relay", 3), ("values", 0), ("hidden", 0),
    ("gather", 0), ("gather", 1), ("take", 0), ("gather", 2), ("gather", 3), ("linear", 0),
    ("linear", 1), ("join", 0), ("emit", 0), ("linear", 2), ("linear", 3), ("join", 1),
    ("join", 2), ("join", 3), ("emit", 1), ("emit", 2), ("emit", 3),
)


def tiles_of(heads, step):
    return sum(-(-heads // (HD // lanes)) for _, lanes in SEGMENTS[step])


def nt_dot(left, right):
    return lax.dot_general(left, right, (((1,), (1,)), ((), ())), preferred_element_type=F32)


def tn_dot(left, right):
    return lax.dot_general(left, right, (((0,), (0,)), ((), ())), preferred_element_type=F32)


def chain_kernel(
    peers, sections, len_ref, hid_in, att_in, que_in, key_in, vw_in, ow_in,
    heat_out, rel_out, hid_ref, att_ref, que_ref, key_ref, vw_ref, ow_ref, load_sem,
    through_ref, keep_ref, ratio_ref, inc_ref, out_ref, prob_ref, pack_ref, gval_ref, val_ref, bv_ref,
    vsend, vrecv, hidt_ref, hida_ref, sv_ref, heats, sm_ref, bvsend, bvbuf,
    asend, abuf, psend, pbuf, below_ref, dsend,
    done, a_recv, p_recv, s_recv, f_recv, x_recv, one_recv, k_recv, b_recv,
    heat_ref, rel_ref, out_sem,
):
    dp = lax.axis_index("dp")
    sec = lax.axis_index("section")
    core = lax.axis_index("mp")
    other = 1 - core
    seq_len, half = hid_ref.shape
    rows_n = seq_len // CHUNKS
    width = ow_ref.shape[1]
    blocks = peers // 2
    local_kv = key_ref.shape[1] // HD
    group = QH // KVH
    heads_n = local_kv * group
    kv_half = local_kv * HD
    block_rows = half // peers
    is_last = sec == sections - 1
    gets = core == dp // blocks
    hops = [(hop, lax.rem(dp + hop, peers)) for hop in range(1, peers)]

    loads = [
        pltpu.make_async_copy(source, target, load_sem.at[at])
        for at, (source, target) in enumerate((
            (hid_in, hid_ref), (att_in, att_ref), (vw_in, vw_ref),
            (que_in, que_ref), (key_in, key_ref), (ow_in, ow_ref),
        ))
    ]
    for load in loads:
        load.start()

    barrier = pltpu.get_barrier_semaphore()
    for hop, to in hops:
        for target in range(2):
            pl.semaphore_signal(
                barrier, inc=1, device_id={"dp": to, "mp": target}, device_id_type=MESH_ID
            )
    pl.semaphore_signal(barrier, inc=1, device_id={"mp": other}, device_id_type=MESH_ID)

    @pl.when(sec > 0)
    def _():
        pl.semaphore_signal(
            barrier, inc=1, device_id={"section": sec - 1}, device_id_type=MESH_ID
        )

    @pl.when(sec < sections - 1)
    def _():
        for at in range(peers):
            pl.semaphore_signal(
                barrier, inc=1, device_id={"dp": at, "section": sec + 1}, device_id_type=MESH_ID
            )

    def barrier_wait():
        greeted = 2 * (peers - 1) + 1

        @pl.when(is_last)
        def _():
            pl.semaphore_wait(barrier, greeted + peers)

        @pl.when(jnp.logical_not(is_last))
        def _():
            pl.semaphore_wait(barrier, greeted + 1)

    def remote(source, target, send, recv, device):
        return pltpu.make_async_remote_copy(
            src_ref=source, dst_ref=target, send_sem=send, recv_sem=recv,
            device_id=device, device_id_type=MESH_ID,
        )

    def rows_of(step):
        return pl.ds((CHUNKS - 1 - step) * rows_n, rows_n)

    def branch_copy(step, block):
        return remote(
            asend.at[step, block], abuf.at[step, dp],
            done.at[0], a_recv.at[step, dp], {"dp": core * blocks + block},
        )

    def direct_copy(step, block):
        return remote(
            dsend.at[step - DIRECT, block], abuf.at[step, dp],
            done.at[1], a_recv.at[step, dp],
            {"dp": core * blocks + block, "section": sec - 1},
        )

    def through_copy(step, target):
        rows = rows_of(step)
        return remote(
            through_ref.at[rows], below_ref.at[rows],
            done.at[0], one_recv.at[3], {"section": target},
        )

    def branch_forward(step, source):
        view = abuf.at[step, source]
        return remote(
            view, view, done.at[0], a_recv.at[step, source], {"mp": other}
        )

    rounds = peers.bit_length() - 1

    def slot_of(turn, target):
        return peers - (peers >> turn) + target // (2 << turn)

    def part_target(turn, at):
        bit = 1 << turn
        return lax.rem(dp, bit) + bit * (2 * at + 1 - lax.rem(dp // bit, 2))

    def part_copy(step, turn, at):
        bit = 1 << turn
        slot = peers - (peers >> turn) + at
        return remote(
            psend.at[step, part_target(turn, at)], pbuf.at[step, slot],
            done.at[0], p_recv.at[step, slot],
            {"dp": dp + bit - 2 * bit * lax.rem(dp // bit, 2)},
        )

    def part_take(step, turn, target):
        slot = slot_of(turn, target)
        view = pbuf.at[step, slot]
        remote(
            view, view, done.at[0], p_recv.at[step, slot], {"mp": other}
        ).wait_recv()
        return pbuf[step, slot].astype(F32)

    def mix_stage(step):
        for turn in range(1, rounds):
            for at in range(peers >> (turn + 1)):
                target = part_target(turn, at)
                running = psend[step, target].astype(F32)
                for before in range(turn):
                    running = running + part_take(step, before, target)
                psend[step, target] = running.astype(BF16)
                part_copy(step, turn, at).start()

    def value_rows(step, source):
        return gval_ref.at[source, pl.ds(0, (CHUNKS - step) * rows_n)]

    def prob_tiles(step, source):
        first = sum(tiles_of(heads_n, before) for before in range(step))
        return pack_ref.at[source, pl.ds(first, tiles_of(heads_n, step))]

    def relays(source, through):
        return jnp.logical_or(
            jnp.logical_and(source == 0, through == peers - 2),
            jnp.logical_and(source == peers - 1, through == 1),
        )

    def lane(source, to):
        return relays(source, to).astype(jnp.int32)

    def gather_value(first, to):
        view = value_rows(first, dp)
        return remote(
            view, view, done.at[0], k_recv.at[CHUNKS, lane(dp, to)], {"dp": to}
        )

    def gather_probs(step, to):
        view = prob_tiles(step, dp)
        return remote(
            view, view, done.at[0], k_recv.at[step, lane(dp, to)], {"dp": to}
        )

    def sum_copy(step, hop, to):
        return remote(
            bvsend.at[step, hop], bvbuf.at[step, dp],
            done.at[0], b_recv.at[step], {"dp": to},
        )

    def sens_copy(step, owner):
        view = sv_ref.at[dp, owner, rows_of(step)]
        return remote(view, view, done.at[0], s_recv.at[step], {"mp": other})

    def final_copy(step, hop, to, side):
        view = sv_ref.at[dp, core, rows_of(step)]
        return remote(
            view, view, done.at[0], f_recv.at[step // (CHUNKS - 1)],
            {"dp": to, "mp": core if side == 0 else other},
        )

    early = pl.ds(rows_n, seq_len - rows_n)

    def final_wait(at, owners, rows):
        view = sv_ref.at[pl.ds(0, peers - 1), owners, rows]
        remote(view, view, done.at[0], f_recv.at[at], {"mp": other}).wait_recv()

    def final_forward(source, owner, at):
        rows = rows_of(CHUNKS - 1) if at else early
        view = sv_ref.at[source, owner, rows]
        return remote(view, view, done.at[0], f_recv.at[2 + at], {"mp": other})

    def final_out(step):
        for hop, to in hops:
            final_copy(step, hop, to, 0).start()

    def section_copy(step, target):
        return remote(
            out_ref.at[rows_of(step)], inc_ref.at[rows_of(step)],
            done.at[0], x_recv.at[step], {"section": target},
        )

    def hidden_copy(hop, to):
        return remote(
            hidt_ref.at[pl.ds(pl.multiple_of(to * block_rows, 16), block_rows)], hida_ref.at[dp],
            done.at[0], one_recv.at[2], {"dp": to},
        )

    def hidden_wait():
        view = hida_ref.at[pl.ds(0, peers - 1)]
        remote(view, view, done.at[0], one_recv.at[2], {"mp": other}).wait_recv()

    def value_copy(slot):
        return remote(
            vsend.at[slot], vrecv, done.at[0], one_recv.at[0], {"mp": other}
        )

    def heat_copy(slot):
        return remote(
            heats.at[slot], heats.at[slot], done.at[0], one_recv.at[1], {"mp": other}
        )

    def branch_stage(step):
        rows = rows_of(step)
        sens = (inc_ref[rows, :].astype(F32) * through_ref[rows, :]).astype(BF16)
        for block in range(blocks):
            to = core * blocks + block
            piece = sens[:, block * width:(block + 1) * width]
            asend[step, block] = piece

            @pl.when(to == dp)
            def _():
                abuf[step, dp] = piece
                branch_forward(step, dp).start()

            @pl.when(to != dp)
            def _():
                branch_copy(step, block).start()

    def branch_wait(step, direct):
        @pl.when(gets)
        def _():
            for hop in range(0 if direct else 1, peers):
                source = lax.rem(dp + hop, peers)
                branch_forward(step, source).wait_recv()
                branch_forward(step, source).start()

        @pl.when(jnp.logical_not(gets))
        def _():
            for source in range(peers):
                branch_forward(step, source).wait_recv()

        return abuf[step].reshape(peers * rows_n, width)

    def part_stage(step):
        stacked = branch_wait(step, False)

        def tile(at, unused):
            start = pl.multiple_of(at * TILE, TILE)
            part = nt_dot(stacked, ow_ref[pl.ds(start, TILE), :]).astype(BF16)
            psend[step, :, :, pl.ds(start, TILE)] = part.reshape(peers, rows_n, TILE)
            return unused

        lax.fori_loop(0, half // TILE, tile, 0, unroll=True)
        for at in range(peers // 2):
            part_copy(step, 0, at).start()

    def add_values(seq, rows, mixed):
        for kv in range(local_kv):
            heads = range(kv * group, (kv + 1) * group)
            left = jnp.concatenate([prob_ref[seq, h, rows, :] for h in heads], axis=0)
            right = jnp.concatenate([mixed[:, h * HD:(h + 1) * HD] for h in heads], axis=0)
            columns = pl.ds(kv * HD, HD)
            bv_ref[seq, :, columns] = bv_ref[seq, :, columns] + tn_dot(left, right)

    def head_stage(step):
        rows = rows_of(step)
        back = psend[step, dp].astype(F32)
        for turn in range(rounds):
            back = back + part_take(step, turn, dp)
        add_values(dp, rows, (ratio_ref[dp, rows, :] * back).astype(BF16))
        settle(step, bv_ref[dp, rows, :])

    def linear_stage(step, direct=False):
        rows = rows_of(step)
        stacked = branch_wait(step, direct)
        for at in range(half // TILE):
            columns = pl.ds(at * TILE, TILE)
            part = nt_dot(stacked, ow_ref[columns, :])
            ratio = ratio_ref[:, rows, columns].reshape(peers * rows_n, TILE)
            sm_ref[:, columns] = (ratio * part).astype(BF16)
        for seq in range(peers):
            add_values(seq, rows, sm_ref[seq * rows_n:(seq + 1) * rows_n, :])
        for hop, to in hops:
            bvsend[step, hop] = bv_ref[to, rows, :].astype(BF16)
            sum_copy(step, hop, to).start()

    def join_stage(step):
        total = bv_ref[dp, rows_of(step), :]
        view = bvbuf.at[step, pl.ds(0, peers - 1)]
        remote(view, view, done.at[0], b_recv.at[step], {"mp": other}).wait_recv()
        for hop, source in hops:
            total = total + bvbuf[step, source].astype(F32)
        settle(step, total)

    def settle(step, back_values):
        rows = rows_of(step)
        sv_ref[dp, core, rows, :] = (val_ref[rows, :] * back_values).astype(BF16)
        sens_copy(step, core).start()

        @pl.when(jnp.logical_not(is_last))
        def _():
            final_out(step)

    def emit_stage(step):
        rows = rows_of(step)
        sens_copy(step, other).wait_recv()
        sens = jnp.concatenate([sv_ref[dp, 0, rows, :], sv_ref[dp, 1, rows, :]], axis=1)
        sums = jnp.zeros((rows_n, HD), F32)
        for at in range(half // TILE):
            columns = pl.ds(at * TILE, TILE)
            back_in = nt_dot(sens, vw_ref[columns, :])
            out = (
                inc_ref[rows, columns].astype(F32) * keep_ref[rows, columns]
                + hid_ref[rows, columns].astype(F32) * back_in
            ).astype(BF16)
            out_ref[rows, columns] = out
            wide = out.astype(F32)
            for lane in range(TILE // HD):
                sums = sums + wide[:, lane * HD:(lane + 1) * HD]
        heats[core, rows, :] = sums

        @pl.when(sec > 0)
        def _():
            if step >= DIRECT:
                if step == DIRECT:
                    view = below_ref.at[pl.ds(0, (CHUNKS - DIRECT) * rows_n)]
                    remote(view, view, done.at[0], one_recv.at[3], {"mp": other}).wait_recv()
                below = (out_ref[rows, :].astype(F32) * below_ref[rows, :]).astype(BF16)
                for block in range(blocks):
                    dsend[step - DIRECT, block] = below[:, block * width:(block + 1) * width]
                    direct_copy(step, block).start()
            else:
                section_copy(step, sec - 1).start()

    lane_at = lax.broadcasted_iota(jnp.int32, (rows_n, HD), 1)

    def shifted(tile, start, count, to):
        inside = (lane_at >= start) & (lane_at < start + count)
        kept = jnp.where(inside, tile, 0.0)
        return kept if start == to else pltpu.roll(kept, (to - start) % HD, 1)

    def pack_stage(step):
        at = sum(tiles_of(heads_n, before) for before in range(step))
        for start, lanes in SEGMENTS[step]:
            per = HD // lanes
            for first in range(0, heads_n, per):
                tile = None
                for h in range(first, min(first + per, heads_n)):
                    piece = shifted(
                        prob_ref[dp, h, rows_of(step), :].astype(F32), start, lanes, (h - first) * lanes
                    )
                    tile = piece if tile is None else tile + piece
                pack_ref[dp, at] = tile.astype(BF16)
                at += 1

    def value_wait(first):
        gather_wait(
            CHUNKS, lambda count: gval_ref.at[pl.ds(0, count), pl.ds(0, (CHUNKS - first) * rows_n)]
        )

    def far(to):
        return jnp.logical_and(dp + to == peers - 1, jnp.logical_or(dp == 0, to == 0))

    def relay_copy(step, view, source):
        return remote(
            view, view, done.at[0], k_recv.at[step, 0], {"dp": peers - 1 - source}
        )

    def gather_wait(step, views):
        def wait(view):
            remote(view, view, done.at[0], k_recv.at[step, 0], {"mp": other}).wait_recv()

        inner = jnp.logical_and(dp > 0, dp < peers - 1)

        @pl.when(inner)
        def _():
            wait(views(peers - 2))

        @pl.when(jnp.logical_not(inner))
        def _():
            wait(views(peers - 1))

    def relay_stage(step, first=0):
        for end, through in ((0, peers - 2), (peers - 1, 1)):
            @pl.when(dp == through)
            def _():
                views = [(step, prob_tiles(step, end))]
                if step == first:
                    views.insert(0, (CHUNKS, value_rows(first, end)))
                for at, view in views:
                    remote(view, view, done.at[0], k_recv.at[at, 1], {"mp": other}).wait_recv()
                    relay_copy(at, view, end).start()

    def gather_stage(step):
        rows = rows_of(step)
        depth = (CHUNKS - step) * rows_n
        first_tile = sum(tiles_of(heads_n, before) for before in range(step))
        tiles = pl.ds(first_tile, tiles_of(heads_n, step))
        gather_wait(step, lambda count: pack_ref.at[pl.ds(0, count), tiles])
        for hop, source in hops:
            for h in range(heads_n):
                at = first_tile
                whole = None
                for start, lanes in SEGMENTS[step]:
                    per = HD // lanes
                    piece = shifted(
                        pack_ref[source, at + h // per].astype(F32), h % per * lanes, lanes, start
                    )
                    whole = piece if whole is None else whole + piece
                    at += -(-heads_n // per)
                prob_ref[source, h, rows, :] = whole.astype(BF16)
            for kv in range(local_kv):
                heads = range(kv * group, (kv + 1) * group)
                left = jnp.concatenate(
                    [prob_ref[source, h, rows, pl.ds(0, depth)] for h in heads], axis=0
                )
                mixed = jnp.dot(
                    left, gval_ref[source, pl.ds(0, depth), pl.ds(kv * HD, HD)],
                    preferred_element_type=F32,
                )
                ratio = mixed / stabilize(mixed)
                for at, h in enumerate(heads):
                    ratio_ref[source, rows, h * HD:(h + 1) * HD] = (
                        ratio[at * rows_n:(at + 1) * rows_n, :]
                    )

    length = len_ref[0]
    loads[0].wait()
    loads[1].wait()
    for step in range(CHUNKS):
        rows = rows_of(step)
        hid = hid_ref[rows, :].astype(F32)
        att = att_ref[rows, :].astype(F32)
        totals = hid + att
        inverse = 1.0 / stabilize(totals)
        keep_ref[rows, :] = hid * inverse
        through_ref[rows, :] = att * inverse / stabilize(att)

        @pl.when(is_last)
        def _():
            token = (CHUNKS - 1 - step) * rows_n + lax.broadcasted_iota(
                jnp.int32, (rows_n, half), 0
            )
            inc_ref[rows, :] = jnp.where(token < length, totals, 0.0).astype(BF16)

    loads[2].wait()
    hid_all = hid_ref[...]
    for slot in range(2):
        part = jnp.dot(
            hid_all, vw_ref[:, slot * kv_half:(slot + 1) * kv_half], preferred_element_type=F32
        )
        vsend[slot] = part.astype(BF16)

        @pl.when(core == slot)
        def _():
            val_ref[...] = part

    for load in loads[3:]:
        load.wait()
    bv_ref[...] = jnp.zeros_like(bv_ref)
    barrier_wait()
    value_copy(other).start()

    @pl.when(is_last)
    def _():
        branch_stage(0)

    @pl.when(jnp.logical_not(is_last))
    def _():
        for step in range(DIRECT, CHUNKS):
            through_copy(step, sec + 1).start()

    query_at = lax.broadcasted_iota(jnp.int32, (seq_len, seq_len), 0)
    key_at = lax.broadcasted_iota(jnp.int32, (seq_len, seq_len), 1)
    allowed = (key_at <= query_at) & (key_at < length)
    for h in range(heads_n):
        kv = h // group
        scores = nt_dot(
            que_ref[:, h * HD:(h + 1) * HD], key_ref[:, kv * HD:(kv + 1) * HD]
        ) / math.sqrt(HD)
        scores = jnp.where(allowed, scores, -1000000000.0)
        weights = jnp.exp(scores - jnp.max(scores, axis=1, keepdims=True))
        prob_ref[dp, h] = (weights / jnp.sum(weights, axis=1, keepdims=True)).astype(BF16)

    value_copy(other).wait_recv()
    values = (val_ref[...] + vrecv[...].astype(F32)).astype(BF16)
    gval_ref[dp] = values

    @pl.when(is_last)
    def _():
        for step in range(RAW, CHUNKS):
            pack_stage(step)

    @pl.when(jnp.logical_not(is_last))
    def _():
        for step in range(CHUNKS):
            pack_stage(step)
        for hop, to in (hops[1], hops[0], hops[2]):
            @pl.when(jnp.logical_not(far(to)))
            def _():
                gather_value(0, to).start()
                for step in range(CHUNKS):
                    gather_probs(step, to).start()

    wide_values = values.astype(F32)
    val_ref[...] = wide_values / stabilize(wide_values)
    for h in range(heads_n):
        kv = h // group
        mixed = jnp.dot(
            prob_ref[dp, h], values[:, kv * HD:(kv + 1) * HD], preferred_element_type=F32
        )
        ratio_ref[dp, :, h * HD:(h + 1) * HD] = mixed / stabilize(mixed)

    for at in range(half // HD):
        flipped = hid_ref[:, at * HD:(at + 1) * HD].astype(F32).T
        hidt_ref[pl.ds(at * HD, HD), :] = flipped.astype(BF16)
    hida_ref[dp] = hidt_ref[pl.ds(pl.multiple_of(dp * block_rows, 16), block_rows), :]

    def branch_next(step):
        section_copy(step, sec + 1).wait_recv()
        branch_stage(step)

    def hidden_stage(step):
        if step == CHUNKS - 1:
            for at in range(DIRECT, CHUNKS):
                for block in range(blocks):
                    direct_copy(at, block).wait_send()
                section_copy(at, sec - 1).start()
        for hop, to in hops:
            if step == 0 or hop not in EARLY:
                hidden_copy(hop, to).start()

    def ahead_stage(step):
        hop, to = hops[step]
        hidden_copy(hop, to).start()

    def emit_next(step):
        if step >= DIRECT:
            section_copy(step, sec + 1).wait_recv()
        emit_stage(step)

    def give_stage(step):
        for hop, to in (hops[1], hops[0], hops[2]):
            @pl.when(jnp.logical_not(far(to)))
            def _():
                if step == RAW:
                    gather_value(RAW, to).start()
                gather_probs(step, to).start()

    stages = {
        "ahead": ahead_stage, "give": give_stage, "emit": emit_stage,
        "values": value_wait, "hidden": hidden_stage, "branch": branch_stage, "relay": relay_stage,
        "gather": gather_stage, "part": part_stage, "mix": mix_stage, "head": head_stage,
        "take": branch_next, "linear": linear_stage, "join": join_stage,
    }

    @pl.when(is_last)
    def _():
        for stage, step in LAST_ORDER:
            if stage == "relay":
                stages[stage] = functools.partial(relay_stage, first=RAW)
            stages[stage](step)
        for step in range(CHUNKS):
            final_out(step)

    @pl.when(jnp.logical_not(is_last))
    def _():
        stages["emit"] = emit_next
        stages["relay"] = relay_stage
        for stage, step in NEXT_ORDER:
            if stage == "linear":
                stages[stage] = functools.partial(linear_stage, direct=step >= DIRECT)
            stages[stage](step)

    heat_copy(core).start()
    last = rows_of(CHUNKS - 1)
    for at, rows in enumerate((early, last)):
        final_wait(at, 0, rows)
        for hop, source in hops:
            final_forward(source, core, at).start()
    hidden_wait()
    final_wait(2, 0, early)
    final_wait(3, 0, last)
    block_at = pl.ds(pl.multiple_of(dp * block_rows, 16), block_rows)
    total = None
    for hop in range(peers):
        source = lax.rem(dp + hop, peers)
        sens = jnp.concatenate([sv_ref[source, 0], sv_ref[source, 1]], axis=1)
        term = jnp.dot(hida_ref[source], sens, preferred_element_type=F32)
        total = term if total is None else total + term
    rel_ref[...] = vw_ref[block_at, :].astype(F32) * total
    stores = [
        pltpu.make_async_copy(source, target, out_sem.at[at])
        for at, (source, target) in enumerate(((heat_ref, heat_out), (rel_ref, rel_out)))
    ]
    stores[1].start()
    heat_copy(other).wait_recv()
    heat_ref[...] = jnp.sum((heats[0] + heats[1]).T, axis=0, keepdims=True) / DW
    stores[0].start()
    for hop, to in hops:
        for step in range(CHUNKS):
            final_copy(step, hop, to, 0).wait_send()

        for at in range(2):
            final_forward(to, core, at).wait_send()
    for step in range(CHUNKS):
        for block in range(blocks):
            mine = core * blocks + block != dp

            @pl.when(mine if step < DIRECT else jnp.logical_and(mine, is_last))
            def _():
                branch_copy(step, block).wait_send()

        @pl.when(gets)
        def _():
            for source in range(peers):
                branch_forward(step, source).wait_send()

        sens_copy(step, core).wait_send()

        @pl.when(sec > 0)
        def _():
            section_copy(step, sec - 1).wait_send()

    def sent(first):
        for hop, to in hops:
            @pl.when(jnp.logical_not(far(to)))
            def _():
                gather_value(first, to).wait_send()
                for step in range(first, CHUNKS):
                    gather_probs(step, to).wait_send()

            @pl.when(relays(to, dp))
            def _():
                relay_copy(CHUNKS, value_rows(first, to), to).wait_send()
                for step in range(first, CHUNKS):
                    relay_copy(step, prob_tiles(step, to), to).wait_send()
            for step in range(first, CHUNKS):
                sum_copy(step, hop, to).wait_send()

    @pl.when(is_last)
    def _():
        sent(RAW)
        for step in range(RAW):
            for turn in range(rounds):
                for at in range(peers >> (turn + 1)):
                    part_copy(step, turn, at).wait_send()

    @pl.when(jnp.logical_not(is_last))
    def _():
        sent(0)
        for step in range(DIRECT, CHUNKS):
            through_copy(step, sec + 1).wait_send()

    value_copy(other).wait_send()
    heat_copy(core).wait_send()
    for hop, to in hops:
        hidden_copy(hop, to).wait_send()
    for store in stores:
        store.wait()


def on_device_chain(hidden_in, attn_out, queries, keys, value_weight, out_weight, lengths):
    peers = lax.axis_size("dp")
    sections = lax.axis_size("section")
    seq_len, half = hidden_in.shape[2:]
    kv_half = keys.shape[3]
    kv_width = value_weight.shape[2]
    width = out_weight.shape[2]
    heads = half // HD
    rows_n = seq_len // CHUNKS
    packed = sum(tiles_of(heads, step) for step in range(CHUNKS))
    vmem = pltpu.VMEM
    dma = pltpu.SemaphoreType.DMA
    heat, relevance = pl.pallas_call(
        functools.partial(chain_kernel, peers, sections),
        out_shape=(
            jax.ShapeDtypeStruct((1, seq_len), F32),
            jax.ShapeDtypeStruct((half // peers, kv_width), F32),
        ),
        in_specs=[pl.BlockSpec(memory_space=pltpu.SMEM)] + [pl.BlockSpec(memory_space=pl.ANY)] * 6,
        out_specs=(pl.BlockSpec(memory_space=pl.ANY), pl.BlockSpec(memory_space=pl.ANY)),
        scratch_shapes=[
            vmem((seq_len, half), BF16),
            vmem((seq_len, half), BF16),
            vmem((seq_len, half), BF16),
            vmem((seq_len, kv_half), BF16),
            vmem((half, kv_width), BF16),
            vmem((half, width), BF16),
            dma((6,)),
            vmem((seq_len, half), F32),
            vmem((seq_len, half), F32),
            vmem((peers, seq_len, half), F32),
            vmem((seq_len, half), BF16),
            vmem((seq_len, half), BF16),
            vmem((peers, heads, seq_len, seq_len), BF16),
            vmem((peers, packed, rows_n, HD), BF16),
            vmem((peers, seq_len, kv_half), BF16),
            vmem((seq_len, kv_half), F32),
            vmem((peers, seq_len, kv_half), F32),
            vmem((2, seq_len, kv_half), BF16),
            vmem((seq_len, kv_half), BF16),
            vmem((half, seq_len), BF16),
            vmem((peers, half // peers, seq_len), BF16),
            vmem((peers, 2, seq_len, kv_half), BF16),
            vmem((2, seq_len, HD), F32),
            vmem((peers * rows_n, half), BF16),
            vmem((CHUNKS, peers, rows_n, kv_half), BF16),
            vmem((CHUNKS, peers, rows_n, kv_half), BF16),
            vmem((CHUNKS, peers // 2, rows_n, width), BF16),
            vmem((CHUNKS, peers, rows_n, width), BF16),
            vmem((RAW, peers, rows_n, half), BF16),
            vmem((RAW, peers - 1, rows_n, half), BF16),
            vmem((seq_len, half), F32),
            vmem((CHUNKS - DIRECT, peers // 2, rows_n, width), BF16),
            dma((2,)),
            dma((CHUNKS, peers)),
            dma((RAW, peers - 1)),
            dma((CHUNKS,)),
            dma((4,)),
            dma((CHUNKS,)),
            dma((4,)),
            dma((CHUNKS + 1, 2)),
            dma((CHUNKS,)),
            vmem((1, seq_len), F32),
            vmem((half // peers, kv_width), F32),
            dma((2,)),
        ],
        compiler_params=pltpu.CompilerParams(
            collective_id=0, has_side_effects=True, vmem_limit_bytes=40 * 1024 * 1024
        ),
        name="relevance_chain",
    )(
        lengths,
        *(
            pltpu.with_memory_space_constraint(operand, pltpu.MemorySpace.HBM)
            for operand in (
                hidden_in[0, 0], attn_out[0, 0], queries[0, 0], keys[0, 0], value_weight[0], out_weight[0],
            )
        ),
    )
    return heat[None], relevance[None]


def solution(mesh):
    placed = (
        P("section", ("groups", "dp"), None, "mp"),
        P("section", ("groups", "dp"), None, "mp"),
        P("section", ("groups", "dp"), None, "mp"),
        P("section", ("groups", "dp"), None, "mp"),
        P("section", "mp", None),
        P("section", "mp", "dp"),
        P(("groups", "dp")),
    )
    peers = mesh.shape["dp"]
    aligned = peers == 4 and mesh.shape["section"] == 2
    return jax.shard_map(
        on_device_chain if aligned else on_device,
        mesh=mesh,
        in_specs=placed,
        out_specs=(
            P("section", ("groups", "dp"), None),
            P(("groups", "section"), ("mp", "dp"), None),
        ),
        check_vma=False,
    )
```
